32 devices in a mesh: groups: 2 (over y), ctx: 4 (over z), head: 2 (over x), dp: 2 (over core).
Axes of the slice: x: 2, y: 2, z: 4, core: 2. Of those that a mesh axis runs over, the one named last changes fastest.
Arguments:
- query_input: bfloat16 [4, 512, 16, 128], P(('groups', 'dp'), 'ctx', 'head'), parts along dimension 0, may hold values from -6 to 6
- key_input: bfloat16 [4, 512, 3, 16, 128], P(('groups', 'dp'), 'ctx', None, 'head'), parts along dimension 0, may hold values from -6 to 6
- value_input: bfloat16 [4, 512, 3, 16, 128], P(('groups', 'dp'), 'ctx', None, 'head'), parts along dimension 0, may hold values from -6 to 6
- beta_logit: float32 [4, 16, 3, 512], P(('groups', 'dp'), 'head', None, 'ctx'), parts along dimension 0, may hold values from -6 to 6
- gate_logit: float32 [4, 16, 512], P(('groups', 'dp'), 'head', 'ctx'), parts along dimension 0, may hold values from -6 to 1536
- decay_rate: float32 [16], P('head'), may hold values from 0.00048828125 to 0.05
- doc_ids: int32 [4, 8], P(('groups', 'dp')), parts along dimension 0, may hold values from 0 to 1, never falling along the last dimension, each value on 1 to 7 neighbouring positions
- out_weight: bfloat16 [2048, 2048], P('head'), may hold values from -0.125 to 0.125
- out_cotangent: bfloat16 [4, 512, 2048], P(('groups', 'dp'), 'ctx'), parts along dimension 0, may hold values from -6 to 6
Outputs:
- mixed: bfloat16 [4, 512, 2048], P(('groups', 'dp'), 'ctx', 'head'), parts along dimension 0
- query_grad: bfloat16 [4, 512, 16, 128], P(('groups', 'dp'), 'ctx', 'head'), parts along dimension 0
- key_grad: bfloat16 [4, 512, 3, 16, 128], P(('groups', 'dp'), 'ctx', None, 'head'), parts along dimension 0
- value_grad: bfloat16 [4, 512, 3, 16, 128], P(('groups', 'dp'), 'ctx', None, 'head'), parts along dimension 0
- beta_grad: float32 [4, 16, 3, 512], P(('groups', 'dp'), 'head', None, 'ctx'), parts along dimension 0
- gate_grad: float32 [4, 16, 512], P(('groups', 'dp'), 'head', 'ctx'), parts along dimension 0
- weight_grad: float32 [4096, 2048], P(('groups', 'ctx'), 'head'), parts along dimension 0
- rate_grad: float32 [32], P(('groups', 'head')), parts along dimension 0
The draws below stay inside these ranges and needn't reach their ends.
There are 2 independent parts, one for each index of `groups`. The reference program is written for one: setup_inputs(seed, part) draws one part's arguments, and reference() takes and returns one part's arrays. A program takes and returns all parts, laid end to end along the dimension named above; an argument that names none is the same for every part. Nothing has to cross between parts.
Inputs may be any that keep to these rules, and one draw needn't show every extreme that they name: `doc_ids`: in each sequence the numbers never fall along the stretches, every number of 0 to 1 appears, each covers 1 to 7 stretches.
All inputs are finite; a program needn't handle non-finite values.
Results may differ from the reference program's by a relative error of at most 0.0051.
Values sent between devices are 32-bit elements; how exact they have to be, the bound alone decides.
A program may use at most 192 MiB of HBM per device.

```python
import math
import jax
import jax.numpy as jnp
import numpy as np
from jax import lax

CH = 64
NF = 3
D = 2048
H = 16
DK = 128
DV = 128
BATCH_DOCUMENTS = 2
CONTEXT_LENGTH = 512
NCHUNK = 8
DOCS = 2
MOSTC = 7


def draw_gate_logit(key, part):
    base_key, layout_seed, size_key = jax.random.split(jax.random.fold_in(key, 11), 3)
    baseline = jnp.clip(jax.random.normal(base_key, (BATCH_DOCUMENTS, H, CONTEXT_LENGTH), jnp.float32), -6.0, 6.0)
    segment_clusters = jax.random.randint(layout_seed, (BATCH_DOCUMENTS, 4, 1), 0, CONTEXT_LENGTH)
    flagged_lines = jnp.any(jnp.arange(CONTEXT_LENGTH)[None, None, :] == segment_clusters, axis=1)
    heights = jax.random.uniform(size_key, (BATCH_DOCUMENTS, 1, CONTEXT_LENGTH), jnp.float32, 1.0, 2.8) * CONTEXT_LENGTH
    return jnp.where(flagged_lines[:, None, :], heights, baseline)


def draw_decay_rate(key, part):
    lowest = 0.25 / CONTEXT_LENGTH
    highest_level = 0.05
    fraction = jax.random.uniform(jax.random.fold_in(key, 23), (H,), jnp.float32)
    return jnp.exp(jnp.log(lowest) + fraction * (jnp.log(highest_level) - jnp.log(lowest)))


def raised(result, key, source, target, blocks, factor):
    def block_of(position):
        return (jnp.arange(result.shape[position]) // (result.shape[position] // blocks)).reshape((-1,) + (1,) * (result.ndim - 1 - position))

    near = jax.random.permutation(key, blocks)[block_of(target)]
    second = (block_of(target) + blocks // 2) % blocks
    return jnp.where((block_of(source) == near) | (block_of(source) == second), factor * result, result)


def block_scale(own_key, dims, cuts, low, largest):
    loudness, own = 1.0, jax.random.fold_in(own_key, 6)
    for position, parts in cuts:
        steps = jnp.exp(jax.random.uniform(jax.random.fold_in(own, position), (parts,), jnp.float32, low / len(cuts), largest / len(cuts)))
        loudness = loudness * jnp.repeat(steps, dims[position] // parts).reshape([-1 if axis == position else 1 for axis in range(len(dims))])
    return loudness


def profile(number_of, total, limit, slope):
    weights = [(1 << 20) // math.isqrt(standing ** slope) + 1 for standing in range(2, number_of + 1)]
    rest, counts = total - limit - (number_of - 1), [1] * (number_of - 1)
    while rest > 0:
        movable = [i for i in range(number_of - 1) if counts[i] < limit]
        whole, remaining = sum([weights[i] for i in movable]), rest
        for i in movable:
            addition = min(limit - counts[i], max(1, remaining * weights[i] // whole), rest)
            counts[i] = counts[i] + addition
            rest = rest - addition
    return np.array([limit] + counts)


def ragged_sizes(key, count, total, most, lean):
    if count == 2:
        one = jax.random.randint(key, (), max(1, total - most), min(most, total - 1) + 1)
        return jnp.stack([one, total - one])
    lengths = jnp.asarray(profile(count, total, most, lean), jnp.int32)
    pairs = (count - 1) // 2
    source_of, sink = lengths[1:1 + 2 * pairs:2], lengths[2:2 + 2 * pairs:2]
    margin = jnp.minimum(source_of - 1, most - sink)
    moved = jax.random.randint(jax.random.fold_in(key, 1), (pairs,), 0, 1 << 20) % (margin + 1)
    lengths = lengths.at[1:1 + 2 * pairs:2].set(source_of - moved).at[2:2 + 2 * pairs:2].set(sink + moved)
    return lengths[jax.random.permutation(jax.random.fold_in(key, 2), count)]


def bell_draw(stream_key, shape, scale, reach, cuts=(), kind=jnp.bfloat16):
    drawn = scale * jax.random.normal(stream_key, shape, jnp.float32)
    if cuts:
        drawn = drawn * block_scale(stream_key, shape, cuts, -0.22, 0.18)
    return jnp.clip(drawn, -reach, reach).astype(kind)


def heavy_noise(stream_key, dims, scale, bound, cuts, heavy, kind=jnp.bfloat16):
    values = scale * jax.random.normal(stream_key, dims, jnp.float32)
    if cuts:
        values = values * block_scale(stream_key, dims, cuts, -0.22, 0.18)
    return jnp.clip(raised(values, jax.random.fold_in(stream_key, 3), *heavy), -bound, bound).astype(kind)


def setup_inputs(seed: int = 0, part: int = 0) -> dict:
    streams_of = jax.random.split(jax.random.key(seed), 10)
    part_splits = jax.random.split(jax.random.fold_in(streams_of[9], part), 10)
    return {
        "query_input": bell_draw(part_splits[0], (BATCH_DOCUMENTS, CONTEXT_LENGTH, H, DK), 1.0, 6.0, ((0, 2), (1, 4), (2, 2))),
        "key_input": bell_draw(part_splits[1], (BATCH_DOCUMENTS, CONTEXT_LENGTH, NF, H, DK), 1.0, 6.0, ((0, 2), (1, 4), (3, 2))),
        "value_input": bell_draw(part_splits[2], (BATCH_DOCUMENTS, CONTEXT_LENGTH, NF, H, DV), 1.0, 6.0, ((0, 2), (1, 4), (3, 2))),
        "beta_logit": bell_draw(part_splits[3], (BATCH_DOCUMENTS, H, NF, CONTEXT_LENGTH), 1.5, 6.0, ((0, 2), (1, 2), (3, 4)), jnp.float32),
        "gate_logit": draw_gate_logit(jax.random.fold_in(jax.random.fold_in(streams_of[9], part), 71), part),
        "decay_rate": draw_decay_rate(jax.random.fold_in(streams_of[9], 71), part),
        "doc_ids": jax.vmap(lambda own: jnp.searchsorted(jnp.cumsum(ragged_sizes(own, DOCS, NCHUNK, MOSTC, 1)), jnp.arange(NCHUNK), side="right"))(jax.random.split(part_splits[6], BATCH_DOCUMENTS)).reshape((BATCH_DOCUMENTS, NCHUNK)).astype(jnp.int32),
        "out_weight": bell_draw(streams_of[7], (H * DK, D), (H * DV) ** -0.5, 0.125, ((0, 2),)),
        "out_cotangent": heavy_noise(part_splits[8], (BATCH_DOCUMENTS, CONTEXT_LENGTH, D), 1.0, 6.0, ((0, 2), (1, 4)), (1, 2, 4, 2.0)),
    }


def prepare(query_input, key_input, value_input, beta_logit, gate_logit, decay_rate):
    seq_count, length, head_count, key_width = query_input.shape
    value_width = value_input.shape[-1]
    batch = seq_count * head_count
    blocks = length // CH
    span = CH * NF
    query = (query_input * key_width ** (-0.5)).transpose(0, 2, 1, 3).reshape(batch, blocks, CH, key_width)
    squares = lax.optimization_barrier(jnp.sum(key_input * key_input, axis=-1, keepdims=True))
    keys = (key_input * lax.rsqrt(squares + 1e-06)).transpose(0, 3, 1, 2, 4).reshape(batch, blocks, span, key_width)
    values = value_input.transpose(0, 3, 1, 2, 4).reshape(batch, blocks, span, value_width)
    betas = (2.0 * jax.nn.sigmoid(beta_logit)).transpose(0, 1, 3, 2).reshape(batch, blocks, span)
    log_decay = -decay_rate[None, :, None] * jax.nn.softplus(gate_logit)
    spread = jnp.concatenate([log_decay[..., None], jnp.zeros(log_decay.shape + (NF - 1,), log_decay.dtype)], axis=-1)
    cumulative = jnp.cumsum(spread.reshape(batch, blocks, span), axis=-1)
    return tuple((jnp.moveaxis(piece, 1, 0) for piece in (query, keys, values, betas, cumulative)))

def stretch_step(carry_state, pieces):
    query_block, key_block, value_block, beta_block, cumul_block, retain_block = pieces
    highest_level = lax.Precision.HIGHEST
    value_width = value_block.shape[-1]
    total_width = carry_state.shape[-1]
    span = key_block.shape[1]
    entry = carry_state * retain_block[:, None, None]
    token_indices = jnp.arange(span)
    strict = token_indices[:, None] > token_indices[None, :]
    gap = cumul_block[:, :, None] - cumul_block[:, None, :]
    decay_pairs = jnp.exp(jnp.where(strict, gap, 0.0)) * strict
    key_gram = jnp.einsum('nid,njd->nij', key_block, key_block, precision=highest_level)
    lower_factor = jnp.eye(span, dtype=key_gram.dtype) + beta_block[:, :, None] * decay_pairs * key_gram
    growth = jnp.exp(cumul_block)
    right_side = jnp.concatenate([value_block, growth[..., None] * key_block], axis=-1) * beta_block[..., None]
    solved = jax.scipy.linalg.solve_triangular(lower_factor, right_side, lower=True, unit_diagonal=True)
    updates = jnp.pad(solved[..., :value_width], ((0, 0), (0, 0), (0, total_width - value_width)))
    correction = updates - jnp.einsum('nmk,nke->nme', solved[..., value_width:], entry, precision=highest_level)
    read_index = token_indices[NF - 1::NF]
    read_cumul = cumul_block[:, NF - 1::NF]
    visible = token_indices[None, :] <= read_index[:, None]
    read_gap = read_cumul[:, :, None] - cumul_block[:, None, :]
    read_decay = jnp.exp(jnp.where(visible, read_gap, 0.0)) * visible
    query_key = jnp.einsum('ntd,njd->ntj', query_block, key_block, precision=highest_level)
    outputs = jnp.exp(read_cumul)[..., None] * jnp.einsum('ntd,nde->nte', query_block, entry, precision=highest_level)
    outputs = outputs + jnp.einsum('ntj,nje->nte', query_key * read_decay, correction, precision=highest_level)
    last_cumul = cumul_block[:, -1]
    scaled_keys = jnp.exp(last_cumul[:, None] - cumul_block)[..., None] * key_block
    advanced = jnp.exp(last_cumul)[:, None, None] * entry + jnp.einsum('njd,nje->nde', scaled_keys, correction, precision=highest_level)
    return (advanced, outputs)

def reference(query_input, key_input, value_input, beta_logit, gate_logit, decay_rate, doc_ids, out_weight, out_cotangent):
    seq_count, length, head_count, key_width = query_input.shape
    value_width = value_input.shape[-1]
    batch = seq_count * head_count
    previous = jnp.concatenate([jnp.full((seq_count, 1), -1, jnp.int32), doc_ids[:, :-1].astype(jnp.int32)], axis=1)
    retain = jnp.repeat((doc_ids.astype(jnp.int32) == previous).astype(jnp.float32), head_count, axis=0)

    def forward(query, keys, values, betas, gates, rates):
        pieces = prepare(query, keys, values, betas, gates, rates) + (jnp.moveaxis(retain, 1, 0),)
        anchor = jnp.zeros((batch, key_width, value_width), jnp.float32)
        closing, outputs = lax.scan(jax.checkpoint(stretch_step), anchor, pieces)
        return jnp.moveaxis(outputs, 0, 1).reshape(batch, length, value_width)
    core_state, pullback = jax.vjp(forward, query_input.astype(jnp.float32), key_input.astype(jnp.float32), value_input.astype(jnp.float32), beta_logit.astype(jnp.float32), gate_logit.astype(jnp.float32), decay_rate.astype(jnp.float32))
    core_rows = core_state.reshape(seq_count, head_count, length, value_width).transpose(0, 2, 1, 3)
    core_rows = core_rows.reshape(seq_count * length, head_count * value_width).astype(jnp.bfloat16)
    mixed = jnp.dot(core_rows.astype(jnp.float32), out_weight.astype(jnp.float32), preferred_element_type=jnp.float32).astype(jnp.bfloat16)
    mixed = mixed.reshape(seq_count, length, -1)
    cot_rows = out_cotangent.reshape(seq_count * length, -1)
    core_state_grad = jnp.dot(cot_rows.astype(jnp.float32), out_weight.T.astype(jnp.float32), preferred_element_type=jnp.float32)
    core_state_grad = core_state_grad.reshape(seq_count, length, head_count, value_width).transpose(0, 2, 1, 3).reshape(batch, length, value_width)
    gradients = pullback(core_state_grad)
    weight_grad = jnp.dot(cot_rows.T.astype(jnp.float32), core_rows.astype(jnp.float32), preferred_element_type=jnp.float32)
    return (mixed, gradients[0].astype(jnp.bfloat16), gradients[1].astype(jnp.bfloat16), gradients[2].astype(jnp.bfloat16), gradients[3], gradients[4], weight_grad, gradients[5])
```

```python
import functools

import jax
import jax.numpy as jnp
from jax import lax
from jax.experimental import pallas as pl
from jax.experimental.pallas import tpu as pltpu
from jax.sharding import PartitionSpec as P

CH = 64
NF = 3
SPAN = CH * NF
WIDTH = 128
GROUP = 2
FIELDS = 16
F32 = jnp.float32
BF16 = jnp.bfloat16
MESH = pl.DeviceIdType.MESH
BETA, CUMUL, GROWTH, TAIL, READ_CUMUL, READ_GROWTH, INVERSE_BETA, SOFT, READ_SOFT, LAST = range(10)


def iota(shape, dim):
    return lax.broadcasted_iota(jnp.int32, shape, dim)


def rows_of(*parts):
    return jnp.concatenate(parts, axis=0)


def lanes_of(*parts):
    return jnp.concatenate(parts, axis=1)


def split(x):
    high = x.astype(BF16)
    return high, (x - high.astype(F32)).astype(BF16)


def dot(a, b, ta=False, tb=False):
    dims = (((0 if ta else 1,), (1 if tb else 0,)), ((), ()))
    return lax.dot_general(a, b, dims, preferred_element_type=F32)


def folded(p):
    return p[:, :WIDTH] + p[:, WIDTH:]


def mm_exact(a, b):
    return folded(dot(a, lanes_of(*split(b))))


def mm_full(a, b):
    size = a.shape[0]
    b_high, b_low = split(b)
    p = dot(rows_of(*split(a)), lanes_of(b_high, b_low))
    return folded(p[:size]) + p[size:, :WIDTH]


def mm_wide(a, b):
    size = a.shape[0]
    a_high, a_low = split(a)
    b_high, b_low = split(b)
    p = dot(rows_of(a_high, a_low), b_high)
    return p[:size] + p[size:] + dot(a_high, b_low)


def mm_tb(a, b):
    size = a.shape[0]
    a_high, a_low = split(a)
    b_high, b_low = split(b)
    p = dot(rows_of(a_high, a_low), b_high, tb=True)
    return p[:size] + p[size:] + dot(a_high, b_low, tb=True)


def mm_ta(a, b):
    a_high, a_low = split(a)
    b_high, b_low = split(b)
    return folded(dot(a_high, lanes_of(b_high, b_low), ta=True)) + dot(a_low, b_high, ta=True)


def lower_halves(x, size):
    return rows_of(*(x[i : i + size] for i in range(size, x.shape[0], 2 * size)))


def spread_halves(low, size, total):
    zero = jnp.zeros((size, low.shape[1]), low.dtype)
    pieces, taken = [], 0
    for i in range(0, total, size):
        if (i // size) % 2:
            pieces.append(low[taken : taken + size])
            taken += size
        else:
            pieces.append(zero)
    return rows_of(*pieces)


def merge_halves(x, low, size):
    pieces, taken = [], 0
    for i in range(0, x.shape[0], size):
        if (i // size) % 2:
            pieces.append(low[taken : taken + size])
            taken += size
        else:
            pieces.append(x[i : i + size])
    return rows_of(*pieces)


def unit_inverses(lowers):
    lane, sub = iota((8, SPAN), 1), iota((8, SPAN), 0)
    lane_here = iota((8, WIDTH), 1)
    starts = []
    for lower in lowers:
        packed = jnp.zeros((8, SPAN), F32)
        for b in range(SPAN // 8):
            packed = packed + jnp.where(lane // 8 == b, lower[8 * b : 8 * b + 8], 0.0)
        wide = lanes_of(packed, jnp.zeros((8, 2 * WIDTH - SPAN), F32))
        block = jnp.where(sub == lane % 8, 1.0, 0.0)
        for c in range(7):
            index = (lane_here // 8) * 8 + c
            factor = lanes_of(
                *(jnp.take_along_axis(wide[:, at : at + WIDTH], index, axis=1) for at in (0, WIDTH))
            )[:, :SPAN]
            block = block - factor * block[c : c + 1, :]
        starts.append(rows_of(*(jnp.where(lane // 8 == b, block, 0.0) for b in range(SPAN // 8))))
    inverses = starts
    row, column = iota((SPAN, SPAN), 0), iota((SPAN, SPAN), 1)
    for level in range(3, (SPAN - 1).bit_length()):
        size = 1 << level
        here = (lower_halves(row, size) >> level) == (lower_halves(column, size) >> level) + 1
        halves = [
            mm_wide(jnp.where(here, lower_halves(low, size), 0.0), inv)
            for low, inv in zip(lowers, inverses)
        ]
        tails = [
            lower_halves(inv, size) - mm_wide(lower_halves(inv, size), spread_halves(half, size, SPAN))
            for inv, half in zip(inverses, halves)
        ]
        inverses = [merge_halves(inv, tail, size) for inv, tail in zip(inverses, tails)]
    return inverses


def layer_kernel(
    sizes,
    retain_ref, q_ref, k_ref, v_ref, cols_ref, rows_ref, cot_ref, w_ref,
    dq_ref, dk_ref, dv_ref, col_out, row_out, mixed_ref, wg_ref, rate_ref,
    grad_s, th_s, tl_s, u_s, w_s, lg_s, l_s, reads_s, rd_s, r_s,
    map_s, offset_s, pull_s, entry_s, exit_s, ke_s, qe_s, corr_s,
    ein_s, eout_s, gin_s, gout_s, cotf_s, slab_s, slab_t, gath_s, core_s,
    mix_out, mix_in, wg_out, wg_in, rate_in, rate_two,
    e_send, e_recv, g_send, g_recv, cot_send, cot_recv, right_send, left_send, core_recv,
    mix_send, mix_recv, wg_send, wg_recv, rate_send, rate_recv, two_send, two_recv,
):
    n, heads_n, dp_n, groups, stretches = sizes
    me = lax.axis_index("ctx")
    head_me = lax.axis_index("head")
    dp_me = lax.axis_index("dp")
    slab = slab_s.shape[-1]
    share = mix_in.shape[-1]
    scale = WIDTH ** (-0.5)
    every = [(g, s) for g in range(GROUP) for s in range(stretches)]
    partner = {"dp": lax.rem(dp_me + 1, dp_n)}

    barrier = pltpu.get_barrier_semaphore()
    for step in range(1, n):
        pl.semaphore_signal(barrier, inc=1, device_id={"ctx": lax.rem(me + step, n)}, device_id_type=MESH)
    for step in range(1, heads_n):
        pl.semaphore_signal(
            barrier, inc=1, device_id={"head": lax.rem(head_me + step, heads_n)}, device_id_type=MESH
        )
    pl.semaphore_signal(barrier, inc=1, device_id=partner, device_id_type=MESH)

    for d in range(n):
        piece = cot_ref[:, d * slab : (d + 1) * slab].astype(F32)

        @pl.when(me == d)
        def _():
            slab_s[d] = piece

        @pl.when(me != d)
        def _():
            cotf_s[d] = piece

    @pl.when(me == 0)
    def _():
        ein_s[...] = jnp.zeros_like(ein_s)

    @pl.when(me == n - 1)
    def _():
        gin_s[...] = jnp.zeros_like(gin_s)

    rate_ref[...] = jnp.zeros_like(rate_ref)
    pl.semaphore_wait(barrier, n - 1 + heads_n - 1 + 1)

    def remote(src, dst, send, recv, where):
        return pltpu.make_async_remote_copy(
            src_ref=src, dst_ref=dst, send_sem=send, recv_sem=recv, device_id=where, device_id_type=MESH
        )

    def cot_copy(source, target):
        return remote(cotf_s.at[target], slab_s.at[source], cot_send.at[target], cot_recv.at[source], {"ctx": target})

    for d in range(n):

        @pl.when(me != d)
        def _():
            cot_copy(me, d).start()

    def enter_copy(j):
        return remote(eout_s.at[j], ein_s.at[j], e_send.at[j], e_recv.at[j], {"ctx": lax.rem(me + 1, n)})

    def leave_copy(j):
        return remote(gout_s.at[j], gin_s.at[j], g_send.at[j], g_recv.at[j], {"ctx": lax.rem(me + n - 1, n)})

    def core_right(source, j):
        at = gath_s.at[source, j]
        return remote(at, at, right_send.at[source, j], core_recv.at[source, j], {"ctx": lax.rem(me + 1, n)})

    def core_left(source, j):
        at = gath_s.at[source, j]
        return remote(at, at, left_send.at[source, j], core_recv.at[source, j], {"ctx": lax.rem(me + n - 1, n)})

    def mix_copy(d):
        return remote(mix_out.at[d], mix_in.at[head_me], mix_send.at[d], mix_recv.at[head_me], {"head": d})

    def wg_copy(j):
        return remote(wg_out.at[j], wg_in.at[j], wg_send.at[j], wg_recv.at[j], partner)

    def lanes(j):
        return pl.ds(pl.multiple_of(j * (GROUP * WIDTH), WIDTH), GROUP * WIDTH)

    def columns(j, g, s):
        block = cols_ref[j, s]
        return lambda f: block[:, g * FIELDS + f : g * FIELDS + f + 1]

    def unit(j, g, s):
        return j, g * stretches + s

    def local_maps(j):
        eye = iota((SPAN, SPAN), 0) == iota((SPAN, SPAN), 1)
        strict = iota((SPAN, SPAN), 0) > iota((SPAN, SPAN), 1)
        diagonal = iota((WIDTH, WIDTH), 0) == iota((WIDTH, WIDTH), 1)
        visible = iota((CH, SPAN), 0) * NF + (NF - 1) >= iota((CH, SPAN), 1)
        w_rows = w_ref[pl.ds(pl.multiple_of(j * (GROUP * WIDTH), WIDTH), GROUP * WIDTH), :]
        grad = dot(cot_ref[...], w_rows, tb=True)
        grad_s[j] = grad
        lowers, kept = [], []
        for g, s in every:
            at = slice(g * WIDTH, (g + 1) * WIDTH)
            k = k_ref[s * SPAN : (s + 1) * SPAN, lanes(j)][:, at]
            q = q_ref[s * CH : (s + 1) * CH, lanes(j)][:, at]
            col = columns(j, g, s)
            row = rows_ref[j, g * stretches + s]
            cumul_row = row[1:2]
            both = dot(rows_of(k, q), k, tb=True)
            gram, scores = both[:SPAN], both[SPAN:]
            squares = jnp.where(eye, gram, 0.0)
            r = lax.rsqrt(jnp.sum(squares, axis=1, keepdims=True) + 1e-06)
            r_row = lax.rsqrt(jnp.sum(squares, axis=0, keepdims=True) + 1e-06)
            pair = jnp.exp(jnp.where(strict, col(CUMUL) - cumul_row, -1e30)) * r_row
            lower_gain = (col(BETA) * r) * pair
            lower = lower_gain * gram
            read_gain = jnp.exp(
                jnp.where(visible, col(READ_CUMUL)[:CH] - cumul_row, -1e30)
            ) * (r_row * scale)
            reads = read_gain * scores
            here = unit(j, g, s)
            r_s[here] = r
            lg_s[here] = lower_gain
            l_s[here] = lower
            rd_s[here] = read_gain
            reads_s[here] = reads
            lowers.append(lower)
            kept.append((k, q, col, row, r, r_row, reads))
        for (g, s), (k, q, col, row, r, r_row, reads), inverse in zip(every, kept, unit_inverses(lowers)):
            here = unit(j, g, s)
            at = slice(g * WIDTH, (g + 1) * WIDTH)
            th_s[here], tl_s[here] = split(inverse)
            v = v_ref[s * SPAN : (s + 1) * SPAN, lanes(j)][:, at]
            p = dot(rows_of(*split(inverse * row[0:1])), v)
            solved_v = p[:SPAN] + p[SPAN:]
            p = dot(rows_of(*split(inverse * (row[2:3] * r_row))), k)
            solved_k = p[:SPAN] + p[SPAN:]
            u_s[here] = solved_v
            w_s[here] = solved_k
            high, low = split(lanes_of(solved_v, solved_k) * (col(TAIL) * r))
            moved = dot(k, high, ta=True) + dot(k, low, ta=True)
            offset_s[here] = moved[:, :WIDTH]
            map_s[here] = jnp.where(diagonal, col(LAST)[:1], 0.0) - moved[:, WIDTH:]
            route = col(READ_GROWTH)[:CH] * q.astype(F32) - mm_full(reads, solved_k)
            pull_s[here] = mm_ta(route, grad[s * CH : (s + 1) * CH, at])

    def forward(j):
        @pl.when(me > 0)
        def _():
            enter_copy(j).wait_recv()

        entries = {}
        for g in range(GROUP):
            state = ein_s[j, g]
            for s in range(stretches):
                entry = retain_ref[s] * state
                entries[g, s] = entry
                entry_s[unit(j, g, s)] = entry
                state = mm_full(map_s[unit(j, g, s)], entry) + offset_s[unit(j, g, s)]
            eout_s[j, g] = state

        @pl.when(me < n - 1)
        def _():
            enter_copy(j).start()

        for g, s in every:
            here = unit(j, g, s)
            at = slice(g * WIDTH, (g + 1) * WIDTH)
            k = k_ref[s * SPAN : (s + 1) * SPAN, lanes(j)][:, at]
            q = q_ref[s * CH : (s + 1) * CH, lanes(j)][:, at]
            col = columns(j, g, s)
            on_entry = mm_exact(rows_of(k, q), entries[g, s])
            key_entry, query_entry = r_s[here] * on_entry[:SPAN], on_entry[SPAN:]
            correction = u_s[here] - mm_full(w_s[here], entries[g, s])
            core = col(READ_GROWTH)[:CH] * query_entry + mm_full(reads_s[here], correction)
            rounded = core.astype(BF16)
            ke_s[here] = key_entry
            qe_s[here] = query_entry
            corr_s[here] = correction
            core_s[j, s * CH : (s + 1) * CH, at] = rounded
            gath_s[me, j, s * CH : (s + 1) * CH, at] = rounded.astype(F32)

        @pl.when(me < n - 1)
        def _():
            core_right(me, j).start()

        @pl.when(me > 0)
        def _():
            core_left(me, j).start()

    def backward_wave(j):
        @pl.when(me < n - 1)
        def _():
            leave_copy(j).wait_recv()

        for g in range(GROUP):
            state = gin_s[j, g]
            for s in reversed(range(stretches)):
                here = unit(j, g, s)
                exit_s[here] = state
                maps_high, maps_low = split(map_s[here])
                high, low = split(state)
                carried = folded(dot(maps_high, lanes_of(high, low), ta=True)) + dot(maps_low, high, ta=True)
                state = retain_ref[s] * (carried + pull_s[here])
            gout_s[j, g] = state

        @pl.when(me > 0)
        def _():
            leave_copy(j).start()

    def project():
        core = lanes_of(*(core_s[j] for j in range(groups)))

        def columns_of(d):
            return dot(core, w_ref[:, d * share : (d + 1) * share])

        for d in range(heads_n):

            @pl.when(head_me != d)
            def _():
                mix_out[d] = columns_of(d)
                mix_copy(d).start()

        for d in range(heads_n):

            @pl.when(head_me == d)
            def _():
                mix_in[d] = columns_of(d)

    def backward(j):
        lane = iota((8, WIDTH), 1)
        token = iota((CH, 1), 0)
        for g, s in every:
            here = unit(j, g, s)
            at = slice(g * WIDTH, (g + 1) * WIDTH)
            k = k_ref[s * SPAN : (s + 1) * SPAN, lanes(j)][:, at]
            q = q_ref[s * CH : (s + 1) * CH, lanes(j)][:, at]
            v = v_ref[s * SPAN : (s + 1) * SPAN, lanes(j)][:, at].astype(F32)
            col = columns(j, g, s)
            row = rows_ref[j, g * stretches + s]
            beta, growth, tail, read_growth = col(BETA), col(GROWTH), col(TAIL), col(READ_GROWTH)[:CH]
            grad = grad_s[j, s * CH : (s + 1) * CH, at]
            entry, leaving, r = entry_s[here], exit_s[here], r_s[here]
            correction, key_entry, query_entry = corr_s[here], ke_s[here], qe_s[here]
            reads, lower = reads_s[here], l_s[here]
            key_leave = r * mm_exact(k, leaving)
            correction_grad = mm_ta(reads, grad) + tail * key_leave
            high, low = split(correction_grad)
            right_grad = folded(dot(th_s[here], lanes_of(high, low), ta=True)) + dot(tl_s[here], high, ta=True)
            rest_grad = beta * right_grad
            outer = mm_tb(rows_of(right_grad, grad), correction)
            outer_key, outer_read = outer[:SPAN], outer[SPAN:]
            gram_grad = -outer_key * lg_s[here]
            score_grad = outer_read * rd_s[here]
            pairs = outer_key * lower
            read_pairs = outer_read * reads
            tailed = tail * correction
            back = mm_tb(
                rows_of(
                    lanes_of(-growth * rest_grad, tailed),
                    lanes_of(read_growth * grad, jnp.zeros((CH, WIDTH), F32)),
                ),
                lanes_of(entry, leaving),
            )
            high, low = split(rows_of(gram_grad, score_grad))
            both = rows_of(k, q)
            p = dot(rows_of(high, low), k)
            direct = p[: SPAN + CH] + p[SPAN + CH :]
            turned = dot(high, both, ta=True) + dot(low, both, ta=True)
            key_grad = r * back[:SPAN] + direct[:SPAN] + turned
            key = k.astype(F32)
            dk = key_grad - key * (r * r * jnp.sum(key * key_grad, axis=1, keepdims=True))
            dq = back[SPAN:] + direct[SPAN:]
            fill = jnp.zeros((SPAN, 2 * WIDTH - SPAN), F32)
            pairs_fold = folded(lanes_of(pairs, fill))
            tail_pairs = tailed * key_leave
            factor_cumul = -jnp.sum(
                pairs_fold + growth * rest_grad * key_entry + tail_pairs, axis=1, keepdims=True
            )
            beta_grad = jnp.sum(
                right_grad * (v - growth * key_entry) - col(INVERSE_BETA) * pairs_fold, axis=1, keepdims=True
            )
            token_cumul = jnp.sum(
                folded(lanes_of(read_pairs, fill[:CH])) + read_growth * grad * query_entry, axis=1, keepdims=True
            )
            last_grad = jnp.sum(
                jnp.sum(tail_pairs, axis=0, keepdims=True)
                + col(LAST)[:1] * jnp.sum(entry * leaving, axis=0, keepdims=True),
                axis=1, keepdims=True,
            )
            token_cumul = token_cumul + jnp.where(token == CH - 1, last_grad, 0.0)
            row_cumul = jnp.sum(pairs, axis=0, keepdims=True) - jnp.sum(read_pairs, axis=0, keepdims=True)
            rate = (
                jnp.sum(factor_cumul * col(SOFT), axis=0, keepdims=True)
                + jnp.sum(token_cumul * col(READ_SOFT)[:CH], axis=0, keepdims=True)
                + jnp.sum(row_cumul * row[3:4], axis=1, keepdims=True)
            )
            rate_ref[...] = rate_ref[...] - jnp.where(lane == j * GROUP + g, rate, 0.0)
            col_out[j, g * stretches + s, :, 0:1] = beta_grad
            col_out[j, g * stretches + s, :, 1:2] = factor_cumul
            col_out[j, g * stretches + s, :CH, 2:3] = token_cumul
            row_out[j, g * stretches + s] = jnp.broadcast_to(row_cumul, (8, SPAN))
            yield g, s, dq.astype(BF16), dk.astype(BF16), rest_grad.astype(BF16)

    def backward_all(j):
        made = {(g, s): rest for g, s, *rest in backward(j)}
        for s in range(stretches):
            for ref, which, size in ((dq_ref, 0, CH), (dk_ref, 1, SPAN), (dv_ref, 2, SPAN)):
                ref[s * size : (s + 1) * size, lanes(j)] = lanes_of(
                    *(made[g, s][which] for g in range(GROUP))
                )

    def turn_slabs():
        for d in range(n):

            @pl.when(me != d)
            def _():
                cot_copy(d, me).wait_recv()

        for d in range(n):
            slab_t[:, d * WIDTH : (d + 1) * WIDTH] = jnp.transpose(slab_s[d]).astype(BF16)

    def relay(i):
        j = i - me

        @pl.when((j >= 0) & (j < groups))
        def _():
            def from_left(step, carry):
                source = me - step

                @pl.when(source >= 0)
                def _():
                    core_right(source, j).wait_recv()

                    @pl.when(me < n - 1)
                    def _():
                        core_right(source, j).start()

                return carry

            lax.fori_loop(1, n, from_left, 0)

        def from_right(step, carry):
            source = me + step
            late = i - me - 2 * step

            @pl.when((source < n) & (late >= 0) & (late < groups))
            def _():
                core_left(source, late).wait_recv()

                @pl.when(me > 0)
                def _():
                    core_left(source, late).start()

            return carry

        lax.fori_loop(1, n, from_right, 0)

    def step(i, carry):
        @pl.when(i < groups)
        def _():
            local_maps(i)

        @pl.when((i >= me) & (i < groups + me))
        def _():
            forward(i - me)

        back = i - (n - 1 - me)

        @pl.when((back >= 0) & (back < groups))
        def _():
            backward_wave(back)

        @pl.when(i == groups - 1 + me)
        def _():
            project()

        @pl.when(i == groups)
        def _():
            turn_slabs()

        ready = i - (n - 1)

        @pl.when((ready >= 0) & (ready < groups))
        def _():
            backward_all(ready)

        relay(i)
        return carry

    lax.fori_loop(0, groups + 2 * (n - 1), step, 0)

    def rate_copy(source, target):
        return remote(rate_ref, rate_in.at[source], rate_send.at[target], rate_recv.at[source], {"ctx": target})

    for d in range(n):

        @pl.when(me != d)
        def _():
            rate_copy(me, d).start()

    for j in range(groups):
        core = rows_of(*(gath_s[d, j] for d in range(n))).astype(BF16)
        wg_out[j] = dot(slab_t[...], core)
        wg_copy(j).start()

    for d in range(heads_n):

        @pl.when(head_me != d)
        def _():
            remote(
                mix_out.at[d], mix_in.at[d], mix_send.at[d], mix_recv.at[d], {"head": d}
            ).wait_recv()

    mixed_ref[...] = sum(mix_in[d] for d in range(heads_n)).astype(BF16)
    for d in range(n):

        @pl.when(me != d)
        def _():
            rate_copy(d, me).wait_recv()

        @pl.when(me == d)
        def _():
            rate_in[d] = rate_ref[...]

    rate_two[0] = sum(rate_in[d] for d in range(n))
    two = remote(rate_two.at[0], rate_two.at[1], two_send.at[0], two_recv.at[0], partner)
    two.start()
    for d in range(n):

        @pl.when(me != d)
        def _():
            rate_copy(me, d).wait_send()
            cot_copy(me, d).wait_send()

    two.wait()
    rate_ref[...] = rate_two[0] + rate_two[1]
    for j in range(groups):
        wg_copy(j).wait_recv()
        wg_ref[:, j * GROUP * WIDTH : (j + 1) * GROUP * WIDTH] = wg_out[j] + wg_in[j]
    for j in range(groups):
        wg_copy(j).wait_send()
    for d in range(heads_n):

        @pl.when(head_me != d)
        def _():
            mix_copy(d).wait_send()

    def drain(j, carry):
        @pl.when(me < n - 1)
        def _():
            enter_copy(j).wait_send()

        @pl.when(me > 0)
        def _():
            leave_copy(j).wait_send()

        def one(source, inner):
            @pl.when((source <= me) & (me < n - 1))
            def _():
                core_right(source, j).wait_send()

            @pl.when((source >= me) & (me > 0))
            def _():
                core_left(source, j).wait_send()

            return inner

        return lax.fori_loop(0, n, one, carry)

    lax.fori_loop(0, groups, drain, 0)


def on_device(
    query_input, key_input, value_input, beta_logit, gate_logit, decay_rate,
    doc_ids, out_weight, out_cotangent,
):
    high = lax.Precision.HIGHEST
    _, length, heads, width = query_input.shape
    model_width = out_cotangent.shape[-1]
    blocks = length // CH
    groups = heads // GROUP
    n, heads_n, dp_n = (lax.axis_size(axis) for axis in ("ctx", "head", "dp"))
    padded = jnp.concatenate([jnp.full((1, 1), -1, jnp.int32), doc_ids], axis=1)
    window = lax.dynamic_slice_in_dim(padded, lax.axis_index("ctx") * blocks, blocks + 1, 1)
    retain = (window[0, 1:] == window[0, :-1]).astype(F32)

    queries = query_input.reshape(length, heads * width)
    keys = key_input.reshape(length * NF, heads * width)
    values = value_input.reshape(length * NF, heads * width)
    cot_rows = out_cotangent.reshape(length, model_width)

    sigmoid = jax.nn.sigmoid(beta_logit[0])
    betas = (2.0 * sigmoid).reshape(heads, NF, blocks, CH).transpose(0, 2, 3, 1).reshape(heads, blocks, SPAN)
    soft = jax.nn.softplus(gate_logit[0]).reshape(heads, blocks, CH)
    log_decay = -decay_rate[:, None, None] * soft
    ordered = (jnp.arange(CH)[:, None] <= jnp.arange(CH)[None, :]).astype(F32)
    soft_sums = jnp.dot(soft, ordered, precision=high)
    sums = jnp.dot(log_decay, ordered, precision=high)
    cumul = jnp.repeat(sums, NF, axis=-1)
    soft_cumul = jnp.repeat(soft_sums, NF, axis=-1)
    growth = jnp.exp(cumul)
    last = sums[:, :, -1:]

    def long(x):
        return jnp.pad(x, ((0, 0), (0, 0), (0, SPAN - CH)))

    fields = [
        betas, cumul, growth, jnp.exp(last - cumul), long(sums),
        long(jnp.exp(sums) * width ** (-0.5)), 1.0 / betas, soft_cumul, long(soft_sums),
        jnp.broadcast_to(jnp.exp(last), cumul.shape),
    ]
    fields += [jnp.zeros_like(betas)] * (FIELDS - len(fields))
    cols = (
        jnp.stack(fields, axis=-1)
        .reshape(groups, GROUP, blocks, SPAN, FIELDS)
        .transpose(0, 2, 3, 1, 4)
        .reshape(groups, blocks, SPAN, GROUP * FIELDS)
    )
    rows = jnp.stack(
        [betas, cumul, betas * growth, soft_cumul] + [jnp.zeros_like(betas)] * 4, axis=2
    ).reshape(groups, GROUP * blocks, 8, SPAN)

    units = GROUP * blocks
    slab = model_width // n
    share = model_width // heads_n
    lanes = GROUP * width

    def vmem(*shape, dtype=F32):
        return pltpu.VMEM(shape, dtype)

    def dma(*shape):
        return pltpu.SemaphoreType.DMA(shape)

    state = (groups, units, width, width)
    moving = (groups, GROUP, width, width)
    scratch = [
        vmem(groups, length, lanes),
        vmem(groups, units, SPAN, SPAN, dtype=BF16),
        vmem(groups, units, SPAN, SPAN, dtype=BF16),
        vmem(groups, units, SPAN, width),
        vmem(groups, units, SPAN, width),
        vmem(groups, units, SPAN, SPAN),
        vmem(groups, units, SPAN, SPAN),
        vmem(groups, units, CH, SPAN),
        vmem(groups, units, CH, SPAN),
        vmem(groups, units, SPAN, 1),
        vmem(*state), vmem(*state), vmem(*state), vmem(*state), vmem(*state),
        vmem(groups, units, SPAN, width),
        vmem(groups, units, CH, width),
        vmem(groups, units, SPAN, width),
        vmem(*moving), vmem(*moving), vmem(*moving), vmem(*moving),
        vmem(n, length, slab),
        vmem(n, length, slab),
        vmem(slab, n * length, dtype=BF16),
        vmem(n, groups, length, lanes),
        vmem(groups, length, lanes, dtype=BF16),
        vmem(heads_n, length, share),
        vmem(heads_n, length, share),
        vmem(groups, slab, lanes),
        vmem(groups, slab, lanes),
        vmem(n, 8, WIDTH),
        vmem(2, 8, WIDTH),
        dma(groups), dma(groups), dma(groups), dma(groups),
        dma(n), dma(n), dma(n, groups), dma(n, groups), dma(n, groups),
        dma(heads_n), dma(heads_n), dma(groups), dma(groups),
        dma(n), dma(n), dma(1), dma(1),
    ]
    whole = pl.BlockSpec(memory_space=pltpu.VMEM)
    dq, dk, dv, col_out, row_out, mixed, weight_grad, rate = pl.pallas_call(
        functools.partial(layer_kernel, (n, heads_n, dp_n, groups, blocks)),
        in_specs=[pl.BlockSpec(memory_space=pltpu.SMEM)] + [whole] * 7,
        out_specs=[whole] * 8,
        out_shape=[
            jax.ShapeDtypeStruct((length, heads * width), BF16),
            jax.ShapeDtypeStruct((length * NF, heads * width), BF16),
            jax.ShapeDtypeStruct((length * NF, heads * width), BF16),
            jax.ShapeDtypeStruct((groups, units, SPAN, 8), F32),
            jax.ShapeDtypeStruct((groups, units, 8, SPAN), F32),
            jax.ShapeDtypeStruct((length, share), BF16),
            jax.ShapeDtypeStruct((slab, heads * width), F32),
            jax.ShapeDtypeStruct((8, WIDTH), F32),
        ],
        scratch_shapes=scratch,
        compiler_params=pltpu.CompilerParams(
            collective_id=0, has_side_effects=True, vmem_limit_bytes=60 << 20
        ),
        name="layer",
    )(retain, queries, keys, values, cols, rows, cot_rows, out_weight)

    by_factor = col_out.reshape(heads, blocks, CH, NF, 8)
    cumul_grad = (
        jnp.sum(by_factor[..., 1], axis=-1)
        + col_out.reshape(heads, blocks, SPAN, 8)[:, :, :CH, 2]
        + jnp.sum(row_out.reshape(heads, blocks, 8, SPAN)[:, :, 0].reshape(heads, blocks, CH, NF), axis=-1)
    )
    decay_grad = jnp.dot(cumul_grad, ordered.T, precision=high).reshape(heads, length)
    gate_grad = -decay_rate[:, None] * jax.nn.sigmoid(gate_logit[0]) * decay_grad
    beta_grad = by_factor[..., 0].transpose(0, 3, 1, 2).reshape(heads, NF, length)
    beta_grad = beta_grad * (2.0 * sigmoid * (1.0 - sigmoid))
    return (
        mixed[None],
        dq.reshape(query_input.shape),
        dk.reshape(key_input.shape),
        dv.reshape(value_input.shape),
        beta_grad[None],
        gate_grad[None],
        weight_grad,
        rate[0, :heads],
    )


def solution(mesh):
    in_specs = (
        P(("groups", "dp"), "ctx", "head", None),
        P(("groups", "dp"), "ctx", None, "head", None),
        P(("groups", "dp"), "ctx", None, "head", None),
        P(("groups", "dp"), "head", None, "ctx"),
        P(("groups", "dp"), "head", "ctx"),
        P("head"),
        P(("groups", "dp"), None),
        P("head", None),
        P(("groups", "dp"), "ctx", None),
    )
    out_specs = (
        P(("groups", "dp"), "ctx", "head"),
        P(("groups", "dp"), "ctx", "head", None),
        P(("groups", "dp"), "ctx", None, "head", None),
        P(("groups", "dp"), "ctx", None, "head", None),
        P(("groups", "dp"), "head", None, "ctx"),
        P(("groups", "dp"), "head", "ctx"),
        P(("groups", "ctx"), "head"),
        P(("groups", "head")),
    )
    return jax.shard_map(
        on_device, mesh=mesh, in_specs=in_specs, out_specs=out_specs, check_vma=False
    )
```

```python
import functools

import jax
import jax.numpy as jnp
from jax import lax
from jax.experimental import pallas as pl
from jax.experimental.pallas import tpu as pltpu
from jax.sharding import PartitionSpec as P

CH = 64
NF = 3
SPAN = CH * NF
WIDTH = 128
GROUP = 2
FIELDS = 8
F32 = jnp.float32
BF16 = jnp.bfloat16
MESH = pl.DeviceIdType.MESH
BETA, CUMUL, BETA_GROWTH, GROWTH, TAIL, INVERSE_BETA, LAST = range(7)
READ_CUMUL, READ_GROWTH = range(2)


def iota(shape, dim):
    return lax.broadcasted_iota(jnp.int32, shape, dim)


def rows_of(*parts):
    return jnp.concatenate(parts, axis=0)


def lanes_of(*parts):
    return jnp.concatenate(parts, axis=1)


def split(x):
    high = x.astype(BF16)
    return high, (x - high.astype(F32)).astype(BF16)


def dot(a, b, ta=False, tb=False):
    dims = (((0 if ta else 1,), (1 if tb else 0,)), ((), ()))
    return lax.dot_general(a, b, dims, preferred_element_type=F32)


def folded(p):
    return p[:, :WIDTH] + p[:, WIDTH:]


def select(x, chosen):
    high = x.astype(BF16)
    rest = x - high.astype(F32)
    middle = rest.astype(BF16)
    low = (rest - middle.astype(F32)).astype(BF16)
    size = x.shape[0]
    p = dot(rows_of(high.astype(F32), middle.astype(F32), low.astype(F32)).astype(BF16), chosen)
    return (p[2 * size :] + p[size : 2 * size]) + p[:size]


def where_one(condition):
    return jnp.where(condition, 1.0, 0.0).astype(BF16)


def mm_exact(a, b):
    return folded(dot(a, lanes_of(*split(b))))


def mm_full(a, b):
    size = a.shape[0]
    b_high, b_low = split(b)
    p = dot(rows_of(*split(a)), lanes_of(b_high, b_low))
    return folded(p[:size]) + p[size:, :WIDTH]


def mm_wide(a, b):
    size = a.shape[0]
    a_high, a_low = split(a)
    b_high, b_low = split(b)
    p = dot(rows_of(a_high, a_low), b_high)
    return p[:size] + p[size:] + dot(a_high, b_low)


def mm_tb(a, b):
    size = a.shape[0]
    a_high, a_low = split(a)
    b_high, b_low = split(b)
    p = dot(rows_of(a_high, a_low), b_high, tb=True)
    return p[:size] + p[size:] + dot(a_high, b_low, tb=True)


def mm_ta(a, b):
    a_high, a_low = split(a)
    b_high, b_low = split(b)
    return folded(dot(a_high, lanes_of(b_high, b_low), ta=True)) + dot(a_low, b_high, ta=True)


def lower_halves(x, size):
    return rows_of(*(x[i : i + size] for i in range(size, x.shape[0], 2 * size)))


def spread_halves(low, size, total):
    zero = jnp.zeros((size, low.shape[1]), low.dtype)
    pieces, taken = [], 0
    for i in range(0, total, size):
        if (i // size) % 2:
            pieces.append(low[taken : taken + size])
            taken += size
        else:
            pieces.append(zero)
    return rows_of(*pieces)


def merge_halves(x, low, size):
    pieces, taken = [], 0
    for i in range(0, x.shape[0], size):
        if (i // size) % 2:
            pieces.append(low[taken : taken + size])
            taken += size
        else:
            pieces.append(x[i : i + size])
    return rows_of(*pieces)


def unit_inverses(lowers):
    lane, sub = iota((8, SPAN), 1), iota((8, SPAN), 0)
    lane_here = iota((8, WIDTH), 1)
    starts = []
    for lower in lowers:
        packed = jnp.zeros((8, SPAN), F32)
        for b in range(SPAN // 8):
            packed = packed + jnp.where(lane // 8 == b, lower[8 * b : 8 * b + 8], 0.0)
        wide = lanes_of(packed, jnp.zeros((8, 2 * WIDTH - SPAN), F32))
        block = jnp.where(sub == lane % 8, 1.0, 0.0)
        for c in range(7):
            index = (lane_here // 8) * 8 + c
            factor = lanes_of(
                *(jnp.take_along_axis(wide[:, at : at + WIDTH], index, axis=1) for at in (0, WIDTH))
            )[:, :SPAN]
            block = block - factor * block[c : c + 1, :]
        starts.append(rows_of(*(jnp.where(lane // 8 == b, block, 0.0) for b in range(SPAN // 8))))
    inverses = starts
    row, column = iota((SPAN, SPAN), 0), iota((SPAN, SPAN), 1)
    for level in range(3, (SPAN - 1).bit_length()):
        size = 1 << level
        here = (lower_halves(row, size) >> level) == (lower_halves(column, size) >> level) + 1
        halves = [
            mm_wide(jnp.where(here, lower_halves(low, size), 0.0), inv)
            for low, inv in zip(lowers, inverses)
        ]
        tails = [
            lower_halves(inv, size) - mm_wide(lower_halves(inv, size), spread_halves(half, size, SPAN))
            for inv, half in zip(inverses, halves)
        ]
        inverses = [merge_halves(inv, tail, size) for inv, tail in zip(inverses, tails)]
    return inverses


def layer_kernel(
    sizes,
    doc_ref, decay_ref, q_ref, k_ref, v_ref, beta_ref, gate_ref, cot_ref, w_ref,
    dq_ref, dk_ref, dv_ref, beta_out, gate_out, mixed_ref, wg_ref, rate_ref,
    qf_s, kf_s, vf_s, frow_s, trow_s, cols_s, tcols_s, gcol_s, gtok_s, grow_s, gt_s, tt_s,
    grad_s, th_s, tl_s, u_s, w_s, lg_s, l_s, reads_s, rd_s, r_s,
    map_s, offset_s, pull_s, entry_s, exit_s, ke_s, qe_s, corr_s,
    ein_s, eout_s, gin_s, gout_s, cotf_s, slab_s, slab_t, gath_s, core_s,
    mix_out, mix_in, wg_out, wg_in, rate_in, rate_two,
    e_send, e_recv, g_send, g_recv, cot_send, cot_recv, right_send, left_send, core_recv,
    mix_send, mix_recv, wg_send, wg_recv, rate_send, rate_recv, two_send, two_recv,
):
    n, heads_n, dp_n, groups, stretches = sizes
    me = lax.axis_index("ctx")
    head_me = lax.axis_index("head")
    dp_me = lax.axis_index("dp")
    slab = slab_s.shape[-1]
    share = mix_in.shape[-1]
    scale = WIDTH ** (-0.5)
    every = [(g, s) for g in range(GROUP) for s in range(stretches)]
    partner = {"dp": lax.rem(dp_me + 1, dp_n)}

    barrier = pltpu.get_barrier_semaphore()
    for step in range(1, n):
        pl.semaphore_signal(barrier, inc=1, device_id={"ctx": lax.rem(me + step, n)}, device_id_type=MESH)
    for step in range(1, heads_n):
        pl.semaphore_signal(
            barrier, inc=1, device_id={"head": lax.rem(head_me + step, heads_n)}, device_id_type=MESH
        )
    pl.semaphore_signal(barrier, inc=1, device_id=partner, device_id_type=MESH)

    for d in range(n):
        piece = cot_ref[:, d * slab : (d + 1) * slab].astype(F32)

        @pl.when(me == d)
        def _():
            slab_s[d] = piece

        @pl.when(me != d)
        def _():
            cotf_s[d] = piece

    @pl.when(me == 0)
    def _():
        ein_s[...] = jnp.zeros_like(ein_s)

    @pl.when(me == n - 1)
    def _():
        gin_s[...] = jnp.zeros_like(gin_s)

    heads = groups * GROUP
    length = stretches * CH
    factors = length * NF
    qf_s[...] = q_ref[...].astype(F32).reshape(qf_s.shape)
    kf_s[...] = k_ref[...].astype(F32).reshape(kf_s.shape)
    vf_s[...] = v_ref[...].astype(F32).reshape(vf_s.shape)

    before, after = iota((length, length), 0), iota((length, length), 1)
    same = before // CH == after // CH
    up_to = where_one(same & (before <= after))
    closing = where_one(before == (after // CH) * CH + (CH - 1))
    widen = where_one(iota((length, factors), 0) == iota((length, factors), 1) // NF)
    source = iota((factors, factors), 0)
    weave = where_one((source % length) * NF + source // length == iota((factors, factors), 1))
    head_row = iota((heads, 1), 0)
    rate_column = jnp.zeros((heads, 1), F32)
    for h in range(heads):
        rate_column = rate_column + jnp.where(head_row == h, decay_ref[h], 0.0)
    gate = gate_ref[...]
    soft = jnp.maximum(gate, 0.0) + jnp.log1p(jnp.exp(-jnp.abs(gate)))
    sums = select(-rate_column * soft, up_to)
    last = select(sums, closing)
    growth_rows = jnp.exp(sums)
    wide = select(rows_of(sums, growth_rows, jnp.exp(last - sums), jnp.exp(last)), widen)
    beta_rows = select(lanes_of(*(2.0 / (1.0 + jnp.exp(-beta_ref[:, f, :])) for f in range(NF))), weave)
    sums_wide, growth_wide, tail_wide, last_wide = (wide[i * heads : (i + 1) * heads] for i in range(4))
    frow_s[...] = jnp.zeros_like(frow_s)
    trow_s[...] = jnp.zeros_like(trow_s)
    for field, value in (
        (BETA, beta_rows), (CUMUL, sums_wide), (BETA_GROWTH, beta_rows * growth_wide), (GROWTH, growth_wide),
        (TAIL, tail_wide), (INVERSE_BETA, 1.0 / beta_rows), (LAST, last_wide),
    ):
        for h in range(heads):
            frow_s[h * FIELDS + field : h * FIELDS + field + 1, :] = value[h : h + 1]
    for field, value in ((READ_CUMUL, sums), (READ_GROWTH, growth_rows * scale)):
        for h in range(heads):
            trow_s[h * FIELDS + field : h * FIELDS + field + 1, :] = value[h : h + 1]
    turned_fields, turned_tokens = jnp.transpose(frow_s[...]), jnp.transpose(trow_s[...])
    per_group = GROUP * FIELDS
    for j in range(groups):
        cols_s[j, :, :per_group] = turned_fields[:, j * per_group : (j + 1) * per_group]
        tcols_s[j, :, :per_group] = turned_tokens[:, j * per_group : (j + 1) * per_group]
    retains = []
    for s in range(stretches):
        place = me * stretches + s
        kept = doc_ref[0, place] == doc_ref[0, jnp.maximum(place - 1, 0)]
        retains.append(jnp.where(kept & (place > 0), 1.0, 0.0))
    pl.semaphore_wait(barrier, n - 1 + heads_n - 1 + 1)

    def remote(src, dst, send, recv, where):
        return pltpu.make_async_remote_copy(
            src_ref=src, dst_ref=dst, send_sem=send, recv_sem=recv, device_id=where, device_id_type=MESH
        )

    def cot_copy(source, target):
        return remote(cotf_s.at[target], slab_s.at[source], cot_send.at[target], cot_recv.at[source], {"ctx": target})

    for d in range(n):

        @pl.when(me != d)
        def _():
            cot_copy(me, d).start()

    def enter_copy(j):
        return remote(eout_s.at[j], ein_s.at[j], e_send.at[j], e_recv.at[j], {"ctx": lax.rem(me + 1, n)})

    def leave_copy(j):
        return remote(gout_s.at[j], gin_s.at[j], g_send.at[j], g_recv.at[j], {"ctx": lax.rem(me + n - 1, n)})

    def core_right(source, j):
        at = gath_s.at[source, j]
        return remote(at, at, right_send.at[source, j], core_recv.at[source, j], {"ctx": lax.rem(me + 1, n)})

    def core_left(source, j):
        at = gath_s.at[source, j]
        return remote(at, at, left_send.at[source, j], core_recv.at[source, j], {"ctx": lax.rem(me + n - 1, n)})

    def mix_copy(d):
        return remote(mix_out.at[d], mix_in.at[head_me], mix_send.at[d], mix_recv.at[head_me], {"head": d})

    def wg_copy(j):
        return remote(wg_out.at[j], wg_in.at[j], wg_send.at[j], wg_recv.at[j], partner)

    def lanes(j):
        return pl.ds(pl.multiple_of(j * (GROUP * WIDTH), WIDTH), GROUP * WIDTH)

    def columns(j, g, s):
        block = cols_s[j, s * SPAN : (s + 1) * SPAN]
        return lambda f: block[:, g * FIELDS + f : g * FIELDS + f + 1]

    def token_columns(j, g, s):
        block = tcols_s[j, s * CH : (s + 1) * CH]
        return lambda f: block[:, g * FIELDS + f : g * FIELDS + f + 1]

    def field_rows(j, g, s):
        block = frow_s[pl.ds(pl.multiple_of((j * GROUP + g) * FIELDS, FIELDS), FIELDS), :]
        return block[:, s * SPAN : (s + 1) * SPAN]

    def place(j, g, s, size):
        return pl.ds(s * size * heads + j * GROUP + g, size, stride=heads)

    def unit(j, g, s):
        return j, g * stretches + s

    def local_maps(j):
        eye = iota((SPAN, SPAN), 0) == iota((SPAN, SPAN), 1)
        strict = iota((SPAN, SPAN), 0) > iota((SPAN, SPAN), 1)
        diagonal = iota((WIDTH, WIDTH), 0) == iota((WIDTH, WIDTH), 1)
        visible = iota((CH, SPAN), 0) * NF + (NF - 1) >= iota((CH, SPAN), 1)
        w_rows = w_ref[pl.ds(pl.multiple_of(j * (GROUP * WIDTH), WIDTH), GROUP * WIDTH), :]
        grad = dot(cot_ref[...], w_rows, tb=True)
        grad_s[j] = grad
        lowers, kept = [], []
        for g, s in every:
            at = slice(g * WIDTH, (g + 1) * WIDTH)
            k = kf_s[place(j, g, s, SPAN), :].astype(BF16)
            q = qf_s[place(j, g, s, CH), :].astype(BF16)
            col, tok = columns(j, g, s), token_columns(j, g, s)
            row = field_rows(j, g, s)
            cumul_row = row[CUMUL : CUMUL + 1]
            both = dot(rows_of(k, q), k, tb=True)
            gram, scores = both[:SPAN], both[SPAN:]
            squares = jnp.where(eye, gram, 0.0)
            r = lax.rsqrt(jnp.sum(squares, axis=1, keepdims=True) + 1e-06)
            r_row = lax.rsqrt(jnp.sum(squares, axis=0, keepdims=True) + 1e-06)
            pair = jnp.exp(jnp.where(strict, col(CUMUL) - cumul_row, -1e30)) * r_row
            lower_gain = (col(BETA) * r) * pair
            lower = lower_gain * gram
            read_gain = jnp.exp(
                jnp.where(visible, tok(READ_CUMUL) - cumul_row, -1e30)
            ) * (r_row * scale)
            reads = read_gain * scores
            here = unit(j, g, s)
            r_s[here] = r
            lg_s[here] = lower_gain
            l_s[here] = lower
            rd_s[here] = read_gain
            reads_s[here] = reads
            lowers.append(lower)
            kept.append((k, q, col, tok, row, r, r_row, reads))
        for (g, s), (k, q, col, tok, row, r, r_row, reads), inverse in zip(every, kept, unit_inverses(lowers)):
            here = unit(j, g, s)
            at = slice(g * WIDTH, (g + 1) * WIDTH)
            th_s[here], tl_s[here] = split(inverse)
            v = vf_s[place(j, g, s, SPAN), :].astype(BF16)
            p = dot(rows_of(*split(inverse * row[BETA : BETA + 1])), v)
            solved_v = p[:SPAN] + p[SPAN:]
            p = dot(rows_of(*split(inverse * (row[BETA_GROWTH : BETA_GROWTH + 1] * r_row))), k)
            solved_k = p[:SPAN] + p[SPAN:]
            u_s[here] = solved_v
            w_s[here] = solved_k
            high, low = split(lanes_of(solved_v, solved_k) * (col(TAIL) * r))
            moved = dot(k, high, ta=True) + dot(k, low, ta=True)
            offset_s[here] = moved[:, :WIDTH]
            map_s[here] = jnp.where(diagonal, col(LAST)[:1], 0.0) - moved[:, WIDTH:]
            route = tok(READ_GROWTH) * q.astype(F32) - mm_full(reads, solved_k)
            pull_s[here] = mm_ta(route, grad[s * CH : (s + 1) * CH, at])

    def forward(j):
        @pl.when(me > 0)
        def _():
            enter_copy(j).wait_recv()

        entries = {}
        for g in range(GROUP):
            state = ein_s[j, g]
            for s in range(stretches):
                entry = retains[s] * state
                entries[g, s] = entry
                entry_s[unit(j, g, s)] = entry
                state = mm_full(map_s[unit(j, g, s)], entry) + offset_s[unit(j, g, s)]
            eout_s[j, g] = state

        @pl.when(me < n - 1)
        def _():
            enter_copy(j).start()

        for g, s in every:
            here = unit(j, g, s)
            at = slice(g * WIDTH, (g + 1) * WIDTH)
            k = kf_s[place(j, g, s, SPAN), :].astype(BF16)
            q = qf_s[place(j, g, s, CH), :].astype(BF16)
            tok = token_columns(j, g, s)
            on_entry = mm_exact(rows_of(k, q), entries[g, s])
            key_entry, query_entry = r_s[here] * on_entry[:SPAN], on_entry[SPAN:]
            correction = u_s[here] - mm_full(w_s[here], entries[g, s])
            core = tok(READ_GROWTH) * query_entry + mm_full(reads_s[here], correction)
            rounded = core.astype(BF16)
            ke_s[here] = key_entry
            qe_s[here] = query_entry
            corr_s[here] = correction
            core_s[j, s * CH : (s + 1) * CH, at] = rounded
            gath_s[me, j, s * CH : (s + 1) * CH, at] = rounded.astype(F32)

        @pl.when(me < n - 1)
        def _():
            core_right(me, j).start()

        @pl.when(me > 0)
        def _():
            core_left(me, j).start()

    def backward_wave(j):
        @pl.when(me < n - 1)
        def _():
            leave_copy(j).wait_recv()

        for g in range(GROUP):
            state = gin_s[j, g]
            for s in reversed(range(stretches)):
                here = unit(j, g, s)
                exit_s[here] = state
                maps_high, maps_low = split(map_s[here])
                high, low = split(state)
                carried = folded(dot(maps_high, lanes_of(high, low), ta=True)) + dot(maps_low, high, ta=True)
                state = retains[s] * (carried + pull_s[here])
            gout_s[j, g] = state

        @pl.when(me > 0)
        def _():
            leave_copy(j).start()

    def project():
        core = lanes_of(*(core_s[j] for j in range(groups)))

        def columns_of(d):
            return dot(core, w_ref[:, d * share : (d + 1) * share])

        for d in range(heads_n):

            @pl.when(head_me != d)
            def _():
                mix_out[d] = columns_of(d)
                mix_copy(d).start()

        for d in range(heads_n):

            @pl.when(head_me == d)
            def _():
                mix_in[d] = columns_of(d)

    def backward(j):
        token = iota((CH, 1), 0)
        for g, s in every:
            here = unit(j, g, s)
            at = slice(g * WIDTH, (g + 1) * WIDTH)
            key = kf_s[place(j, g, s, SPAN), :]
            v = vf_s[place(j, g, s, SPAN), :]
            k, q = key.astype(BF16), qf_s[place(j, g, s, CH), :].astype(BF16)
            col = columns(j, g, s)
            beta, growth, tail, read_growth = col(BETA), col(GROWTH), col(TAIL), token_columns(j, g, s)(READ_GROWTH)
            grad = grad_s[j, s * CH : (s + 1) * CH, at]
            entry, leaving, r = entry_s[here], exit_s[here], r_s[here]
            correction, key_entry, query_entry = corr_s[here], ke_s[here], qe_s[here]
            reads, lower = reads_s[here], l_s[here]
            key_leave = r * mm_exact(k, leaving)
            correction_grad = mm_ta(reads, grad) + tail * key_leave
            high, low = split(correction_grad)
            right_grad = folded(dot(th_s[here], lanes_of(high, low), ta=True)) + dot(tl_s[here], high, ta=True)
            rest_grad = beta * right_grad
            outer = mm_tb(rows_of(right_grad, grad), correction)
            outer_key, outer_read = outer[:SPAN], outer[SPAN:]
            gram_grad = -outer_key * lg_s[here]
            score_grad = outer_read * rd_s[here]
            pairs = outer_key * lower
            read_pairs = outer_read * reads
            tailed = tail * correction
            back = mm_tb(
                rows_of(
                    lanes_of(-growth * rest_grad, tailed),
                    lanes_of(read_growth * grad, jnp.zeros((CH, WIDTH), F32)),
                ),
                lanes_of(entry, leaving),
            )
            high, low = split(rows_of(gram_grad, score_grad))
            both = rows_of(k, q)
            p = dot(rows_of(high, low), k)
            direct = p[: SPAN + CH] + p[SPAN + CH :]
            turned = dot(high, both, ta=True) + dot(low, both, ta=True)
            key_grad = r * back[:SPAN] + direct[:SPAN] + turned
            dk = key_grad - key * (r * r * jnp.sum(key * key_grad, axis=1, keepdims=True))
            dq = back[SPAN:] + direct[SPAN:]
            fill = jnp.zeros((SPAN, 2 * WIDTH - SPAN), F32)
            pairs_fold = folded(lanes_of(pairs, fill))
            tail_pairs = tailed * key_leave
            factor_cumul = -jnp.sum(
                pairs_fold + growth * rest_grad * key_entry + tail_pairs, axis=1, keepdims=True
            )
            beta_grad = jnp.sum(
                right_grad * (v - growth * key_entry) - col(INVERSE_BETA) * pairs_fold, axis=1, keepdims=True
            )
            token_cumul = jnp.sum(
                folded(lanes_of(read_pairs, fill[:CH])) + read_growth * grad * query_entry, axis=1, keepdims=True
            )
            last_grad = jnp.sum(
                jnp.sum(tail_pairs, axis=0, keepdims=True)
                + col(LAST)[:1] * jnp.sum(entry * leaving, axis=0, keepdims=True),
                axis=1, keepdims=True,
            )
            token_cumul = token_cumul + jnp.where(token == CH - 1, last_grad, 0.0)
            row_cumul = jnp.sum(pairs, axis=0, keepdims=True) - jnp.sum(read_pairs, axis=0, keepdims=True)
            lane_at = g * FIELDS
            rows_here = slice(s * SPAN, (s + 1) * SPAN)
            gcol_s[j, rows_here, lane_at : lane_at + 1] = beta_grad
            gcol_s[j, rows_here, lane_at + 1 : lane_at + 2] = factor_cumul
            gtok_s[j, s * CH : (s + 1) * CH, lane_at : lane_at + 1] = token_cumul
            grow_s[s, pl.ds(j * GROUP + g, 1), :] = row_cumul
            qf_s[place(j, g, s, CH), :] = dq
            kf_s[place(j, g, s, SPAN), :] = dk
            vf_s[place(j, g, s, SPAN), :] = rest_grad

    def finish_local():
        fill = jnp.zeros((factors, WIDTH - groups * per_group), F32)
        gt_s[...] = jnp.transpose(lanes_of(*(gcol_s[j, :, :per_group] for j in range(groups)), fill))
        tt_s[...] = jnp.transpose(lanes_of(*(gtok_s[j, :, :per_group] for j in range(groups)), fill[:length]))

        def field(ref, f):
            return rows_of(*(ref[h * FIELDS + f : h * FIELDS + f + 1, :] for h in range(heads)))

        cumul_wide = field(gt_s, 1) + lanes_of(*(grow_s[s] for s in range(stretches)))
        narrow = where_one(iota((factors, length), 0) // NF == iota((factors, length), 1))
        cumul_grad = select(cumul_wide, narrow) + field(tt_s, 0)
        decay_grad = select(cumul_grad, where_one(same & (before >= after)))
        gate_out[...] = -rate_column * decay_grad / (1.0 + jnp.exp(-gate))
        share_of = jnp.sum(-soft * decay_grad, axis=1, keepdims=True)
        rate_ref[...] = jnp.zeros_like(rate_ref)
        rate_ref[:heads] = jnp.broadcast_to(share_of, (heads, WIDTH))
        target = iota((factors, factors), 1)
        unweave = where_one((target % length) * NF + target // length == iota((factors, factors), 0))
        beta_parts = select(field(gt_s, 0), unweave)
        for f in range(NF):
            sigmoid = 1.0 / (1.0 + jnp.exp(-beta_ref[:, f, :]))
            beta_out[:, f, :] = beta_parts[:, f * length : (f + 1) * length] * (2.0 * sigmoid * (1.0 - sigmoid))
        dq_ref[...] = qf_s[...].reshape(dq_ref.shape).astype(BF16)
        dk_ref[...] = kf_s[...].reshape(dk_ref.shape).astype(BF16)
        dv_ref[...] = vf_s[...].reshape(dv_ref.shape).astype(BF16)

    def turn_slabs():
        for d in range(n):

            @pl.when(me != d)
            def _():
                cot_copy(d, me).wait_recv()

        for d in range(n):
            slab_t[:, d * WIDTH : (d + 1) * WIDTH] = jnp.transpose(slab_s[d]).astype(BF16)

    def relay(i):
        j = i - me

        @pl.when((j >= 0) & (j < groups))
        def _():
            def from_left(step, carry):
                source = me - step

                @pl.when(source >= 0)
                def _():
                    core_right(source, j).wait_recv()

                    @pl.when(me < n - 1)
                    def _():
                        core_right(source, j).start()

                return carry

            lax.fori_loop(1, n, from_left, 0)

        def from_right(step, carry):
            source = me + step
            late = i - me - 2 * step

            @pl.when((source < n) & (late >= 0) & (late < groups))
            def _():
                core_left(source, late).wait_recv()

                @pl.when(me > 0)
                def _():
                    core_left(source, late).start()

            return carry

        lax.fori_loop(1, n, from_right, 0)

    def step(i, carry):
        @pl.when(i < groups)
        def _():
            local_maps(i)

        @pl.when((i >= me) & (i < groups + me))
        def _():
            forward(i - me)

        back = i - (n - 1 - me)

        @pl.when((back >= 0) & (back < groups))
        def _():
            backward_wave(back)

        @pl.when(i == groups - 1 + me)
        def _():
            project()

        @pl.when(i == groups)
        def _():
            turn_slabs()

        ready = i - (n - 1)

        @pl.when((ready >= 0) & (ready < groups))
        def _():
            backward(ready)

        @pl.when(ready == groups - 1)
        def _():
            finish_local()

        relay(i)
        return carry

    lax.fori_loop(0, groups + 2 * (n - 1), step, 0)

    def rate_copy(source, target):
        return remote(rate_ref, rate_in.at[source], rate_send.at[target], rate_recv.at[source], {"ctx": target})

    for d in range(n):

        @pl.when(me != d)
        def _():
            rate_copy(me, d).start()

    for j in range(groups):
        core = rows_of(*(gath_s[d, j] for d in range(n))).astype(BF16)
        wg_out[j] = dot(slab_t[...], core)
        wg_copy(j).start()

    for d in range(heads_n):

        @pl.when(head_me != d)
        def _():
            remote(
                mix_out.at[d], mix_in.at[d], mix_send.at[d], mix_recv.at[d], {"head": d}
            ).wait_recv()

    mixed_ref[...] = sum(mix_in[d] for d in range(heads_n)).astype(BF16)
    for d in range(n):

        @pl.when(me != d)
        def _():
            rate_copy(d, me).wait_recv()

        @pl.when(me == d)
        def _():
            rate_in[d] = rate_ref[...]

    rate_two[0] = sum(rate_in[d] for d in range(n))
    two = remote(rate_two.at[0], rate_two.at[1], two_send.at[0], two_recv.at[0], partner)
    two.start()
    for d in range(n):

        @pl.when(me != d)
        def _():
            rate_copy(me, d).wait_send()
            cot_copy(me, d).wait_send()

    two.wait()
    rate_ref[...] = rate_two[0] + rate_two[1]
    for j in range(groups):
        wg_copy(j).wait_recv()
        wg_ref[:, j * GROUP * WIDTH : (j + 1) * GROUP * WIDTH] = wg_out[j] + wg_in[j]
    for j in range(groups):
        wg_copy(j).wait_send()
    for d in range(heads_n):

        @pl.when(head_me != d)
        def _():
            mix_copy(d).wait_send()

    def drain(j, carry):
        @pl.when(me < n - 1)
        def _():
            enter_copy(j).wait_send()

        @pl.when(me > 0)
        def _():
            leave_copy(j).wait_send()

        def one(source, inner):
            @pl.when((source <= me) & (me < n - 1))
            def _():
                core_right(source, j).wait_send()

            @pl.when((source >= me) & (me > 0))
            def _():
                core_left(source, j).wait_send()

            return inner

        return lax.fori_loop(0, n, one, carry)

    lax.fori_loop(0, groups, drain, 0)


def on_device(
    query_input, key_input, value_input, beta_logit, gate_logit, decay_rate,
    doc_ids, out_weight, out_cotangent,
):
    _, length, heads, width = query_input.shape
    model_width = out_cotangent.shape[-1]
    blocks = length // CH
    groups = heads // GROUP
    factors = length * NF
    n, heads_n, dp_n = (lax.axis_size(axis) for axis in ("ctx", "head", "dp"))
    units = GROUP * blocks
    slab = model_width // n
    share = model_width // heads_n
    lanes = GROUP * width

    def vmem(*shape, dtype=F32):
        return pltpu.VMEM(shape, dtype)

    def dma(*shape):
        return pltpu.SemaphoreType.DMA(shape)

    state = (groups, units, width, width)
    moving = (groups, GROUP, width, width)
    scratch = [
        vmem(length * heads, width), vmem(factors * heads, width), vmem(factors * heads, width),
        vmem(WIDTH, factors), vmem(WIDTH, length),
        vmem(groups, factors, WIDTH), vmem(groups, length, WIDTH),
        vmem(groups, factors, WIDTH), vmem(groups, length, WIDTH),
        vmem(blocks, heads, SPAN), vmem(WIDTH, factors), vmem(WIDTH, length),
        vmem(groups, length, lanes),
        vmem(groups, units, SPAN, SPAN, dtype=BF16),
        vmem(groups, units, SPAN, SPAN, dtype=BF16),
        vmem(groups, units, SPAN, width),
        vmem(groups, units, SPAN, width),
        vmem(groups, units, SPAN, SPAN),
        vmem(groups, units, SPAN, SPAN),
        vmem(groups, units, CH, SPAN),
        vmem(groups, units, CH, SPAN),
        vmem(groups, units, SPAN, 1),
        vmem(*state), vmem(*state), vmem(*state), vmem(*state), vmem(*state),
        vmem(groups, units, SPAN, width),
        vmem(groups, units, CH, width),
        vmem(groups, units, SPAN, width),
        vmem(*moving), vmem(*moving), vmem(*moving), vmem(*moving),
        vmem(n, length, slab),
        vmem(n, length, slab),
        vmem(slab, n * length, dtype=BF16),
        vmem(n, groups, length, lanes),
        vmem(groups, length, lanes, dtype=BF16),
        vmem(heads_n, length, share),
        vmem(heads_n, length, share),
        vmem(groups, slab, lanes),
        vmem(groups, slab, lanes),
        vmem(n, 8, WIDTH),
        vmem(2, 8, WIDTH),
        dma(groups), dma(groups), dma(groups), dma(groups),
        dma(n), dma(n), dma(n, groups), dma(n, groups), dma(n, groups),
        dma(heads_n), dma(heads_n), dma(groups), dma(groups),
        dma(n), dma(n), dma(1), dma(1),
    ]
    whole = pl.BlockSpec(memory_space=pltpu.VMEM)
    scalars = pl.BlockSpec(memory_space=pltpu.SMEM)
    dq, dk, dv, beta_grad, gate_grad, mixed, weight_grad, rate = pl.pallas_call(
        functools.partial(layer_kernel, (n, heads_n, dp_n, groups, blocks)),
        in_specs=[scalars] * 2 + [whole] * 7,
        out_specs=[whole] * 8,
        out_shape=[
            jax.ShapeDtypeStruct((length, heads, width), BF16),
            jax.ShapeDtypeStruct((factors, heads, width), BF16),
            jax.ShapeDtypeStruct((factors, heads, width), BF16),
            jax.ShapeDtypeStruct((heads, NF, length), F32),
            jax.ShapeDtypeStruct((heads, length), F32),
            jax.ShapeDtypeStruct((length, share), BF16),
            jax.ShapeDtypeStruct((slab, heads * width), F32),
            jax.ShapeDtypeStruct((8, WIDTH), F32),
        ],
        scratch_shapes=scratch,
        compiler_params=pltpu.CompilerParams(
            collective_id=0, has_side_effects=True, vmem_limit_bytes=60 << 20
        ),
        name="layer",
    )(
        doc_ids, decay_rate, query_input[0], key_input.reshape(factors, heads, width),
        value_input.reshape(factors, heads, width), beta_logit[0], gate_logit[0], out_cotangent[0], out_weight,
    )
    return (
        mixed[None],
        dq[None],
        dk.reshape(key_input.shape),
        dv.reshape(value_input.shape),
        beta_grad[None],
        gate_grad[None],
        weight_grad,
        rate[:heads, 0],
    )


def solution(mesh):
    in_specs = (
        P(("groups", "dp"), "ctx", "head", None),
        P(("groups", "dp"), "ctx", None, "head", None),
        P(("groups", "dp"), "ctx", None, "head", None),
        P(("groups", "dp"), "head", None, "ctx"),
        P(("groups", "dp"), "head", "ctx"),
        P("head"),
        P(("groups", "dp"), None),
        P("head", None),
        P(("groups", "dp"), "ctx", None),
    )
    out_specs = (
        P(("groups", "dp"), "ctx", "head"),
        P(("groups", "dp"), "ctx", "head", None),
        P(("groups", "dp"), "ctx", None, "head", None),
        P(("groups", "dp"), "ctx", None, "head", None),
        P(("groups", "dp"), "head", None, "ctx"),
        P(("groups", "dp"), "head", "ctx"),
        P(("groups", "ctx"), "head"),
        P(("groups", "head")),
    )
    return jax.shard_map(
        on_device, mesh=mesh, in_specs=in_specs, out_specs=out_specs, check_vma=False
    )
```

```python
import functools

import jax
import jax.numpy as jnp
from jax import lax
from jax.experimental import pallas as pl
from jax.experimental.pallas import tpu as pltpu
from jax.sharding import PartitionSpec as P

CH = 64
NF = 3
SPAN = CH * NF
WIDTH = 128
GROUP = 2
FIELDS = 8
F32 = jnp.float32
BF16 = jnp.bfloat16
MESH = pl.DeviceIdType.MESH
BETA, CUMUL, BETA_GROWTH, GROWTH, TAIL, INVERSE_BETA, LAST = range(7)
READ_CUMUL, READ_GROWTH = range(2)


def iota(shape, dim):
    return lax.broadcasted_iota(jnp.int32, shape, dim)


def rows_of(*parts):
    return jnp.concatenate(parts, axis=0)


def lanes_of(*parts):
    return jnp.concatenate(parts, axis=1)


def split(x):
    high = x.astype(BF16)
    return high, (x - high.astype(F32)).astype(BF16)


def dot(a, b, ta=False, tb=False):
    dims = (((0 if ta else 1,), (1 if tb else 0,)), ((), ()))
    return lax.dot_general(a, b, dims, preferred_element_type=F32)


def folded(p):
    return p[:, :WIDTH] + p[:, WIDTH:]


def select(x, chosen):
    high = x.astype(BF16)
    rest = x - high.astype(F32)
    middle = rest.astype(BF16)
    low = (rest - middle.astype(F32)).astype(BF16)
    size = x.shape[0]
    p = dot(rows_of(high.astype(F32), middle.astype(F32), low.astype(F32)).astype(BF16), chosen)
    return (p[2 * size :] + p[size : 2 * size]) + p[:size]


def where_one(condition):
    return jnp.where(condition, 1.0, 0.0).astype(BF16)


def mm_exact(a, b):
    return folded(dot(a, lanes_of(*split(b))))


def mm_full(a, b):
    size = a.shape[0]
    b_high, b_low = split(b)
    p = dot(rows_of(*split(a)), lanes_of(b_high, b_low))
    return folded(p[:size]) + p[size:, :WIDTH]


def mm_wide(a, b):
    size = a.shape[0]
    a_high, a_low = split(a)
    b_high, b_low = split(b)
    p = dot(rows_of(a_high, a_low), b_high)
    return p[:size] + p[size:] + dot(a_high, b_low)


def mm_tb(a, b):
    size = a.shape[0]
    a_high, a_low = split(a)
    b_high, b_low = split(b)
    p = dot(rows_of(a_high, a_low), b_high, tb=True)
    return p[:size] + p[size:] + dot(a_high, b_low, tb=True)


def mm_ta(a, b):
    a_high, a_low = split(a)
    b_high, b_low = split(b)
    return folded(dot(a_high, lanes_of(b_high, b_low), ta=True)) + dot(a_low, b_high, ta=True)


def lower_halves(x, size):
    return rows_of(*(x[i : i + size] for i in range(size, x.shape[0], 2 * size)))


def spread_halves(low, size, total):
    zero = jnp.zeros((size, low.shape[1]), low.dtype)
    pieces, taken = [], 0
    for i in range(0, total, size):
        if (i // size) % 2:
            pieces.append(low[taken : taken + size])
            taken += size
        else:
            pieces.append(zero)
    return rows_of(*pieces)


def merge_halves(x, low, size):
    pieces, taken = [], 0
    for i in range(0, x.shape[0], size):
        if (i // size) % 2:
            pieces.append(low[taken : taken + size])
            taken += size
        else:
            pieces.append(x[i : i + size])
    return rows_of(*pieces)


def unit_inverses(lowers):
    lane, sub = iota((8, SPAN), 1), iota((8, SPAN), 0)
    lane_here = iota((8, WIDTH), 1)
    starts = []
    for lower in lowers:
        packed = jnp.zeros((8, SPAN), F32)
        for b in range(SPAN // 8):
            packed = packed + jnp.where(lane // 8 == b, lower[8 * b : 8 * b + 8], 0.0)
        wide = lanes_of(packed, jnp.zeros((8, 2 * WIDTH - SPAN), F32))
        block = jnp.where(sub == lane % 8, 1.0, 0.0)
        for c in range(7):
            index = (lane_here // 8) * 8 + c
            factor = lanes_of(
                *(jnp.take_along_axis(wide[:, at : at + WIDTH], index, axis=1) for at in (0, WIDTH))
            )[:, :SPAN]
            block = block - factor * block[c : c + 1, :]
        starts.append(rows_of(*(jnp.where(lane // 8 == b, block, 0.0) for b in range(SPAN // 8))))
    inverses = starts
    row, column = iota((SPAN, SPAN), 0), iota((SPAN, SPAN), 1)
    for level in range(3, (SPAN - 1).bit_length()):
        size = 1 << level
        here = (lower_halves(row, size) >> level) == (lower_halves(column, size) >> level) + 1
        halves = [
            mm_wide(jnp.where(here, lower_halves(low, size), 0.0), inv)
            for low, inv in zip(lowers, inverses)
        ]
        tails = [
            lower_halves(inv, size) - mm_wide(lower_halves(inv, size), spread_halves(half, size, SPAN))
            for inv, half in zip(inverses, halves)
        ]
        inverses = [merge_halves(inv, tail, size) for inv, tail in zip(inverses, tails)]
    return inverses


def layer_kernel(
    sizes,
    doc_ref, decay_ref, q_ref, k_ref, v_ref, beta_ref, gate_ref, cot_ref, w_ref,
    dq_ref, dk_ref, dv_ref, beta_out, gate_out, mixed_ref, wg_ref, rate_ref,
    qf_s, kf_s, vf_s, frow_s, trow_s, cols_s, tcols_s, grow_s, gt_s, tt_s,
    grad_s, th_s, tl_s, u_s, w_s, lg_s, reads_s, rd_s, r_s,
    map_s, offset_s, pull_s, qe_s,
    ein_s, eout_s, gin_s, gout_s, cotf_s, slab_s, slab_t, far_s, far_t, gath_s, core_s,
    mix_out, mix_in, wg_out, wg_in, far_out, far_in, far_sum, end_in, rate_in, rate_two,
    e_send, e_recv, g_send, g_recv, cot_send, cot_recv, far_recv, side_send, side_recv, fars_send, fars_recv,
    right_send, left_send, core_recv,
    mix_send, mix_recv, wg_send, wg_recv, half_send, half_recv, end_send, end_recv,
    rate_send, rate_recv, two_send, two_recv,
):
    n, heads_n, dp_n, groups, stretches = sizes
    me = lax.axis_index("ctx")
    head_me = lax.axis_index("head")
    dp_me = lax.axis_index("dp")
    slab = slab_s.shape[-1]
    share = mix_in.shape[-1]
    scale = WIDTH ** (-0.5)
    every = [(g, s) for g in range(GROUP) for s in range(stretches)]
    partner = {"dp": lax.rem(dp_me + 1, dp_n)}

    barrier = pltpu.get_barrier_semaphore()
    for step in range(1, n):
        pl.semaphore_signal(barrier, inc=1, device_id={"ctx": lax.rem(me + step, n)}, device_id_type=MESH)
    for step in range(1, heads_n):
        pl.semaphore_signal(
            barrier, inc=1, device_id={"head": lax.rem(head_me + step, heads_n)}, device_id_type=MESH
        )
    pl.semaphore_signal(barrier, inc=1, device_id=partner, device_id_type=MESH)

    is_end = (me == 0) | (me == n - 1)
    is_next = (me == 1) | (me == n - 2)
    first_far = jnp.where(me == 1, 1, 0)

    def holder(d):
        return 1 if d == 0 else n - 2 if d == n - 1 else d

    def travels(source, d):
        return (source != d) & (source != holder(d))

    for d in range(n):
        piece = cot_ref[:, d * slab : (d + 1) * slab].astype(F32)

        @pl.when(me == d)
        def _():
            slab_s[d] = piece

        if holder(d) != d:

            @pl.when(me == holder(d))
            def _():
                far_s[holder(d)] = piece

        @pl.when(travels(me, d))
        def _():
            cotf_s[d] = piece

    @pl.when(me == 0)
    def _():
        ein_s[...] = jnp.zeros_like(ein_s)

    @pl.when(me == n - 1)
    def _():
        gin_s[...] = jnp.zeros_like(gin_s)

    heads = groups * GROUP
    length = stretches * CH
    factors = length * NF
    qf_s[...] = q_ref[...].astype(F32).reshape(qf_s.shape)
    kf_s[...] = k_ref[...].astype(F32).reshape(kf_s.shape)
    vf_s[...] = v_ref[...].astype(F32).reshape(vf_s.shape)

    before, after = iota((length, length), 0), iota((length, length), 1)
    same = before // CH == after // CH
    up_to = where_one(same & (before <= after))
    closing = where_one(before == (after // CH) * CH + (CH - 1))
    widen = where_one(iota((length, factors), 0) == iota((length, factors), 1) // NF)
    source = iota((factors, factors), 0)
    weave = where_one((source % length) * NF + source // length == iota((factors, factors), 1))
    head_row = iota((heads, 1), 0)
    rate_column = jnp.zeros((heads, 1), F32)
    for h in range(heads):
        rate_column = rate_column + jnp.where(head_row == h, decay_ref[h], 0.0)
    gate = gate_ref[...]
    soft = jnp.maximum(gate, 0.0) + jnp.log1p(jnp.exp(-jnp.abs(gate)))
    sums = select(-rate_column * soft, up_to)
    last = select(sums, closing)
    growth_rows = jnp.exp(sums)
    wide = select(rows_of(sums, growth_rows, jnp.exp(last - sums), jnp.exp(last)), widen)
    beta_rows = select(lanes_of(*(2.0 / (1.0 + jnp.exp(-beta_ref[:, f, :])) for f in range(NF))), weave)
    sums_wide, growth_wide, tail_wide, last_wide = (wide[i * heads : (i + 1) * heads] for i in range(4))
    frow_s[...] = jnp.zeros_like(frow_s)
    trow_s[...] = jnp.zeros_like(trow_s)
    for field, value in (
        (BETA, beta_rows), (CUMUL, sums_wide), (BETA_GROWTH, beta_rows * growth_wide), (GROWTH, growth_wide),
        (TAIL, tail_wide), (INVERSE_BETA, 1.0 / beta_rows), (LAST, last_wide),
    ):
        for h in range(heads):
            frow_s[h * FIELDS + field : h * FIELDS + field + 1, :] = value[h : h + 1]
    for field, value in ((READ_CUMUL, sums), (READ_GROWTH, growth_rows * scale)):
        for h in range(heads):
            trow_s[h * FIELDS + field : h * FIELDS + field + 1, :] = value[h : h + 1]
    turned_fields, turned_tokens = jnp.transpose(frow_s[...]), jnp.transpose(trow_s[...])
    per_group = GROUP * FIELDS
    for j in range(groups):
        cols_s[j, :, :per_group] = turned_fields[:, j * per_group : (j + 1) * per_group]
        tcols_s[j, :, :per_group] = turned_tokens[:, j * per_group : (j + 1) * per_group]
    retains = []
    for s in range(stretches):
        place = me * stretches + s
        kept = doc_ref[0, place] == doc_ref[0, jnp.maximum(place - 1, 0)]
        retains.append(jnp.where(kept & (place > 0), 1.0, 0.0))
    pl.semaphore_wait(barrier, n - 1 + heads_n - 1 + 1)

    def remote(src, dst, send, recv, where):
        return pltpu.make_async_remote_copy(
            src_ref=src, dst_ref=dst, send_sem=send, recv_sem=recv, device_id=where, device_id_type=MESH
        )

    part = cot_ref.shape[0] // heads_n

    def part_rows(h):
        return pl.ds(pl.multiple_of(h * part, part), part)

    def cot_copy(d):
        mine = part_rows(head_me)
        far = holder(d) != d
        return remote(
            cotf_s.at[d, mine], (far_s if far else slab_s).at[me, mine], cot_send.at[d],
            (far_recv if far else cot_recv).at[me], {"ctx": holder(d)},
        )

    def cot_landed(source, far):
        mine = part_rows(head_me)
        at = (far_s if far else slab_s).at[source, mine]
        return remote(at, at, cot_send.at[0], (far_recv if far else cot_recv).at[source], {"ctx": source})

    def side_copy(source, h, far):
        at = (far_s if far else slab_s).at[source, part_rows(head_me)]
        return remote(
            at, at, (fars_send if far else side_send).at[source, h],
            (fars_recv if far else side_recv).at[source, head_me], {"head": h},
        )

    def side_landed(source, h, far):
        at = (far_s if far else slab_s).at[source, part_rows(h)]
        return remote(
            at, at, (fars_send if far else side_send).at[source, h],
            (fars_recv if far else side_recv).at[source, h], {"head": h},
        )

    def arrivals(what):
        for d in range(n):

            @pl.when((me != d) & jnp.logical_not(is_end))
            def _():
                what(d, False)

            @pl.when(is_next & (me != d) & (d >= first_far) & (d < first_far + n - 1))
            def _():
                what(d, True)

    def to_sides(what):
        for h in range(heads_n):

            @pl.when(head_me != h)
            def _():
                what(h)

    def pass_aside():
        def one(source, far):
            cot_landed(source, far).wait_recv()
            to_sides(lambda h: side_copy(source, h, far).start())

        arrivals(one)

    for d in range(n):

        @pl.when(travels(me, d))
        def _():
            cot_copy(d).start()

    def enter_copy(j):
        return remote(eout_s.at[j], ein_s.at[j], e_send.at[j], e_recv.at[j], {"ctx": lax.rem(me + 1, n)})

    def leave_copy(j):
        return remote(gout_s.at[j], gin_s.at[j], g_send.at[j], g_recv.at[j], {"ctx": lax.rem(me + n - 1, n)})

    def core_right(source, j):
        at = gath_s.at[source, j]
        return remote(at, at, right_send.at[source, j], core_recv.at[source, j], {"ctx": lax.rem(me + 1, n)})

    def core_left(source, j):
        at = gath_s.at[source, j]
        return remote(at, at, left_send.at[source, j], core_recv.at[source, j], {"ctx": lax.rem(me + n - 1, n)})

    def mix_copy(d):
        return remote(mix_out.at[d], mix_in.at[head_me], mix_send.at[d], mix_recv.at[head_me], {"head": d})

    half = far_in.shape[1]

    def half_rows(index):
        return pl.ds(pl.multiple_of(index * half, half), half)

    def half_copy(j):
        other = lax.rem(dp_me + 1, dp_n)
        return remote(far_out.at[j, half_rows(other)], far_in.at[j], half_send.at[j], half_recv.at[j], partner)

    def end_copy(j):
        return remote(
            far_sum.at[j], end_in.at[j], end_send.at[j], end_recv.at[j], {"ctx": jnp.where(me == 1, 0, n - 1)}
        )

    def wg_copy(j):
        return remote(wg_out.at[j], wg_in.at[j], wg_send.at[j], wg_recv.at[j], partner)

    def lanes(j):
        return pl.ds(pl.multiple_of(j * (GROUP * WIDTH), WIDTH), GROUP * WIDTH)

    def columns(j, g, s):
        block = cols_s[j, s * SPAN : (s + 1) * SPAN]
        return lambda f: block[:, g * FIELDS + f : g * FIELDS + f + 1]

    def token_columns(j, g, s):
        block = tcols_s[j, s * CH : (s + 1) * CH]
        return lambda f: block[:, g * FIELDS + f : g * FIELDS + f + 1]

    def field_rows(j, g, s):
        block = frow_s[pl.ds(pl.multiple_of((j * GROUP + g) * FIELDS, FIELDS), FIELDS), :]
        return block[:, s * SPAN : (s + 1) * SPAN]

    def place(j, g, s, size):
        return pl.ds(s * size * heads + j * GROUP + g, size, stride=heads)

    def unit(j, g, s):
        return j, g * stretches + s

    def local_maps(j):
        eye = iota((SPAN, SPAN), 0) == iota((SPAN, SPAN), 1)
        strict = iota((SPAN, SPAN), 0) > iota((SPAN, SPAN), 1)
        diagonal = iota((WIDTH, WIDTH), 0) == iota((WIDTH, WIDTH), 1)
        visible = iota((CH, SPAN), 0) * NF + (NF - 1) >= iota((CH, SPAN), 1)
        w_rows = w_ref[pl.ds(pl.multiple_of(j * (GROUP * WIDTH), WIDTH), GROUP * WIDTH), :]
        grad = dot(cot_ref[...], w_rows, tb=True)
        grad_s[j] = grad
        lowers, kept = [], []
        for g, s in every:
            at = slice(g * WIDTH, (g + 1) * WIDTH)
            k = kf_s[place(j, g, s, SPAN), :].astype(BF16)
            q = qf_s[place(j, g, s, CH), :].astype(BF16)
            col, tok = columns(j, g, s), token_columns(j, g, s)
            row = field_rows(j, g, s)
            cumul_row = row[CUMUL : CUMUL + 1]
            both = dot(rows_of(k, q), k, tb=True)
            gram, scores = both[:SPAN], both[SPAN:]
            squares = jnp.where(eye, gram, 0.0)
            r = lax.rsqrt(jnp.sum(squares, axis=1, keepdims=True) + 1e-06)
            r_row = lax.rsqrt(jnp.sum(squares, axis=0, keepdims=True) + 1e-06)
            pair = jnp.exp(jnp.where(strict, col(CUMUL) - cumul_row, -1e30)) * r_row
            lower_gain = (col(BETA) * r) * pair
            lower = lower_gain * gram
            read_gain = jnp.exp(
                jnp.where(visible, tok(READ_CUMUL) - cumul_row, -1e30)
            ) * (r_row * scale)
            reads = read_gain * scores
            here = unit(j, g, s)
            r_s[here] = r
            lg_s[here] = lower_gain
            rd_s[here] = read_gain
            reads_s[here] = reads
            lowers.append(lower)
            kept.append((k, q, col, tok, row, r, r_row, reads))
        for (g, s), (k, q, col, tok, row, r, r_row, reads), inverse in zip(every, kept, unit_inverses(lowers)):
            here = unit(j, g, s)
            at = slice(g * WIDTH, (g + 1) * WIDTH)
            th_s[here], tl_s[here] = split(inverse)
            v = vf_s[place(j, g, s, SPAN), :].astype(BF16)
            p = dot(rows_of(*split(inverse * row[BETA : BETA + 1])), v)
            solved_v = p[:SPAN] + p[SPAN:]
            p = dot(rows_of(*split(inverse * (row[BETA_GROWTH : BETA_GROWTH + 1] * r_row))), k)
            solved_k = p[:SPAN] + p[SPAN:]
            u_s[here] = solved_v
            w_s[here] = solved_k
            high, low = split(lanes_of(solved_v, solved_k) * (col(TAIL) * r))
            moved = dot(k, high, ta=True) + dot(k, low, ta=True)
            offset_s[here] = moved[:, :WIDTH]
            map_s[here] = jnp.where(diagonal, col(LAST)[:1], 0.0) - moved[:, WIDTH:]
            route = tok(READ_GROWTH) * q.astype(F32) - mm_full(reads, solved_k)
            pull_s[here] = mm_ta(route, grad[s * CH : (s + 1) * CH, at])

    def forward(j):
        @pl.when(me > 0)
        def _():
            enter_copy(j).wait_recv()

        entries = {}
        for g in range(GROUP):
            state = ein_s[j, g]
            for s in range(stretches):
                entry = retains[s] * state
                entries[g, s] = entry
                state = mm_full(map_s[unit(j, g, s)], entry) + offset_s[unit(j, g, s)]
                offset_s[unit(j, g, s)] = entry
            eout_s[j, g] = state

        @pl.when(me < n - 1)
        def _():
            enter_copy(j).start()

        for g, s in every:
            here = unit(j, g, s)
            at = slice(g * WIDTH, (g + 1) * WIDTH)
            k = kf_s[place(j, g, s, SPAN), :].astype(BF16)
            q = qf_s[place(j, g, s, CH), :].astype(BF16)
            tok = token_columns(j, g, s)
            on_entry = mm_exact(rows_of(k, q), entries[g, s])
            key_entry, query_entry = r_s[here] * on_entry[:SPAN], on_entry[SPAN:]
            correction = u_s[here] - mm_full(w_s[here], entries[g, s])
            core = tok(READ_GROWTH) * query_entry + mm_full(reads_s[here], correction)
            rounded = core.astype(BF16)
            w_s[here] = key_entry
            qe_s[here] = query_entry
            u_s[here] = correction
            core_s[j, s * CH : (s + 1) * CH, at] = rounded
            gath_s[me, j, s * CH : (s + 1) * CH, at] = rounded.astype(F32)

        @pl.when(me < n - 2)
        def _():
            core_right(me, j).start()

        @pl.when(me > 1)
        def _():
            core_left(me, j).start()

    def backward_wave(j):
        @pl.when(me < n - 1)
        def _():
            leave_copy(j).wait_recv()

        for g in range(GROUP):
            state = gin_s[j, g]
            for s in reversed(range(stretches)):
                here = unit(j, g, s)
                maps_high, maps_low = split(map_s[here])
                high, low = split(state)
                carried = folded(dot(maps_high, lanes_of(high, low), ta=True)) + dot(maps_low, high, ta=True)
                before = retains[s] * (carried + pull_s[here])
                pull_s[here] = state
                state = before
            gout_s[j, g] = state

        @pl.when(me > 0)
        def _():
            leave_copy(j).start()

    def project():
        core = lanes_of(*(core_s[j] for j in range(groups)))

        def columns_of(d):
            return dot(core, w_ref[:, d * share : (d + 1) * share])

        for d in range(heads_n):

            @pl.when(head_me != d)
            def _():
                mix_out[d] = columns_of(d)
                mix_copy(d).start()

        for d in range(heads_n):

            @pl.when(head_me == d)
            def _():
                mix_in[d] = columns_of(d)

    def backward(j):
        token = iota((CH, 1), 0)
        for g, s in every:
            here = unit(j, g, s)
            at = slice(g * WIDTH, (g + 1) * WIDTH)
            key = kf_s[place(j, g, s, SPAN), :]
            v = vf_s[place(j, g, s, SPAN), :]
            k, q = key.astype(BF16), qf_s[place(j, g, s, CH), :].astype(BF16)
            col = columns(j, g, s)
            beta, growth, tail, read_growth = col(BETA), col(GROWTH), col(TAIL), token_columns(j, g, s)(READ_GROWTH)
            grad = grad_s[j, s * CH : (s + 1) * CH, at]
            entry, leaving, r = offset_s[here], pull_s[here], r_s[here]
            correction, key_entry, query_entry = u_s[here], w_s[here], qe_s[here]
            reads = reads_s[here]
            key_leave = r * mm_exact(k, leaving)
            correction_grad = mm_ta(reads, grad) + tail * key_leave
            high, low = split(correction_grad)
            right_grad = folded(dot(th_s[here], lanes_of(high, low), ta=True)) + dot(tl_s[here], high, ta=True)
            rest_grad = beta * right_grad
            outer = mm_tb(rows_of(right_grad, grad), correction)
            outer_key, outer_read = outer[:SPAN], outer[SPAN:]
            gram_grad = -outer_key * lg_s[here]
            score_grad = outer_read * rd_s[here]
            pairs = -gram_grad * dot(k, k, tb=True)
            read_pairs = outer_read * reads
            tailed = tail * correction
            back = mm_tb(
                rows_of(
                    lanes_of(-growth * rest_grad, tailed),
                    lanes_of(read_growth * grad, jnp.zeros((CH, WIDTH), F32)),
                ),
                lanes_of(entry, leaving),
            )
            high, low = split(rows_of(gram_grad, score_grad))
            both = rows_of(k, q)
            p = dot(rows_of(high, low), k)
            direct = p[: SPAN + CH] + p[SPAN + CH :]
            turned = dot(high, both, ta=True) + dot(low, both, ta=True)
            key_grad = r * back[:SPAN] + direct[:SPAN] + turned
            dk = key_grad - key * (r * r * jnp.sum(key * key_grad, axis=1, keepdims=True))
            dq = back[SPAN:] + direct[SPAN:]
            fill = jnp.zeros((SPAN, 2 * WIDTH - SPAN), F32)
            pairs_fold = folded(lanes_of(pairs, fill))
            tail_pairs = tailed * key_leave
            factor_cumul = -jnp.sum(
                pairs_fold + growth * rest_grad * key_entry + tail_pairs, axis=1, keepdims=True
            )
            beta_grad = jnp.sum(
                right_grad * (v - growth * key_entry) - col(INVERSE_BETA) * pairs_fold, axis=1, keepdims=True
            )
            token_cumul = jnp.sum(
                folded(lanes_of(read_pairs, fill[:CH])) + read_growth * grad * query_entry, axis=1, keepdims=True
            )
            last_grad = jnp.sum(
                jnp.sum(tail_pairs, axis=0, keepdims=True)
                + col(LAST)[:1] * jnp.sum(entry * leaving, axis=0, keepdims=True),
                axis=1, keepdims=True,
            )
            token_cumul = token_cumul + jnp.where(token == CH - 1, last_grad, 0.0)
            row_cumul = jnp.sum(pairs, axis=0, keepdims=True) - jnp.sum(read_pairs, axis=0, keepdims=True)
            lane_at = WIDTH // 2 + g * FIELDS
            rows_here = slice(s * SPAN, (s + 1) * SPAN)
            cols_s[j, rows_here, lane_at : lane_at + 1] = beta_grad
            cols_s[j, rows_here, lane_at + 1 : lane_at + 2] = factor_cumul
            tcols_s[j, s * CH : (s + 1) * CH, lane_at : lane_at + 1] = token_cumul
            grow_s[s, pl.ds(j * GROUP + g, 1), :] = row_cumul
            qf_s[place(j, g, s, CH), :] = dq
            kf_s[place(j, g, s, SPAN), :] = dk
            vf_s[place(j, g, s, SPAN), :] = rest_grad

    def finish_local():
        fill = jnp.zeros((factors, WIDTH - groups * per_group), F32)
        gt_s[...] = jnp.transpose(lanes_of(*(cols_s[j, :, WIDTH // 2 : WIDTH // 2 + per_group] for j in range(groups)), fill))
        tt_s[...] = jnp.transpose(lanes_of(*(tcols_s[j, :, WIDTH // 2 : WIDTH // 2 + per_group] for j in range(groups)), fill[:length]))

        def field(ref, f):
            return rows_of(*(ref[h * FIELDS + f : h * FIELDS + f + 1, :] for h in range(heads)))

        cumul_wide = field(gt_s, 1) + lanes_of(*(grow_s[s] for s in range(stretches)))
        narrow = where_one(iota((factors, length), 0) // NF == iota((factors, length), 1))
        cumul_grad = select(cumul_wide, narrow) + field(tt_s, 0)
        decay_grad = select(cumul_grad, where_one(same & (before >= after)))
        gate_out[...] = -rate_column * decay_grad / (1.0 + jnp.exp(-gate))
        share_of = jnp.sum(-soft * decay_grad, axis=1, keepdims=True)
        rate_ref[...] = jnp.zeros_like(rate_ref)
        rate_ref[:heads] = jnp.broadcast_to(share_of, (heads, WIDTH))
        target = iota((factors, factors), 1)
        unweave = where_one((target % length) * NF + target // length == iota((factors, factors), 0))
        beta_parts = select(field(gt_s, 0), unweave)
        for f in range(NF):
            sigmoid = 1.0 / (1.0 + jnp.exp(-beta_ref[:, f, :]))
            beta_out[:, f, :] = beta_parts[:, f * length : (f + 1) * length] * (2.0 * sigmoid * (1.0 - sigmoid))
        dq_ref[...] = qf_s[...].reshape(dq_ref.shape).astype(BF16)
        dk_ref[...] = kf_s[...].reshape(dk_ref.shape).astype(BF16)
        dv_ref[...] = vf_s[...].reshape(dv_ref.shape).astype(BF16)

    def turn_slabs():
        def landed(source, far):
            to_sides(lambda h: side_landed(source, h, far).wait_recv())

        arrivals(landed)

        @pl.when(is_end)
        def _():
            slab_t[:, :length] = jnp.transpose(slab_s[me]).astype(BF16)

        @pl.when(jnp.logical_not(is_end))
        def _():
            for d in range(n):
                slab_t[:, d * length : (d + 1) * length] = jnp.transpose(slab_s[d]).astype(BF16)

        @pl.when(is_next)
        def _():
            for d in range(n - 1):
                far_t[:, d * length : (d + 1) * length] = jnp.transpose(far_s[first_far + d]).astype(BF16)

    def own_weight(j):
        wg_out[j] = dot(slab_t[...], rows_of(*(gath_s[d, j] for d in range(n))).astype(BF16))
        wg_copy(j).start()

    def far_weight(j):
        far_out[j] = dot(far_t[...], rows_of(*(gath_s[first_far + d, j] for d in range(n - 1))).astype(BF16))
        half_copy(j).start()

    def far_pass(j):
        half_copy(j).wait_recv()
        far_sum[j] = far_out[j, half_rows(dp_me)] + far_in[j]
        end_copy(j).start()

    def end_weight(j):
        wg_out[j] = dot(slab_t[:, :length], gath_s[me, j].astype(BF16))
        end_landed = remote(
            far_sum.at[j], end_in.at[j], end_send.at[j], end_recv.at[j], {"ctx": jnp.where(me == 0, 1, n - 2)}
        )
        end_landed.wait_recv()
        mine = half_rows(dp_me)
        wg_out[j, mine] = wg_out[j, mine] + end_in[j]
        wg_copy(j).start()

    def relay(i):
        j = i - me - (groups - 1)

        @pl.when((j >= 0) & (j < groups) & (me < n - 1))
        def _():
            def from_left(step, carry):
                source = me - step

                @pl.when(source >= 0)
                def _():
                    core_right(source, j).wait_recv()

                    @pl.when(me < n - 2)
                    def _():
                        core_right(source, j).start()

                return carry

            lax.fori_loop(1, n, from_left, 0)

        def from_right(step, carry):
            source = me + step
            late = i - me - 2 * step

            @pl.when((source < n) & (late >= 0) & (late < groups) & (me > 0))
            def _():
                core_left(source, late).wait_recv()

                @pl.when(me > 1)
                def _():
                    core_left(source, late).start()

            return carry

        lax.fori_loop(1, n, from_right, 0)

    def when_group(j, condition, what):
        @pl.when((j >= 0) & (j < groups) & condition)
        def _():
            what(j)

    def step(i, carry):
        @pl.when(i < groups)
        def _():
            local_maps(i)

        @pl.when((i >= me) & (i < groups + me))
        def _():
            forward(i - me)

        back = i - (n - 1 - me)

        @pl.when((back >= 0) & (back < groups))
        def _():
            backward_wave(back)

        @pl.when(i == groups - 1 + me)
        def _():
            project()

        @pl.when(i == min(groups - 1, 2))
        def _():
            pass_aside()

        @pl.when(i == groups)
        def _():
            turn_slabs()

        relay(i)
        far = i - jnp.where(me == 1, 2 * n - 3, n - 2 + groups - 1)
        when_group(far - 1, is_next, far_pass)
        when_group(far, is_next, far_weight)
        when_group(i - jnp.maximum(2 * (n - 1) - me, me + groups - 1), jnp.logical_not(is_end), own_weight)
        ready = i - (n - 1 + 0)

        @pl.when((ready >= 0) & (ready < groups))
        def _():
            backward(ready)

        @pl.when(ready == groups - 1)
        def _():
            finish_local()

        return carry

    lax.fori_loop(0, groups + 2 * (n - 1), step, 0)

    def rate_copy(source, target):
        return remote(rate_ref, rate_in.at[source], rate_send.at[target], rate_recv.at[source], {"ctx": target})

    for d in range(n):

        @pl.when(me != d)
        def _():
            rate_copy(me, d).start()

    for j in range(groups):
        when_group(j, is_end, end_weight)

    for d in range(heads_n):

        @pl.when(head_me != d)
        def _():
            remote(
                mix_out.at[d], mix_in.at[d], mix_send.at[d], mix_recv.at[d], {"head": d}
            ).wait_recv()

    mixed_ref[...] = sum(mix_in[d] for d in range(heads_n)).astype(BF16)
    for d in range(n):

        @pl.when(me != d)
        def _():
            rate_copy(d, me).wait_recv()

        @pl.when(me == d)
        def _():
            rate_in[d] = rate_ref[...]

    rate_two[0] = sum(rate_in[d] for d in range(n))
    two = remote(rate_two.at[0], rate_two.at[1], two_send.at[0], two_recv.at[0], partner)
    two.start()
    for d in range(n):

        @pl.when(me != d)
        def _():
            rate_copy(me, d).wait_send()

    two.wait()
    rate_ref[...] = rate_two[0] + rate_two[1]
    for j in range(groups):
        wg_copy(j).wait_recv()
        wg_ref[:, j * GROUP * WIDTH : (j + 1) * GROUP * WIDTH] = wg_out[j] + wg_in[j]
    for j in range(groups):
        wg_copy(j).wait_send()
    for d in range(heads_n):

        @pl.when(head_me != d)
        def _():
            mix_copy(d).wait_send()

    for d in range(n):

        @pl.when(travels(me, d))
        def _():
            cot_copy(d).wait_send()

    arrivals(lambda source, far: to_sides(lambda h: side_copy(source, h, far).wait_send()))

    def drain(j, carry):
        @pl.when(is_next)
        def _():
            half_copy(j).wait_send()
            end_copy(j).wait_send()

        @pl.when(me < n - 1)
        def _():
            enter_copy(j).wait_send()

        @pl.when(me > 0)
        def _():
            leave_copy(j).wait_send()

        def one(source, inner):
            @pl.when((source <= me) & (me < n - 2))
            def _():
                core_right(source, j).wait_send()

            @pl.when((source >= me) & (me > 1))
            def _():
                core_left(source, j).wait_send()

            return inner

        return lax.fori_loop(0, n, one, carry)

    lax.fori_loop(0, groups, drain, 0)


def on_device(
    query_input, key_input, value_input, beta_logit, gate_logit, decay_rate,
    doc_ids, out_weight, out_cotangent,
):
    _, length, heads, width = query_input.shape
    model_width = out_cotangent.shape[-1]
    blocks = length // CH
    groups = heads // GROUP
    factors = length * NF
    n, heads_n, dp_n = (lax.axis_size(axis) for axis in ("ctx", "head", "dp"))
    units = GROUP * blocks
    slab = model_width // n
    share = model_width // heads_n
    lanes = GROUP * width

    def vmem(*shape, dtype=F32):
        return pltpu.VMEM(shape, dtype)

    def dma(*shape):
        return pltpu.SemaphoreType.DMA(shape)

    state = (groups, units, width, width)
    moving = (groups, GROUP, width, width)
    scratch = [
        vmem(length * heads, width), vmem(factors * heads, width), vmem(factors * heads, width),
        vmem(WIDTH, factors), vmem(WIDTH, length),
        vmem(groups, factors, WIDTH), vmem(groups, length, WIDTH),
        vmem(blocks, heads, SPAN), vmem(WIDTH, factors), vmem(WIDTH, length),
        vmem(groups, length, lanes),
        vmem(groups, units, SPAN, SPAN, dtype=BF16),
        vmem(groups, units, SPAN, SPAN, dtype=BF16),
        vmem(groups, units, SPAN, width),
        vmem(groups, units, SPAN, width),
        vmem(groups, units, SPAN, SPAN),
        vmem(groups, units, CH, SPAN),
        vmem(groups, units, CH, SPAN),
        vmem(groups, units, SPAN, 1),
        vmem(*state), vmem(*state), vmem(*state),
        vmem(groups, units, CH, width),
        vmem(*moving), vmem(*moving), vmem(*moving), vmem(*moving),
        vmem(n, length, slab),
        vmem(n, length, slab),
        vmem(slab, n * length, dtype=BF16),
        vmem(n, length, slab),
        vmem(slab, (n - 1) * length, dtype=BF16),
        vmem(n, groups, length, lanes),
        vmem(groups, length, lanes, dtype=BF16),
        vmem(heads_n, length, share),
        vmem(heads_n, length, share),
        vmem(groups, slab, lanes),
        vmem(groups, slab, lanes),
        vmem(groups, slab, lanes),
        vmem(groups, slab // dp_n, lanes),
        vmem(groups, slab // dp_n, lanes),
        vmem(groups, slab // dp_n, lanes),
        vmem(n, 8, WIDTH),
        vmem(2, 8, WIDTH),
        dma(groups), dma(groups), dma(groups), dma(groups),
        dma(n), dma(n), dma(n), dma(n, heads_n), dma(n, heads_n), dma(n, heads_n), dma(n, heads_n),
        dma(n, groups), dma(n, groups), dma(n, groups),
        dma(heads_n), dma(heads_n), dma(groups), dma(groups), dma(groups), dma(groups), dma(groups), dma(groups),
        dma(n), dma(n), dma(1), dma(1),
    ]
    whole = pl.BlockSpec(memory_space=pltpu.VMEM)
    scalars = pl.BlockSpec(memory_space=pltpu.SMEM)
    dq, dk, dv, beta_grad, gate_grad, mixed, weight_grad, rate = pl.pallas_call(
        functools.partial(layer_kernel, (n, heads_n, dp_n, groups, blocks)),
        in_specs=[scalars] * 2 + [whole] * 7,
        out_specs=[whole] * 8,
        out_shape=[
            jax.ShapeDtypeStruct((length, heads, width), BF16),
            jax.ShapeDtypeStruct((factors, heads, width), BF16),
            jax.ShapeDtypeStruct((factors, heads, width), BF16),
            jax.ShapeDtypeStruct((heads, NF, length), F32),
            jax.ShapeDtypeStruct((heads, length), F32),
            jax.ShapeDtypeStruct((length, share), BF16),
            jax.ShapeDtypeStruct((slab, heads * width), F32),
            jax.ShapeDtypeStruct((8, WIDTH), F32),
        ],
        scratch_shapes=scratch,
        compiler_params=pltpu.CompilerParams(
            collective_id=0, has_side_effects=True, vmem_limit_bytes=61 << 20
        ),
        name="layer",
    )(
        doc_ids, decay_rate, query_input[0], key_input.reshape(factors, heads, width),
        value_input.reshape(factors, heads, width), beta_logit[0], gate_logit[0], out_cotangent[0], out_weight,
    )
    return (
        mixed[None],
        dq[None],
        dk.reshape(key_input.shape),
        dv.reshape(value_input.shape),
        beta_grad[None],
        gate_grad[None],
        weight_grad,
        rate[:heads, 0],
    )


def solution(mesh):
    in_specs = (
        P(("groups", "dp"), "ctx", "head", None),
        P(("groups", "dp"), "ctx", None, "head", None),
        P(("groups", "dp"), "ctx", None, "head", None),
        P(("groups", "dp"), "head", None, "ctx"),
        P(("groups", "dp"), "head", "ctx"),
        P("head"),
        P(("groups", "dp"), None),
        P("head", None),
        P(("groups", "dp"), "ctx", None),
    )
    out_specs = (
        P(("groups", "dp"), "ctx", "head"),
        P(("groups", "dp"), "ctx", "head", None),
        P(("groups", "dp"), "ctx", None, "head", None),
        P(("groups", "dp"), "ctx", None, "head", None),
        P(("groups", "dp"), "head", None, "ctx"),
        P(("groups", "dp"), "head", "ctx"),
        P(("groups", "ctx"), "head"),
        P(("groups", "head")),
    )
    return jax.shard_map(
        on_device, mesh=mesh, in_specs=in_specs, out_specs=out_specs, check_vma=False
    )
```

```python
import functools

import jax
import jax.numpy as jnp
from jax import lax
from jax.experimental import pallas as pl
from jax.experimental.pallas import tpu as pltpu
from jax.sharding import PartitionSpec as P

CH = 64
NF = 3
SPAN = CH * NF
WIDTH = 128
GROUP = 2
FIELDS = 8
F32 = jnp.float32
BF16 = jnp.bfloat16
MESH = pl.DeviceIdType.MESH
BETA, CUMUL, BETA_GROWTH, GROWTH, TAIL, INVERSE_BETA, LAST = range(7)
READ_CUMUL, READ_GROWTH = range(2)


def iota(shape, dim):
    return lax.broadcasted_iota(jnp.int32, shape, dim)


def rows_of(*parts):
    return jnp.concatenate(parts, axis=0)


def lanes_of(*parts):
    return jnp.concatenate(parts, axis=1)


def split(x):
    high = x.astype(BF16)
    return high, (x - high.astype(F32)).astype(BF16)


def dot(a, b, ta=False, tb=False):
    dims = (((0 if ta else 1,), (1 if tb else 0,)), ((), ()))
    return lax.dot_general(a, b, dims, preferred_element_type=F32)


def folded(p):
    return p[:, :WIDTH] + p[:, WIDTH:]


def select(x, chosen):
    high = x.astype(BF16)
    rest = x - high.astype(F32)
    middle = rest.astype(BF16)
    low = (rest - middle.astype(F32)).astype(BF16)
    size = x.shape[0]
    p = dot(rows_of(high.astype(F32), middle.astype(F32), low.astype(F32)).astype(BF16), chosen)
    return (p[2 * size :] + p[size : 2 * size]) + p[:size]


def where_one(condition):
    return jnp.where(condition, 1.0, 0.0).astype(BF16)


def mm_exact(a, b):
    return folded(dot(a, lanes_of(*split(b))))


def mm_full(a, b):
    size = a.shape[0]
    b_high, b_low = split(b)
    p = dot(rows_of(*split(a)), lanes_of(b_high, b_low))
    return folded(p[:size]) + p[size:, :WIDTH]


def mm_wide(a, b):
    size = a.shape[0]
    a_high, a_low = split(a)
    b_high, b_low = split(b)
    p = dot(rows_of(a_high, a_low), b_high)
    return p[:size] + p[size:] + dot(a_high, b_low)


def mm_tb(a, b):
    size = a.shape[0]
    a_high, a_low = split(a)
    b_high, b_low = split(b)
    p = dot(rows_of(a_high, a_low), b_high, tb=True)
    return p[:size] + p[size:] + dot(a_high, b_low, tb=True)


def mm_ta(a, b):
    a_high, a_low = split(a)
    b_high, b_low = split(b)
    return folded(dot(a_high, lanes_of(b_high, b_low), ta=True)) + dot(a_low, b_high, ta=True)


def lower_halves(x, size):
    return rows_of(*(x[i : i + size] for i in range(size, x.shape[0], 2 * size)))


def spread_halves(low, size, total):
    zero = jnp.zeros((size, low.shape[1]), low.dtype)
    pieces, taken = [], 0
    for i in range(0, total, size):
        if (i // size) % 2:
            pieces.append(low[taken : taken + size])
            taken += size
        else:
            pieces.append(zero)
    return rows_of(*pieces)


def merge_halves(x, low, size):
    pieces, taken = [], 0
    for i in range(0, x.shape[0], size):
        if (i // size) % 2:
            pieces.append(low[taken : taken + size])
            taken += size
        else:
            pieces.append(x[i : i + size])
    return rows_of(*pieces)


def unit_inverses(lowers):
    lane, sub = iota((8, SPAN), 1), iota((8, SPAN), 0)
    lane_here = iota((8, WIDTH), 1)
    starts = []
    for lower in lowers:
        packed = jnp.zeros((8, SPAN), F32)
        for b in range(SPAN // 8):
            packed = packed + jnp.where(lane // 8 == b, lower[8 * b : 8 * b + 8], 0.0)
        wide = lanes_of(packed, jnp.zeros((8, 2 * WIDTH - SPAN), F32))
        block = jnp.where(sub == lane % 8, 1.0, 0.0)
        for c in range(7):
            index = (lane_here // 8) * 8 + c
            factor = lanes_of(
                *(jnp.take_along_axis(wide[:, at : at + WIDTH], index, axis=1) for at in (0, WIDTH))
            )[:, :SPAN]
            block = block - factor * block[c : c + 1, :]
        starts.append(rows_of(*(jnp.where(lane // 8 == b, block, 0.0) for b in range(SPAN // 8))))
    inverses = starts
    row, column = iota((SPAN, SPAN), 0), iota((SPAN, SPAN), 1)
    for level in range(3, (SPAN - 1).bit_length()):
        size = 1 << level
        here = (lower_halves(row, size) >> level) == (lower_halves(column, size) >> level) + 1
        halves = [
            mm_wide(jnp.where(here, lower_halves(low, size), 0.0), inv)
            for low, inv in zip(lowers, inverses)
        ]
        tails = [
            lower_halves(inv, size) - mm_wide(lower_halves(inv, size), spread_halves(half, size, SPAN))
            for inv, half in zip(inverses, halves)
        ]
        inverses = [merge_halves(inv, tail, size) for inv, tail in zip(inverses, tails)]
    return inverses


def layer_kernel(
    sizes,
    doc_ref, decay_ref, q_ref, k_ref, v_ref, beta_ref, gate_ref, cot_ref, w_in,
    dq_out, dk_out, dv_out, beta_out, gate_out, mixed_ref, wg_ref, rate_ref,
    w_ref, dq_ref, dk_ref, dv_ref, own_sems, weight_sems,
    qf_s, kf_s, vf_s, frow_s, trow_s, cols_s, tcols_s, grow_s, gt_s, tt_s,
    grad_s, th_s, tl_s, u_s, w_s, lg_s, reads_s, rd_s, r_s,
    map_s, offset_s, pull_s, qe_s,
    ein_s, eout_s, gin_s, gout_s, cotf_s, slab_s, slab_t, far_s, far_t, gath_s, core_s,
    mix_out, mix_in, wg_out, wg_in, far_out, far_in, far_sum, end_in, rate_in, rate_two,
    e_send, e_recv, g_send, g_recv, cot_send, cot_recv, far_recv, side_send, side_recv, fars_send, fars_recv,
    right_send, left_send, core_recv,
    mix_send, mix_recv, wg_send, wg_recv, half_send, half_recv, end_send, end_recv,
    rate_send, rate_recv, two_send, two_recv,
):
    n, heads_n, dp_n, groups, stretches = sizes
    me = lax.axis_index("ctx")
    head_me = lax.axis_index("head")
    dp_me = lax.axis_index("dp")
    slab = slab_s.shape[-1]
    share = mix_in.shape[-1]
    scale = WIDTH ** (-0.5)
    every = [(g, s) for g in range(GROUP) for s in range(stretches)]
    partner = {"dp": lax.rem(dp_me + 1, dp_n)}

    load_w = pltpu.make_async_copy(w_in, w_ref, own_sems.at[0])
    load_w.start()
    barrier = pltpu.get_barrier_semaphore()
    for step in range(1, n):
        pl.semaphore_signal(barrier, inc=1, device_id={"ctx": lax.rem(me + step, n)}, device_id_type=MESH)
    for step in range(1, heads_n):
        pl.semaphore_signal(
            barrier, inc=1, device_id={"head": lax.rem(head_me + step, heads_n)}, device_id_type=MESH
        )
    pl.semaphore_signal(barrier, inc=1, device_id=partner, device_id_type=MESH)

    is_end = (me == 0) | (me == n - 1)
    is_next = (me == 1) | (me == n - 2)
    first_far = jnp.where(me == 1, 1, 0)

    def holder(d):
        return 1 if d == 0 else n - 2 if d == n - 1 else d

    def travels(source, d):
        return (source != d) & (source != holder(d))

    for d in range(n):
        piece = cot_ref[:, d * slab : (d + 1) * slab].astype(F32)

        @pl.when(me == d)
        def _():
            slab_s[d] = piece

        if holder(d) != d:

            @pl.when(me == holder(d))
            def _():
                far_s[holder(d)] = piece

        @pl.when(travels(me, d))
        def _():
            cotf_s[d] = piece

    @pl.when(me == 0)
    def _():
        ein_s[...] = jnp.zeros_like(ein_s)

    @pl.when(me == n - 1)
    def _():
        gin_s[...] = jnp.zeros_like(gin_s)

    heads = groups * GROUP
    length = stretches * CH
    factors = length * NF
    qf_s[...] = q_ref[...].astype(F32).reshape(qf_s.shape)
    kf_s[...] = k_ref[...].astype(F32).reshape(kf_s.shape)
    vf_s[...] = v_ref[...].astype(F32).reshape(vf_s.shape)

    before, after = iota((length, length), 0), iota((length, length), 1)
    same = before // CH == after // CH
    up_to = where_one(same & (before <= after))
    closing = where_one(before == (after // CH) * CH + (CH - 1))
    widen = where_one(iota((length, factors), 0) == iota((length, factors), 1) // NF)
    source = iota((factors, factors), 0)
    weave = where_one((source % length) * NF + source // length == iota((factors, factors), 1))
    head_row = iota((heads, 1), 0)
    rate_column = jnp.zeros((heads, 1), F32)
    for h in range(heads):
        rate_column = rate_column + jnp.where(head_row == h, decay_ref[h], 0.0)
    gate = gate_ref[...]
    soft = jnp.maximum(gate, 0.0) + jnp.log1p(jnp.exp(-jnp.abs(gate)))
    sums = select(-rate_column * soft, up_to)
    last = select(sums, closing)
    growth_rows = jnp.exp(sums)
    wide = select(rows_of(sums, growth_rows, jnp.exp(last - sums), jnp.exp(last)), widen)
    beta_rows = select(lanes_of(*(2.0 / (1.0 + jnp.exp(-beta_ref[f])) for f in range(NF))), weave)
    sums_wide, growth_wide, tail_wide, last_wide = (wide[i * heads : (i + 1) * heads] for i in range(4))
    frow_s[...] = jnp.zeros_like(frow_s)
    trow_s[...] = jnp.zeros_like(trow_s)
    for field, value in (
        (BETA, beta_rows), (CUMUL, sums_wide), (BETA_GROWTH, beta_rows * growth_wide), (GROWTH, growth_wide),
        (TAIL, tail_wide), (INVERSE_BETA, 1.0 / beta_rows), (LAST, last_wide),
    ):
        for h in range(heads):
            frow_s[h * FIELDS + field : h * FIELDS + field + 1, :] = value[h : h + 1]
    for field, value in ((READ_CUMUL, sums), (READ_GROWTH, growth_rows * scale)):
        for h in range(heads):
            trow_s[h * FIELDS + field : h * FIELDS + field + 1, :] = value[h : h + 1]
    turned_fields, turned_tokens = jnp.transpose(frow_s[...]), jnp.transpose(trow_s[...])
    per_group = GROUP * FIELDS
    for j in range(groups):
        cols_s[j, :, :per_group] = turned_fields[:, j * per_group : (j + 1) * per_group]
        tcols_s[j, :, :per_group] = turned_tokens[:, j * per_group : (j + 1) * per_group]
    retains = []
    for s in range(stretches):
        place = me * stretches + s
        kept = doc_ref[0, place] == doc_ref[0, jnp.maximum(place - 1, 0)]
        retains.append(jnp.where(kept & (place > 0), 1.0, 0.0))
    pl.semaphore_wait(barrier, n - 1 + heads_n - 1 + 1)

    def remote(src, dst, send, recv, where):
        return pltpu.make_async_remote_copy(
            src_ref=src, dst_ref=dst, send_sem=send, recv_sem=recv, device_id=where, device_id_type=MESH
        )

    part = cot_ref.shape[0] // heads_n

    def part_rows(h):
        return pl.ds(pl.multiple_of(h * part, part), part)

    def cot_copy(d):
        mine = part_rows(head_me)
        far = holder(d) != d
        return remote(
            cotf_s.at[d, mine], (far_s if far else slab_s).at[me, mine], cot_send.at[d],
            (far_recv if far else cot_recv).at[me], {"ctx": holder(d)},
        )

    def cot_landed(source, far):
        mine = part_rows(head_me)
        at = (far_s if far else slab_s).at[source, mine]
        return remote(at, at, cot_send.at[0], (far_recv if far else cot_recv).at[source], {"ctx": source})

    def side_copy(source, h, far):
        at = (far_s if far else slab_s).at[source, part_rows(head_me)]
        return remote(
            at, at, (fars_send if far else side_send).at[source, h],
            (fars_recv if far else side_recv).at[source, head_me], {"head": h},
        )

    def side_landed(source, h, far):
        at = (far_s if far else slab_s).at[source, part_rows(h)]
        return remote(
            at, at, (fars_send if far else side_send).at[source, h],
            (fars_recv if far else side_recv).at[source, h], {"head": h},
        )

    def arrivals(what):
        for d in range(n):

            @pl.when((me != d) & jnp.logical_not(is_end))
            def _():
                what(d, False)

            @pl.when(is_next & (me != d) & (d >= first_far) & (d < first_far + n - 1))
            def _():
                what(d, True)

    def to_sides(what):
        for h in range(heads_n):

            @pl.when(head_me != h)
            def _():
                what(h)

    def pass_aside():
        def one(source, far):
            cot_landed(source, far).wait_recv()
            to_sides(lambda h: side_copy(source, h, far).start())

        arrivals(one)

    for d in range(n):

        @pl.when(travels(me, d))
        def _():
            cot_copy(d).start()

    def enter_copy(j):
        return remote(eout_s.at[j], ein_s.at[j], e_send.at[j], e_recv.at[j], {"ctx": lax.rem(me + 1, n)})

    def leave_copy(j):
        return remote(gout_s.at[j], gin_s.at[j], g_send.at[j], g_recv.at[j], {"ctx": lax.rem(me + n - 1, n)})

    def core_right(source, j):
        at = gath_s.at[source, j]
        return remote(at, at, right_send.at[source, j], core_recv.at[source, j], {"ctx": lax.rem(me + 1, n)})

    def core_left(source, j):
        at = gath_s.at[source, j]
        return remote(at, at, left_send.at[source, j], core_recv.at[source, j], {"ctx": lax.rem(me + n - 1, n)})

    def mix_copy(d):
        return remote(mix_out.at[d], mix_in.at[head_me], mix_send.at[d], mix_recv.at[head_me], {"head": d})

    half = far_in.shape[1]

    def half_rows(index):
        return pl.ds(pl.multiple_of(index * half, half), half)

    def half_copy(j):
        other = lax.rem(dp_me + 1, dp_n)
        return remote(far_out.at[j, half_rows(other)], far_in.at[j], half_send.at[j], half_recv.at[j], partner)

    def end_copy(j):
        return remote(
            far_sum.at[j], end_in.at[j], end_send.at[j], end_recv.at[j], {"ctx": jnp.where(me == 1, 0, n - 1)}
        )

    def wg_copy(j):
        return remote(wg_out.at[j], wg_in.at[j], wg_send.at[j], wg_recv.at[j], partner)

    def lanes(j):
        return pl.ds(pl.multiple_of(j * (GROUP * WIDTH), WIDTH), GROUP * WIDTH)

    def columns(j, g, s):
        block = cols_s[j, s * SPAN : (s + 1) * SPAN]
        return lambda f: block[:, g * FIELDS + f : g * FIELDS + f + 1]

    def token_columns(j, g, s):
        block = tcols_s[j, s * CH : (s + 1) * CH]
        return lambda f: block[:, g * FIELDS + f : g * FIELDS + f + 1]

    def field_rows(j, g, s):
        block = frow_s[pl.ds(pl.multiple_of((j * GROUP + g) * FIELDS, FIELDS), FIELDS), :]
        return block[:, s * SPAN : (s + 1) * SPAN]

    def place(j, g, s, size):
        return pl.ds(s * size * heads + j * GROUP + g, size, stride=heads)

    def unit(j, g, s):
        return j, g * stretches + s

    def local_maps(j):
        eye = iota((SPAN, SPAN), 0) == iota((SPAN, SPAN), 1)
        strict = iota((SPAN, SPAN), 0) > iota((SPAN, SPAN), 1)
        diagonal = iota((WIDTH, WIDTH), 0) == iota((WIDTH, WIDTH), 1)
        visible = iota((CH, SPAN), 0) * NF + (NF - 1) >= iota((CH, SPAN), 1)
        w_rows = w_ref[pl.ds(pl.multiple_of(j * (GROUP * WIDTH), WIDTH), GROUP * WIDTH), :]
        grad = dot(cot_ref[...], w_rows, tb=True)
        grad_s[j] = grad
        lowers, kept = [], []
        for g, s in every:
            at = slice(g * WIDTH, (g + 1) * WIDTH)
            k = kf_s[place(j, g, s, SPAN), :].astype(BF16)
            q = qf_s[place(j, g, s, CH), :].astype(BF16)
            col, tok = columns(j, g, s), token_columns(j, g, s)
            row = field_rows(j, g, s)
            cumul_row = row[CUMUL : CUMUL + 1]
            both = dot(rows_of(k, q), k, tb=True)
            gram, scores = both[:SPAN], both[SPAN:]
            squares = jnp.where(eye, gram, 0.0)
            r = lax.rsqrt(jnp.sum(squares, axis=1, keepdims=True) + 1e-06)
            r_row = lax.rsqrt(jnp.sum(squares, axis=0, keepdims=True) + 1e-06)
            pair = jnp.exp(jnp.where(strict, col(CUMUL) - cumul_row, -1e30)) * r_row
            lower_gain = (col(BETA) * r) * pair
            lower = lower_gain * gram
            read_gain = jnp.exp(
                jnp.where(visible, tok(READ_CUMUL) - cumul_row, -1e30)
            ) * (r_row * scale)
            reads = read_gain * scores
            here = unit(j, g, s)
            r_s[here] = r
            lg_s[here] = lower_gain
            rd_s[here] = read_gain
            reads_s[here] = reads
            lowers.append(lower)
            kept.append((k, q, col, tok, row, r, r_row, reads))
        for (g, s), (k, q, col, tok, row, r, r_row, reads), inverse in zip(every, kept, unit_inverses(lowers)):
            here = unit(j, g, s)
            at = slice(g * WIDTH, (g + 1) * WIDTH)
            th_s[here], tl_s[here] = split(inverse)
            v = vf_s[place(j, g, s, SPAN), :].astype(BF16)
            p = dot(rows_of(*split(inverse * row[BETA : BETA + 1])), v)
            solved_v = p[:SPAN] + p[SPAN:]
            p = dot(rows_of(*split(inverse * (row[BETA_GROWTH : BETA_GROWTH + 1] * r_row))), k)
            solved_k = p[:SPAN] + p[SPAN:]
            u_s[here] = solved_v
            w_s[here] = solved_k
            high, low = split(lanes_of(solved_v, solved_k) * (col(TAIL) * r))
            moved = dot(k, high, ta=True) + dot(k, low, ta=True)
            offset_s[here] = moved[:, :WIDTH]
            map_s[here] = jnp.where(diagonal, col(LAST)[:1], 0.0) - moved[:, WIDTH:]
            route = tok(READ_GROWTH) * q.astype(F32) - mm_full(reads, solved_k)
            pull_s[here] = mm_ta(route, grad[s * CH : (s + 1) * CH, at])

    def forward(j):
        @pl.when(me > 0)
        def _():
            enter_copy(j).wait_recv()

        entries = {}
        for g in range(GROUP):
            state = ein_s[j, g]
            for s in range(stretches):
                entry = retains[s] * state
                entries[g, s] = entry
                state = mm_full(map_s[unit(j, g, s)], entry) + offset_s[unit(j, g, s)]
                offset_s[unit(j, g, s)] = entry
            eout_s[j, g] = state

        @pl.when(me < n - 1)
        def _():
            enter_copy(j).start()

        for g, s in every:
            here = unit(j, g, s)
            at = slice(g * WIDTH, (g + 1) * WIDTH)
            k = kf_s[place(j, g, s, SPAN), :].astype(BF16)
            q = qf_s[place(j, g, s, CH), :].astype(BF16)
            tok = token_columns(j, g, s)
            on_entry = mm_exact(rows_of(k, q), entries[g, s])
            key_entry, query_entry = r_s[here] * on_entry[:SPAN], on_entry[SPAN:]
            correction = u_s[here] - mm_full(w_s[here], entries[g, s])
            core = tok(READ_GROWTH) * query_entry + mm_full(reads_s[here], correction)
            rounded = core.astype(BF16)
            w_s[here] = key_entry
            qe_s[here] = query_entry
            u_s[here] = correction
            core_s[j, s * CH : (s + 1) * CH, at] = rounded
            gath_s[me, j, s * CH : (s + 1) * CH, at] = rounded.astype(F32)

        @pl.when(me < n - 2)
        def _():
            core_right(me, j).start()

        @pl.when(me > 1)
        def _():
            core_left(me, j).start()

    def backward_wave(j):
        @pl.when(me < n - 1)
        def _():
            leave_copy(j).wait_recv()

        for g in range(GROUP):
            state = gin_s[j, g]
            for s in reversed(range(stretches)):
                here = unit(j, g, s)
                maps_high, maps_low = split(map_s[here])
                high, low = split(state)
                carried = folded(dot(maps_high, lanes_of(high, low), ta=True)) + dot(maps_low, high, ta=True)
                before = retains[s] * (carried + pull_s[here])
                pull_s[here] = state
                state = before
            gout_s[j, g] = state

        @pl.when(me > 0)
        def _():
            leave_copy(j).start()

    def project():
        core = lanes_of(*(core_s[j] for j in range(groups)))

        def columns_of(d):
            return dot(core, w_ref[:, d * share : (d + 1) * share])

        for d in range(heads_n):

            @pl.when(head_me != d)
            def _():
                mix_out[d] = columns_of(d)
                mix_copy(d).start()

        for d in range(heads_n):

            @pl.when(head_me == d)
            def _():
                mix_in[d] = columns_of(d)

    def backward(j):
        token = iota((CH, 1), 0)
        for g, s in every:
            here = unit(j, g, s)
            at = slice(g * WIDTH, (g + 1) * WIDTH)
            key = kf_s[place(j, g, s, SPAN), :]
            v = vf_s[place(j, g, s, SPAN), :]
            k, q = key.astype(BF16), qf_s[place(j, g, s, CH), :].astype(BF16)
            col = columns(j, g, s)
            beta, growth, tail, read_growth = col(BETA), col(GROWTH), col(TAIL), token_columns(j, g, s)(READ_GROWTH)
            grad = grad_s[j, s * CH : (s + 1) * CH, at]
            entry, leaving, r = offset_s[here], pull_s[here], r_s[here]
            correction, key_entry, query_entry = u_s[here], w_s[here], qe_s[here]
            reads = reads_s[here]
            key_leave = r * mm_exact(k, leaving)
            correction_grad = mm_ta(reads, grad) + tail * key_leave
            high, low = split(correction_grad)
            right_grad = folded(dot(th_s[here], lanes_of(high, low), ta=True)) + dot(tl_s[here], high, ta=True)
            rest_grad = beta * right_grad
            outer = mm_tb(rows_of(right_grad, grad), correction)
            outer_key, outer_read = outer[:SPAN], outer[SPAN:]
            gram_grad = -outer_key * lg_s[here]
            score_grad = outer_read * rd_s[here]
            pairs = -gram_grad * dot(k, k, tb=True)
            read_pairs = outer_read * reads
            tailed = tail * correction
            back = mm_tb(
                rows_of(
                    lanes_of(-growth * rest_grad, tailed),
                    lanes_of(read_growth * grad, jnp.zeros((CH, WIDTH), F32)),
                ),
                lanes_of(entry, leaving),
            )
            high, low = split(rows_of(gram_grad, score_grad))
            both = rows_of(k, q)
            p = dot(rows_of(high, low), k)
            direct = p[: SPAN + CH] + p[SPAN + CH :]
            turned = dot(high, both, ta=True) + dot(low, both, ta=True)
            key_grad = r * back[:SPAN] + direct[:SPAN] + turned
            dk = key_grad - key * (r * r * jnp.sum(key * key_grad, axis=1, keepdims=True))
            dq = back[SPAN:] + direct[SPAN:]
            fill = jnp.zeros((SPAN, 2 * WIDTH - SPAN), F32)
            pairs_fold = folded(lanes_of(pairs, fill))
            tail_pairs = tailed * key_leave
            factor_cumul = -jnp.sum(
                pairs_fold + growth * rest_grad * key_entry + tail_pairs, axis=1, keepdims=True
            )
            beta_grad = jnp.sum(
                right_grad * (v - growth * key_entry) - col(INVERSE_BETA) * pairs_fold, axis=1, keepdims=True
            )
            token_cumul = jnp.sum(
                folded(lanes_of(read_pairs, fill[:CH])) + read_growth * grad * query_entry, axis=1, keepdims=True
            )
            last_grad = jnp.sum(
                jnp.sum(tail_pairs, axis=0, keepdims=True)
                + col(LAST)[:1] * jnp.sum(entry * leaving, axis=0, keepdims=True),
                axis=1, keepdims=True,
            )
            token_cumul = token_cumul + jnp.where(token == CH - 1, last_grad, 0.0)
            row_cumul = jnp.sum(pairs, axis=0, keepdims=True) - jnp.sum(read_pairs, axis=0, keepdims=True)
            lane_at = WIDTH // 2 + g * FIELDS
            rows_here = slice(s * SPAN, (s + 1) * SPAN)
            cols_s[j, rows_here, lane_at : lane_at + 1] = beta_grad
            cols_s[j, rows_here, lane_at + 1 : lane_at + 2] = factor_cumul
            tcols_s[j, s * CH : (s + 1) * CH, lane_at : lane_at + 1] = token_cumul
            grow_s[s, pl.ds(j * GROUP + g, 1), :] = row_cumul
            qf_s[place(j, g, s, CH), :] = dq
            kf_s[place(j, g, s, SPAN), :] = dk
            vf_s[place(j, g, s, SPAN), :] = rest_grad

    gradients_out = [
        pltpu.make_async_copy(source, target, own_sems.at[1 + i])
        for i, (source, target) in enumerate(((dq_ref, dq_out), (dk_ref, dk_out), (dv_ref, dv_out)))
    ]

    def weight_out(j):
        return pltpu.make_async_copy(wg_in.at[j], wg_ref.at[:, j * GROUP * WIDTH : (j + 1) * GROUP * WIDTH], weight_sems.at[j])

    def finish_local():
        fill = jnp.zeros((factors, WIDTH - groups * per_group), F32)
        gt_s[...] = jnp.transpose(lanes_of(*(cols_s[j, :, WIDTH // 2 : WIDTH // 2 + per_group] for j in range(groups)), fill))
        tt_s[...] = jnp.transpose(lanes_of(*(tcols_s[j, :, WIDTH // 2 : WIDTH // 2 + per_group] for j in range(groups)), fill[:length]))

        def field(ref, f):
            return rows_of(*(ref[h * FIELDS + f : h * FIELDS + f + 1, :] for h in range(heads)))

        cumul_wide = field(gt_s, 1) + lanes_of(*(grow_s[s] for s in range(stretches)))
        narrow = where_one(iota((factors, length), 0) // NF == iota((factors, length), 1))
        cumul_grad = select(cumul_wide, narrow) + field(tt_s, 0)
        decay_grad = select(cumul_grad, where_one(same & (before >= after)))
        gate_out[...] = -rate_column * decay_grad / (1.0 + jnp.exp(-gate))
        share_of = jnp.sum(-soft * decay_grad, axis=1, keepdims=True)
        rate_ref[...] = jnp.zeros_like(rate_ref)
        rate_ref[:heads] = jnp.broadcast_to(share_of, (heads, WIDTH))
        target = iota((factors, factors), 1)
        unweave = where_one((target % length) * NF + target // length == iota((factors, factors), 0))
        beta_parts = select(field(gt_s, 0), unweave)
        for f in range(NF):
            sigmoid = 1.0 / (1.0 + jnp.exp(-beta_ref[f]))
            beta_out[f] = beta_parts[:, f * length : (f + 1) * length] * (2.0 * sigmoid * (1.0 - sigmoid))
        dq_ref[...] = qf_s[...].reshape(dq_ref.shape).astype(BF16)
        dk_ref[...] = kf_s[...].reshape(dk_ref.shape).astype(BF16)
        dv_ref[...] = vf_s[...].reshape(dv_ref.shape).astype(BF16)
        for copy in gradients_out:
            copy.start()

    def turn_slabs():
        def landed(source, far):
            to_sides(lambda h: side_landed(source, h, far).wait_recv())

        arrivals(landed)

        @pl.when(is_end)
        def _():
            slab_t[:, :length] = jnp.transpose(slab_s[me]).astype(BF16)

        @pl.when(jnp.logical_not(is_end))
        def _():
            for d in range(n):
                slab_t[:, d * length : (d + 1) * length] = jnp.transpose(slab_s[d]).astype(BF16)

        @pl.when(is_next)
        def _():
            for d in range(n - 1):
                far_t[:, d * length : (d + 1) * length] = jnp.transpose(far_s[first_far + d]).astype(BF16)

    def own_weight(j):
        wg_out[j] = dot(slab_t[...], rows_of(*(gath_s[d, j] for d in range(n))).astype(BF16))
        wg_copy(j).start()

    def far_weight(j):
        far_out[j] = dot(far_t[...], rows_of(*(gath_s[first_far + d, j] for d in range(n - 1))).astype(BF16))
        half_copy(j).start()

    def far_pass(j):
        half_copy(j).wait_recv()
        far_sum[j] = far_out[j, half_rows(dp_me)] + far_in[j]
        end_copy(j).start()

    def end_weight(j):
        wg_out[j] = dot(slab_t[:, :length], gath_s[me, j].astype(BF16))
        end_landed = remote(
            far_sum.at[j], end_in.at[j], end_send.at[j], end_recv.at[j], {"ctx": jnp.where(me == 0, 1, n - 2)}
        )
        end_landed.wait_recv()
        mine = half_rows(dp_me)
        wg_out[j, mine] = wg_out[j, mine] + end_in[j]
        wg_copy(j).start()

    def relay(i):
        j = i - me - (groups - 1)

        @pl.when((j >= 0) & (j < groups) & (me < n - 1))
        def _():
            def from_left(step, carry):
                source = me - step

                @pl.when(source >= 0)
                def _():
                    core_right(source, j).wait_recv()

                    @pl.when(me < n - 2)
                    def _():
                        core_right(source, j).start()

                return carry

            lax.fori_loop(1, n, from_left, 0)

        def from_right(step, carry):
            source = me + step
            late = i - me - 2 * step

            @pl.when((source < n) & (late >= 0) & (late < groups) & (me > 0))
            def _():
                core_left(source, late).wait_recv()

                @pl.when(me > 1)
                def _():
                    core_left(source, late).start()

            return carry

        lax.fori_loop(1, n, from_right, 0)

    def when_group(j, condition, what):
        @pl.when((j >= 0) & (j < groups) & condition)
        def _():
            what(j)

    def rate_copy(source, target):
        return remote(rate_ref, rate_in.at[source], rate_send.at[target], rate_recv.at[source], {"ctx": target})

    def step(i, carry):
        @pl.when(i < groups)
        def _():
            local_maps(i)

        @pl.when((i >= me) & (i < groups + me))
        def _():
            forward(i - me)

        back = i - (n - 1 - me)

        @pl.when((back >= 0) & (back < groups))
        def _():
            backward_wave(back)

        @pl.when(i == groups - 1 + me)
        def _():
            project()

        @pl.when(i == min(groups - 1, 2))
        def _():
            pass_aside()

        @pl.when(i == groups)
        def _():
            turn_slabs()

        relay(i)
        far = i - jnp.where(me == 1, 2 * n - 3, n - 2 + groups - 1)
        when_group(far - 1, is_next, far_pass)
        when_group(far, is_next, far_weight)
        when_group(i - jnp.maximum(2 * (n - 1) - me, me + groups - 1), jnp.logical_not(is_end), own_weight)
        ready = i - (n - 1 + 0)

        @pl.when((ready >= 0) & (ready < groups))
        def _():
            backward(ready)

        @pl.when(ready == groups - 1)
        def _():
            finish_local()
            for d in range(n):

                @pl.when(me != d)
                def _():
                    rate_copy(me, d).start()

        return carry

    load_w.wait()
    lax.fori_loop(0, groups + 2 * (n - 1), step, 0)

    for d in range(n):

        @pl.when(me != d)
        def _():
            rate_copy(d, me).wait_recv()

        @pl.when(me == d)
        def _():
            rate_in[d] = rate_ref[...]

    rate_two[0] = sum(rate_in[d] for d in range(n))
    two = remote(rate_two.at[0], rate_two.at[1], two_send.at[0], two_recv.at[0], partner)
    two.start()
    for j in range(groups):
        when_group(j, is_end, end_weight)

    for d in range(heads_n):

        @pl.when(head_me != d)
        def _():
            remote(
                mix_out.at[d], mix_in.at[d], mix_send.at[d], mix_recv.at[d], {"head": d}
            ).wait_recv()

    mixed_ref[...] = sum(mix_in[d] for d in range(heads_n)).astype(BF16)
    for d in range(n):

        @pl.when(me != d)
        def _():
            rate_copy(me, d).wait_send()

    for j in range(groups):
        wg_copy(j).wait_recv()
        wg_in[j] = wg_out[j] + wg_in[j]
        weight_out(j).start()
    two.wait()
    rate_ref[...] = rate_two[0] + rate_two[1]
    for j in range(groups):
        wg_copy(j).wait_send()
    for d in range(heads_n):

        @pl.when(head_me != d)
        def _():
            mix_copy(d).wait_send()

    for d in range(n):

        @pl.when(travels(me, d))
        def _():
            cot_copy(d).wait_send()

    arrivals(lambda source, far: to_sides(lambda h: side_copy(source, h, far).wait_send()))

    def drain(j, carry):
        @pl.when(is_next)
        def _():
            half_copy(j).wait_send()
            end_copy(j).wait_send()

        @pl.when(me < n - 1)
        def _():
            enter_copy(j).wait_send()

        @pl.when(me > 0)
        def _():
            leave_copy(j).wait_send()

        def one(source, inner):
            @pl.when((source <= me) & (me < n - 2))
            def _():
                core_right(source, j).wait_send()

            @pl.when((source >= me) & (me > 1))
            def _():
                core_left(source, j).wait_send()

            return inner

        return lax.fori_loop(0, n, one, carry)

    lax.fori_loop(0, groups, drain, 0)
    for copy in gradients_out:
        copy.wait()
    for j in range(groups):
        weight_out(j).wait()


def hand_over_kernel(rate_ref, *refs):
    count = (len(refs) - 2) // 2
    sources, targets, rate_out, sems = refs[:count], refs[count : 2 * count], refs[-2], refs[-1]
    copies = [
        pltpu.make_async_copy(source, target, sems.at[i]) for i, (source, target) in enumerate(zip(sources, targets))
    ]
    for copy in copies:
        copy.start()
    for h in range(rate_out.shape[0]):
        rate_out[h] = rate_ref[h, 0]
    for copy in copies:
        copy.wait()


def on_device(
    query_input, key_input, value_input, beta_logit, gate_logit, decay_rate,
    doc_ids, out_weight, out_cotangent,
):
    _, length, heads, width = query_input.shape
    model_width = out_cotangent.shape[-1]
    blocks = length // CH
    groups = heads // GROUP
    factors = length * NF
    n, heads_n, dp_n = (lax.axis_size(axis) for axis in ("ctx", "head", "dp"))
    units = GROUP * blocks
    slab = model_width // n
    share = model_width // heads_n
    lanes = GROUP * width

    def vmem(*shape, dtype=F32):
        return pltpu.VMEM(shape, dtype)

    def dma(*shape):
        return pltpu.SemaphoreType.DMA(shape)

    state = (groups, units, width, width)
    moving = (groups, GROUP, width, width)
    scratch = [
        vmem(*out_weight.shape, dtype=BF16), vmem(length, heads, width, dtype=BF16),
        vmem(factors, heads, width, dtype=BF16), vmem(factors, heads, width, dtype=BF16), dma(4), dma(groups),
        vmem(length * heads, width), vmem(factors * heads, width), vmem(factors * heads, width),
        vmem(WIDTH, factors), vmem(WIDTH, length),
        vmem(groups, factors, WIDTH), vmem(groups, length, WIDTH),
        vmem(blocks, heads, SPAN), vmem(WIDTH, factors), vmem(WIDTH, length),
        vmem(groups, length, lanes),
        vmem(groups, units, SPAN, SPAN, dtype=BF16),
        vmem(groups, units, SPAN, SPAN, dtype=BF16),
        vmem(groups, units, SPAN, width),
        vmem(groups, units, SPAN, width),
        vmem(groups, units, SPAN, SPAN),
        vmem(groups, units, CH, SPAN),
        vmem(groups, units, CH, SPAN),
        vmem(groups, units, SPAN, 1),
        vmem(*state), vmem(*state), vmem(*state),
        vmem(groups, units, CH, width),
        vmem(*moving), vmem(*moving), vmem(*moving), vmem(*moving),
        vmem(n, length, slab),
        vmem(n, length, slab),
        vmem(slab, n * length, dtype=BF16),
        vmem(n, length, slab),
        vmem(slab, (n - 1) * length, dtype=BF16),
        vmem(n, groups, length, lanes),
        vmem(groups, length, lanes, dtype=BF16),
        vmem(heads_n, length, share),
        vmem(heads_n, length, share),
        vmem(groups, slab, lanes),
        vmem(groups, slab, lanes),
        vmem(groups, slab, lanes),
        vmem(groups, slab // dp_n, lanes),
        vmem(groups, slab // dp_n, lanes),
        vmem(groups, slab // dp_n, lanes),
        vmem(n, 8, WIDTH),
        vmem(2, 8, WIDTH),
        dma(groups), dma(groups), dma(groups), dma(groups),
        dma(n), dma(n), dma(n), dma(n, heads_n), dma(n, heads_n), dma(n, heads_n), dma(n, heads_n),
        dma(n, groups), dma(n, groups), dma(n, groups),
        dma(heads_n), dma(heads_n), dma(groups), dma(groups), dma(groups), dma(groups), dma(groups), dma(groups),
        dma(n), dma(n), dma(1), dma(1),
    ]
    whole = pl.BlockSpec(memory_space=pltpu.VMEM)
    scalars = pl.BlockSpec(memory_space=pltpu.SMEM)
    anywhere = pl.BlockSpec(memory_space=pl.ANY)
    dq, dk, dv, beta_grad, gate_grad, mixed, weight_grad, rate = pl.pallas_call(
        functools.partial(layer_kernel, (n, heads_n, dp_n, groups, blocks)),
        in_specs=[scalars] * 2 + [whole] * 6 + [anywhere],
        out_specs=[anywhere] * 3 + [whole] * 3 + [anywhere, whole],
        out_shape=[
            jax.ShapeDtypeStruct((length, heads, width), BF16),
            jax.ShapeDtypeStruct((factors, heads, width), BF16),
            jax.ShapeDtypeStruct((factors, heads, width), BF16),
            jax.ShapeDtypeStruct((NF, heads, length), F32),
            jax.ShapeDtypeStruct((heads, length), F32),
            jax.ShapeDtypeStruct((length, share), BF16),
            jax.ShapeDtypeStruct((slab, heads * width), F32),
            jax.ShapeDtypeStruct((8, WIDTH), F32),
        ],
        scratch_shapes=scratch,
        compiler_params=pltpu.CompilerParams(
            collective_id=0, has_side_effects=True, vmem_limit_bytes=61 << 20
        ),
        name="layer",
    )(
        doc_ids, decay_rate, query_input[0], key_input.reshape(factors, heads, width),
        value_input.reshape(factors, heads, width), beta_logit[0].transpose(1, 0, 2), gate_logit[0], out_cotangent[0], out_weight,
    )
    moved = (mixed, dq, dk, dv, beta_grad, gate_grad, weight_grad)
    mixed, dq, dk, dv, beta_grad, gate_grad, weight_grad, rate_grad = pl.pallas_call(
        hand_over_kernel,
        in_specs=[scalars] + [whole] * len(moved),
        out_specs=[anywhere] * len(moved) + [scalars],
        out_shape=[jax.ShapeDtypeStruct(x.shape, x.dtype) for x in moved]
        + [jax.ShapeDtypeStruct((heads,), F32)],
        scratch_shapes=[pltpu.SemaphoreType.DMA((len(moved),))],
        name="hand_over",
    )(rate, *moved)
    return (
        mixed[None],
        dq[None],
        dk.reshape(key_input.shape),
        dv.reshape(value_input.shape),
        beta_grad.transpose(1, 0, 2)[None],
        gate_grad[None],
        weight_grad,
        rate_grad,
    )


def solution(mesh):
    in_specs = (
        P(("groups", "dp"), "ctx", "head", None),
        P(("groups", "dp"), "ctx", None, "head", None),
        P(("groups", "dp"), "ctx", None, "head", None),
        P(("groups", "dp"), "head", None, "ctx"),
        P(("groups", "dp"), "head", "ctx"),
        P("head"),
        P(("groups", "dp"), None),
        P("head", None),
        P(("groups", "dp"), "ctx", None),
    )
    out_specs = (
        P(("groups", "dp"), "ctx", "head"),
        P(("groups", "dp"), "ctx", "head", None),
        P(("groups", "dp"), "ctx", None, "head", None),
        P(("groups", "dp"), "ctx", None, "head", None),
        P(("groups", "dp"), "head", None, "ctx"),
        P(("groups", "dp"), "head", "ctx"),
        P(("groups", "ctx"), "head"),
        P(("groups", "head")),
    )
    return jax.shard_map(
        on_device, mesh=mesh, in_specs=in_specs, out_specs=out_specs, check_vma=False
    )
```

```python
import functools

import jax
import jax.numpy as jnp
from jax import lax
from jax.experimental import pallas as pl
from jax.experimental.pallas import tpu as pltpu
from jax.sharding import PartitionSpec as P

CH = 64
NF = 3
SPAN = CH * NF
WIDTH = 128
GROUP = 2
FIELDS = 8
F32 = jnp.float32
BF16 = jnp.bfloat16
MESH = pl.DeviceIdType.MESH
BETA, CUMUL, BETA_GROWTH, GROWTH, TAIL, INVERSE_BETA, LAST = range(7)
READ_CUMUL, READ_GROWTH = range(2)


def iota(shape, dim):
    return lax.broadcasted_iota(jnp.int32, shape, dim)


def rows_of(*parts):
    return jnp.concatenate(parts, axis=0)


def lanes_of(*parts):
    return jnp.concatenate(parts, axis=1)


def split(x):
    high = x.astype(BF16)
    return high, (x - high.astype(F32)).astype(BF16)


def dot(a, b, ta=False, tb=False):
    dims = (((0 if ta else 1,), (1 if tb else 0,)), ((), ()))
    return lax.dot_general(a, b, dims, preferred_element_type=F32)


def folded(p):
    return p[:, :WIDTH] + p[:, WIDTH:]


def select(x, chosen):
    high = x.astype(BF16)
    rest = x - high.astype(F32)
    middle = rest.astype(BF16)
    low = (rest - middle.astype(F32)).astype(BF16)
    size = x.shape[0]
    p = dot(rows_of(high.astype(F32), middle.astype(F32), low.astype(F32)).astype(BF16), chosen)
    return (p[2 * size :] + p[size : 2 * size]) + p[:size]


def where_one(condition):
    return jnp.where(condition, 1.0, 0.0).astype(BF16)


def mm_exact(a, b):
    return folded(dot(a, lanes_of(*split(b))))


def mm_full(a, b):
    size = a.shape[0]
    b_high, b_low = split(b)
    p = dot(rows_of(*split(a)), lanes_of(b_high, b_low))
    return folded(p[:size]) + p[size:, :WIDTH]


def mm_wide(a, b):
    size = a.shape[0]
    a_high, a_low = split(a)
    b_high, b_low = split(b)
    p = dot(rows_of(a_high, a_low), b_high)
    return p[:size] + p[size:] + dot(a_high, b_low)


def mm_tb(a, b):
    size = a.shape[0]
    a_high, a_low = split(a)
    b_high, b_low = split(b)
    p = dot(rows_of(a_high, a_low), b_high, tb=True)
    return p[:size] + p[size:] + dot(a_high, b_low, tb=True)


def mm_ta(a, b):
    a_high, a_low = split(a)
    b_high, b_low = split(b)
    return folded(dot(a_high, lanes_of(b_high, b_low), ta=True)) + dot(a_low, b_high, ta=True)


def lower_halves(x, size):
    return rows_of(*(x[i : i + size] for i in range(size, x.shape[0], 2 * size)))


def spread_halves(low, size, total):
    zero = jnp.zeros((size, low.shape[1]), low.dtype)
    pieces, taken = [], 0
    for i in range(0, total, size):
        if (i // size) % 2:
            pieces.append(low[taken : taken + size])
            taken += size
        else:
            pieces.append(zero)
    return rows_of(*pieces)


def merge_halves(x, low, size):
    pieces, taken = [], 0
    for i in range(0, x.shape[0], size):
        if (i // size) % 2:
            pieces.append(low[taken : taken + size])
            taken += size
        else:
            pieces.append(x[i : i + size])
    return rows_of(*pieces)


def unit_inverses(lowers):
    lane, sub = iota((8, SPAN), 1), iota((8, SPAN), 0)
    lane_here = iota((8, WIDTH), 1)
    starts = []
    for lower in lowers:
        packed = jnp.zeros((8, SPAN), F32)
        for b in range(SPAN // 8):
            packed = packed + jnp.where(lane // 8 == b, lower[8 * b : 8 * b + 8], 0.0)
        wide = lanes_of(packed, jnp.zeros((8, 2 * WIDTH - SPAN), F32))
        block = jnp.where(sub == lane % 8, 1.0, 0.0)
        for c in range(7):
            index = (lane_here // 8) * 8 + c
            factor = lanes_of(
                *(jnp.take_along_axis(wide[:, at : at + WIDTH], index, axis=1) for at in (0, WIDTH))
            )[:, :SPAN]
            block = block - factor * block[c : c + 1, :]
        starts.append(rows_of(*(jnp.where(lane // 8 == b, block, 0.0) for b in range(SPAN // 8))))
    inverses = starts
    row, column = iota((SPAN, SPAN), 0), iota((SPAN, SPAN), 1)
    for level in range(3, (SPAN - 1).bit_length()):
        size = 1 << level
        here = (lower_halves(row, size) >> level) == (lower_halves(column, size) >> level) + 1
        halves = [
            mm_wide(jnp.where(here, lower_halves(low, size), 0.0), inv)
            for low, inv in zip(lowers, inverses)
        ]
        tails = [
            lower_halves(inv, size) - mm_wide(lower_halves(inv, size), spread_halves(half, size, SPAN))
            for inv, half in zip(inverses, halves)
        ]
        inverses = [merge_halves(inv, tail, size) for inv, tail in zip(inverses, tails)]
    return inverses


def layer_kernel(
    sizes,
    doc_ref, decay_ref, q_ref, k_ref, v_ref, beta_ref, gate_ref, cot_ref, w_in,
    dq_out, dk_out, dv_out, beta_out, gate_out, mixed_ref, wg_ref, rate_ref,
    w_ref, dq_ref, dk_ref, dv_ref, own_sems, weight_sems,
    qf_s, kf_s, vf_s, frow_s, trow_s, cols_s, tcols_s, grow_s, gt_s, tt_s,
    grad_s, th_s, tl_s, u_s, w_s, lg_s, reads_s, rd_s, r_s,
    map_s, offset_s, pull_s, qe_s,
    ein_s, eout_s, gin_s, gout_s, cotf_s, slab_s, slab_t, gath_s, core_s,
    mix_out, mix_in, wg_out, wg_in, rate_in, rate_two,
    e_send, e_recv, g_send, g_recv, cot_send, cot_recv, side_send, side_recv,
    right_send, left_send, core_recv,
    mix_send, mix_recv, wg_send, wg_recv,
    rate_send, rate_recv, two_send, two_recv,
):
    n, heads_n, dp_n, groups, stretches = sizes
    me = lax.axis_index("ctx")
    head_me = lax.axis_index("head")
    dp_me = lax.axis_index("dp")
    slab = slab_s.shape[-1]
    share = mix_in.shape[-1]
    scale = WIDTH ** (-0.5)
    every = [(g, s) for g in range(GROUP) for s in range(stretches)]
    partner = {"dp": lax.rem(dp_me + 1, dp_n)}

    load_w = pltpu.make_async_copy(w_in, w_ref, own_sems.at[0])
    load_w.start()
    barrier = pltpu.get_barrier_semaphore()
    for step in range(1, n):
        pl.semaphore_signal(barrier, inc=1, device_id={"ctx": lax.rem(me + step, n)}, device_id_type=MESH)
    for step in range(1, heads_n):
        pl.semaphore_signal(
            barrier, inc=1, device_id={"head": lax.rem(head_me + step, heads_n)}, device_id_type=MESH
        )
    pl.semaphore_signal(barrier, inc=1, device_id=partner, device_id_type=MESH)

    for d in range(n):
        piece = cot_ref[:, d * slab : (d + 1) * slab].astype(F32)

        @pl.when(me == d)
        def _():
            slab_s[d] = piece

        @pl.when(me != d)
        def _():
            cotf_s[d] = piece

    @pl.when(me == 0)
    def _():
        ein_s[...] = jnp.zeros_like(ein_s)

    @pl.when(me == n - 1)
    def _():
        gin_s[...] = jnp.zeros_like(gin_s)

    heads = groups * GROUP
    length = stretches * CH
    factors = length * NF
    qf_s[...] = q_ref[...].astype(F32).reshape(qf_s.shape)
    kf_s[...] = k_ref[...].astype(F32).reshape(kf_s.shape)
    vf_s[...] = v_ref[...].astype(F32).reshape(vf_s.shape)

    before, after = iota((length, length), 0), iota((length, length), 1)
    same = before // CH == after // CH
    up_to = where_one(same & (before <= after))
    closing = where_one(before == (after // CH) * CH + (CH - 1))
    widen = where_one(iota((length, factors), 0) == iota((length, factors), 1) // NF)
    source = iota((factors, factors), 0)
    weave = where_one((source % length) * NF + source // length == iota((factors, factors), 1))
    head_row = iota((heads, 1), 0)
    rate_column = jnp.zeros((heads, 1), F32)
    for h in range(heads):
        rate_column = rate_column + jnp.where(head_row == h, decay_ref[h], 0.0)
    gate = gate_ref[...]
    soft = jnp.maximum(gate, 0.0) + jnp.log1p(jnp.exp(-jnp.abs(gate)))
    sums = select(-rate_column * soft, up_to)
    last = select(sums, closing)
    growth_rows = jnp.exp(sums)
    wide = select(rows_of(sums, growth_rows, jnp.exp(last - sums), jnp.exp(last)), widen)
    beta_rows = select(lanes_of(*(2.0 / (1.0 + jnp.exp(-beta_ref[f])) for f in range(NF))), weave)
    sums_wide, growth_wide, tail_wide, last_wide = (wide[i * heads : (i + 1) * heads] for i in range(4))
    frow_s[...] = jnp.zeros_like(frow_s)
    trow_s[...] = jnp.zeros_like(trow_s)
    for field, value in (
        (BETA, beta_rows), (CUMUL, sums_wide), (BETA_GROWTH, beta_rows * growth_wide), (GROWTH, growth_wide),
        (TAIL, tail_wide), (INVERSE_BETA, 1.0 / beta_rows), (LAST, last_wide),
    ):
        for h in range(heads):
            frow_s[h * FIELDS + field : h * FIELDS + field + 1, :] = value[h : h + 1]
    for field, value in ((READ_CUMUL, sums), (READ_GROWTH, growth_rows * scale)):
        for h in range(heads):
            trow_s[h * FIELDS + field : h * FIELDS + field + 1, :] = value[h : h + 1]
    turned_fields, turned_tokens = jnp.transpose(frow_s[...]), jnp.transpose(trow_s[...])
    per_group = GROUP * FIELDS
    for j in range(groups):
        cols_s[j, :, :per_group] = turned_fields[:, j * per_group : (j + 1) * per_group]
        tcols_s[j, :, :per_group] = turned_tokens[:, j * per_group : (j + 1) * per_group]
    retains = []
    for s in range(stretches):
        place = me * stretches + s
        kept = doc_ref[0, place] == doc_ref[0, jnp.maximum(place - 1, 0)]
        retains.append(jnp.where(kept & (place > 0), 1.0, 0.0))
    pl.semaphore_wait(barrier, n - 1 + heads_n - 1 + 1)

    def remote(src, dst, send, recv, where):
        return pltpu.make_async_remote_copy(
            src_ref=src, dst_ref=dst, send_sem=send, recv_sem=recv, device_id=where, device_id_type=MESH
        )

    part = cot_ref.shape[0] // heads_n

    def part_rows(h):
        return pl.ds(pl.multiple_of(h * part, part), part)

    def cot_copy(d):
        mine = part_rows(head_me)
        return remote(cotf_s.at[d, mine], slab_s.at[me, mine], cot_send.at[d], cot_recv.at[me], {"ctx": d})

    def cot_landed(source):
        at = slab_s.at[source, part_rows(head_me)]
        return remote(at, at, cot_send.at[0], cot_recv.at[source], {"ctx": source})

    def side_copy(source, h):
        at = slab_s.at[source, part_rows(head_me)]
        return remote(at, at, side_send.at[source, h], side_recv.at[source, head_me], {"head": h})

    def side_landed(source, h):
        at = slab_s.at[source, part_rows(h)]
        return remote(at, at, side_send.at[source, h], side_recv.at[source, h], {"head": h})

    def arrivals(what):
        for d in range(n):

            @pl.when(me != d)
            def _():
                what(d)

    def to_sides(what):
        for h in range(heads_n):

            @pl.when(head_me != h)
            def _():
                what(h)

    def pass_aside():
        def one(source):
            cot_landed(source).wait_recv()
            to_sides(lambda h: side_copy(source, h).start())

        arrivals(one)

    for d in range(n):

        @pl.when(me != d)
        def _():
            cot_copy(d).start()

    def enter_copy(j):
        return remote(eout_s.at[j], ein_s.at[j], e_send.at[j], e_recv.at[j], {"ctx": lax.rem(me + 1, n)})

    def leave_copy(j):
        return remote(gout_s.at[j], gin_s.at[j], g_send.at[j], g_recv.at[j], {"ctx": lax.rem(me + n - 1, n)})

    def core_right(source, j):
        at = gath_s.at[source, j]
        return remote(at, at, right_send.at[source, j], core_recv.at[source, j], {"ctx": lax.rem(me + 1, n)})

    def core_left(source, j):
        at = gath_s.at[source, j]
        return remote(at, at, left_send.at[source, j], core_recv.at[source, j], {"ctx": lax.rem(me + n - 1, n)})

    def mix_copy(d):
        return remote(mix_out.at[d], mix_in.at[head_me], mix_send.at[d], mix_recv.at[head_me], {"head": d})

    def wg_copy(j):
        return remote(wg_out.at[j], wg_in.at[j], wg_send.at[j], wg_recv.at[j], partner)

    def lanes(j):
        return pl.ds(pl.multiple_of(j * (GROUP * WIDTH), WIDTH), GROUP * WIDTH)

    def columns(j, g, s):
        block = cols_s[j, s * SPAN : (s + 1) * SPAN]
        return lambda f: block[:, g * FIELDS + f : g * FIELDS + f + 1]

    def token_columns(j, g, s):
        block = tcols_s[j, s * CH : (s + 1) * CH]
        return lambda f: block[:, g * FIELDS + f : g * FIELDS + f + 1]

    def field_rows(j, g, s):
        block = frow_s[pl.ds(pl.multiple_of((j * GROUP + g) * FIELDS, FIELDS), FIELDS), :]
        return block[:, s * SPAN : (s + 1) * SPAN]

    def place(j, g, s, size):
        return pl.ds(s * size * heads + j * GROUP + g, size, stride=heads)

    def unit(j, g, s):
        return j, g * stretches + s

    def local_maps(j):
        eye = iota((SPAN, SPAN), 0) == iota((SPAN, SPAN), 1)
        strict = iota((SPAN, SPAN), 0) > iota((SPAN, SPAN), 1)
        diagonal = iota((WIDTH, WIDTH), 0) == iota((WIDTH, WIDTH), 1)
        visible = iota((CH, SPAN), 0) * NF + (NF - 1) >= iota((CH, SPAN), 1)
        w_rows = w_ref[pl.ds(pl.multiple_of(j * (GROUP * WIDTH), WIDTH), GROUP * WIDTH), :]
        grad = dot(cot_ref[...], w_rows, tb=True)
        grad_s[j] = grad
        lowers, kept = [], []
        for g, s in every:
            at = slice(g * WIDTH, (g + 1) * WIDTH)
            k = kf_s[place(j, g, s, SPAN), :].astype(BF16)
            q = qf_s[place(j, g, s, CH), :].astype(BF16)
            col, tok = columns(j, g, s), token_columns(j, g, s)
            row = field_rows(j, g, s)
            cumul_row = row[CUMUL : CUMUL + 1]
            both = dot(rows_of(k, q), k, tb=True)
            gram, scores = both[:SPAN], both[SPAN:]
            squares = jnp.where(eye, gram, 0.0)
            r = lax.rsqrt(jnp.sum(squares, axis=1, keepdims=True) + 1e-06)
            r_row = lax.rsqrt(jnp.sum(squares, axis=0, keepdims=True) + 1e-06)
            pair = jnp.exp(jnp.where(strict, col(CUMUL) - cumul_row, -1e30)) * r_row
            lower_gain = (col(BETA) * r) * pair
            lower = lower_gain * gram
            read_gain = jnp.exp(
                jnp.where(visible, tok(READ_CUMUL) - cumul_row, -1e30)
            ) * (r_row * scale)
            reads = read_gain * scores
            here = unit(j, g, s)
            r_s[here] = r
            lg_s[here] = lower_gain
            rd_s[here] = read_gain
            reads_s[here] = reads
            lowers.append(lower)
            kept.append((k, q, col, tok, row, r, r_row, reads))
        for (g, s), (k, q, col, tok, row, r, r_row, reads), inverse in zip(every, kept, unit_inverses(lowers)):
            here = unit(j, g, s)
            at = slice(g * WIDTH, (g + 1) * WIDTH)
            th_s[here], tl_s[here] = split(inverse)
            v = vf_s[place(j, g, s, SPAN), :].astype(BF16)
            p = dot(rows_of(*split(inverse * row[BETA : BETA + 1])), v)
            solved_v = p[:SPAN] + p[SPAN:]
            p = dot(rows_of(*split(inverse * (row[BETA_GROWTH : BETA_GROWTH + 1] * r_row))), k)
            solved_k = p[:SPAN] + p[SPAN:]
            u_s[here] = solved_v
            w_s[here] = solved_k
            high, low = split(lanes_of(solved_v, solved_k) * (col(TAIL) * r))
            moved = dot(k, high, ta=True) + dot(k, low, ta=True)
            offset_s[here] = moved[:, :WIDTH]
            map_s[here] = jnp.where(diagonal, col(LAST)[:1], 0.0) - moved[:, WIDTH:]
            route = tok(READ_GROWTH) * q.astype(F32) - mm_full(reads, solved_k)
            pull_s[here] = mm_ta(route, grad[s * CH : (s + 1) * CH, at])

    def forward(j):
        @pl.when(me > 0)
        def _():
            enter_copy(j).wait_recv()

        entries = {}
        for g in range(GROUP):
            state = ein_s[j, g]
            for s in range(stretches):
                entry = retains[s] * state
                entries[g, s] = entry
                state = mm_full(map_s[unit(j, g, s)], entry) + offset_s[unit(j, g, s)]
                offset_s[unit(j, g, s)] = entry
            eout_s[j, g] = state

        @pl.when(me < n - 1)
        def _():
            enter_copy(j).start()

        for g, s in every:
            here = unit(j, g, s)
            at = slice(g * WIDTH, (g + 1) * WIDTH)
            k = kf_s[place(j, g, s, SPAN), :].astype(BF16)
            q = qf_s[place(j, g, s, CH), :].astype(BF16)
            tok = token_columns(j, g, s)
            on_entry = mm_exact(rows_of(k, q), entries[g, s])
            key_entry, query_entry = r_s[here] * on_entry[:SPAN], on_entry[SPAN:]
            correction = u_s[here] - mm_full(w_s[here], entries[g, s])
            core = tok(READ_GROWTH) * query_entry + mm_full(reads_s[here], correction)
            rounded = core.astype(BF16)
            w_s[here] = key_entry
            qe_s[here] = query_entry
            u_s[here] = correction
            core_s[j, s * CH : (s + 1) * CH, at] = rounded
            gath_s[me, j, s * CH : (s + 1) * CH, at] = rounded.astype(F32)

        @pl.when(me < n - 1)
        def _():
            core_right(me, j).start()

        @pl.when(me > 0)
        def _():
            core_left(me, j).start()

    def backward_wave(j):
        @pl.when(me < n - 1)
        def _():
            leave_copy(j).wait_recv()

        for g in range(GROUP):
            state = gin_s[j, g]
            for s in reversed(range(stretches)):
                here = unit(j, g, s)
                maps_high, maps_low = split(map_s[here])
                high, low = split(state)
                carried = folded(dot(maps_high, lanes_of(high, low), ta=True)) + dot(maps_low, high, ta=True)
                before = retains[s] * (carried + pull_s[here])
                pull_s[here] = state
                state = before
            gout_s[j, g] = state

        @pl.when(me > 0)
        def _():
            leave_copy(j).start()

    def project():
        core = lanes_of(*(core_s[j] for j in range(groups)))

        def columns_of(d):
            return dot(core, w_ref[:, d * share : (d + 1) * share])

        for d in range(heads_n):

            @pl.when(head_me != d)
            def _():
                mix_out[d] = columns_of(d)
                mix_copy(d).start()

        for d in range(heads_n):

            @pl.when(head_me == d)
            def _():
                mix_in[d] = columns_of(d)

    def backward(j):
        token = iota((CH, 1), 0)
        for g, s in every:
            here = unit(j, g, s)
            at = slice(g * WIDTH, (g + 1) * WIDTH)
            key = kf_s[place(j, g, s, SPAN), :]
            v = vf_s[place(j, g, s, SPAN), :]
            k, q = key.astype(BF16), qf_s[place(j, g, s, CH), :].astype(BF16)
            col = columns(j, g, s)
            beta, growth, tail, read_growth = col(BETA), col(GROWTH), col(TAIL), token_columns(j, g, s)(READ_GROWTH)
            grad = grad_s[j, s * CH : (s + 1) * CH, at]
            entry, leaving, r = offset_s[here], pull_s[here], r_s[here]
            correction, key_entry, query_entry = u_s[here], w_s[here], qe_s[here]
            reads = reads_s[here]
            key_leave = r * mm_exact(k, leaving)
            correction_grad = mm_ta(reads, grad) + tail * key_leave
            high, low = split(correction_grad)
            right_grad = folded(dot(th_s[here], lanes_of(high, low), ta=True)) + dot(tl_s[here], high, ta=True)
            rest_grad = beta * right_grad
            outer = mm_tb(rows_of(right_grad, grad), correction)
            outer_key, outer_read = outer[:SPAN], outer[SPAN:]
            gram_grad = -outer_key * lg_s[here]
            score_grad = outer_read * rd_s[here]
            pairs = -gram_grad * dot(k, k, tb=True)
            read_pairs = outer_read * reads
            tailed = tail * correction
            back = mm_tb(
                rows_of(
                    lanes_of(-growth * rest_grad, tailed),
                    lanes_of(read_growth * grad, jnp.zeros((CH, WIDTH), F32)),
                ),
                lanes_of(entry, leaving),
            )
            high, low = split(rows_of(gram_grad, score_grad))
            both = rows_of(k, q)
            p = dot(rows_of(high, low), k)
            direct = p[: SPAN + CH] + p[SPAN + CH :]
            turned = dot(high, both, ta=True) + dot(low, both, ta=True)
            key_grad = r * back[:SPAN] + direct[:SPAN] + turned
            dk = key_grad - key * (r * r * jnp.sum(key * key_grad, axis=1, keepdims=True))
            dq = back[SPAN:] + direct[SPAN:]
            fill = jnp.zeros((SPAN, 2 * WIDTH - SPAN), F32)
            pairs_fold = folded(lanes_of(pairs, fill))
            tail_pairs = tailed * key_leave
            factor_cumul = -jnp.sum(
                pairs_fold + growth * rest_grad * key_entry + tail_pairs, axis=1, keepdims=True
            )
            beta_grad = jnp.sum(
                right_grad * (v - growth * key_entry) - col(INVERSE_BETA) * pairs_fold, axis=1, keepdims=True
            )
            token_cumul = jnp.sum(
                folded(lanes_of(read_pairs, fill[:CH])) + read_growth * grad * query_entry, axis=1, keepdims=True
            )
            last_grad = jnp.sum(
                jnp.sum(tail_pairs, axis=0, keepdims=True)
                + col(LAST)[:1] * jnp.sum(entry * leaving, axis=0, keepdims=True),
                axis=1, keepdims=True,
            )
            token_cumul = token_cumul + jnp.where(token == CH - 1, last_grad, 0.0)
            row_cumul = jnp.sum(pairs, axis=0, keepdims=True) - jnp.sum(read_pairs, axis=0, keepdims=True)
            lane_at = WIDTH // 2 + g * FIELDS
            rows_here = slice(s * SPAN, (s + 1) * SPAN)
            cols_s[j, rows_here, lane_at : lane_at + 1] = beta_grad
            cols_s[j, rows_here, lane_at + 1 : lane_at + 2] = factor_cumul
            tcols_s[j, s * CH : (s + 1) * CH, lane_at : lane_at + 1] = token_cumul
            grow_s[s, pl.ds(j * GROUP + g, 1), :] = row_cumul
            qf_s[place(j, g, s, CH), :] = dq
            kf_s[place(j, g, s, SPAN), :] = dk
            vf_s[place(j, g, s, SPAN), :] = rest_grad

    gradients_out = [
        pltpu.make_async_copy(source, target, own_sems.at[1 + i])
        for i, (source, target) in enumerate(((dq_ref, dq_out), (dk_ref, dk_out), (dv_ref, dv_out)))
    ]

    def weight_out(j):
        return pltpu.make_async_copy(wg_in.at[j], wg_ref.at[:, j * GROUP * WIDTH : (j + 1) * GROUP * WIDTH], weight_sems.at[j])

    def finish_local():
        fill = jnp.zeros((factors, WIDTH - groups * per_group), F32)
        gt_s[...] = jnp.transpose(lanes_of(*(cols_s[j, :, WIDTH // 2 : WIDTH // 2 + per_group] for j in range(groups)), fill))
        tt_s[...] = jnp.transpose(lanes_of(*(tcols_s[j, :, WIDTH // 2 : WIDTH // 2 + per_group] for j in range(groups)), fill[:length]))

        def field(ref, f):
            return rows_of(*(ref[h * FIELDS + f : h * FIELDS + f + 1, :] for h in range(heads)))

        cumul_wide = field(gt_s, 1) + lanes_of(*(grow_s[s] for s in range(stretches)))
        narrow = where_one(iota((factors, length), 0) // NF == iota((factors, length), 1))
        cumul_grad = select(cumul_wide, narrow) + field(tt_s, 0)
        decay_grad = select(cumul_grad, where_one(same & (before >= after)))
        gate_out[...] = -rate_column * decay_grad / (1.0 + jnp.exp(-gate))
        share_of = jnp.sum(-soft * decay_grad, axis=1, keepdims=True)
        rate_ref[...] = jnp.zeros_like(rate_ref)
        rate_ref[:heads] = jnp.broadcast_to(share_of, (heads, WIDTH))
        target = iota((factors, factors), 1)
        unweave = where_one((target % length) * NF + target // length == iota((factors, factors), 0))
        beta_parts = select(field(gt_s, 0), unweave)
        for f in range(NF):
            sigmoid = 1.0 / (1.0 + jnp.exp(-beta_ref[f]))
            beta_out[f] = beta_parts[:, f * length : (f + 1) * length] * (2.0 * sigmoid * (1.0 - sigmoid))
        dq_ref[...] = qf_s[...].reshape(dq_ref.shape).astype(BF16)
        dk_ref[...] = kf_s[...].reshape(dk_ref.shape).astype(BF16)
        dv_ref[...] = vf_s[...].reshape(dv_ref.shape).astype(BF16)
        for copy in gradients_out:
            copy.start()

    def turn_slabs():
        arrivals(lambda source: to_sides(lambda h: side_landed(source, h).wait_recv()))
        for d in range(n):
            slab_t[:, d * length : (d + 1) * length] = jnp.transpose(slab_s[d]).astype(BF16)

    def own_weight(j):
        wg_out[j] = dot(slab_t[...], rows_of(*(gath_s[d, j] for d in range(n))).astype(BF16))
        wg_copy(j).start()

    def relay(i):
        j = i - me - (groups - 1)

        @pl.when((j >= 0) & (j < groups))
        def _():
            def from_left(step, carry):
                source = me - step

                @pl.when(source >= 0)
                def _():
                    core_right(source, j).wait_recv()

                    @pl.when(me < n - 1)
                    def _():
                        core_right(source, j).start()

                return carry

            lax.fori_loop(1, n, from_left, 0)

        def from_right(step, carry):
            source = me + step
            late = i - me - 2 * step

            @pl.when((source < n) & (late >= 0) & (late < groups))
            def _():
                core_left(source, late).wait_recv()

                @pl.when(me > 0)
                def _():
                    core_left(source, late).start()

            return carry

        lax.fori_loop(1, n, from_right, 0)

    def when_group(j, what):
        @pl.when((j >= 0) & (j < groups))
        def _():
            what(j)

    def rate_copy(source, target):
        return remote(rate_ref, rate_in.at[source], rate_send.at[target], rate_recv.at[source], {"ctx": target})

    def step(i, carry):
        @pl.when(i < groups)
        def _():
            local_maps(i)

        @pl.when((i >= me) & (i < groups + me))
        def _():
            forward(i - me)

        back = i - (n - 1 - me)

        @pl.when((back >= 0) & (back < groups))
        def _():
            backward_wave(back)

        @pl.when(i == groups - 1 + me)
        def _():
            project()

        @pl.when(i == min(groups - 1, 2))
        def _():
            pass_aside()

        @pl.when(i == groups)
        def _():
            turn_slabs()

        relay(i)
        when_group(i - jnp.maximum(jnp.maximum(2 * (n - 1) - me, me + (groups - 1)), groups), own_weight)
        ready = i - (n - 1 + 0)

        @pl.when((ready >= 0) & (ready < groups))
        def _():
            backward(ready)

        @pl.when(ready == groups - 1)
        def _():
            finish_local()
            for d in range(n):

                @pl.when(me != d)
                def _():
                    rate_copy(me, d).start()

        return carry

    load_w.wait()
    lax.fori_loop(0, groups + 2 * (n - 1), step, 0)

    for d in range(n):

        @pl.when(me != d)
        def _():
            rate_copy(d, me).wait_recv()

        @pl.when(me == d)
        def _():
            rate_in[d] = rate_ref[...]

    rate_two[0] = sum(rate_in[d] for d in range(n))
    two = remote(rate_two.at[0], rate_two.at[1], two_send.at[0], two_recv.at[0], partner)
    two.start()
    for d in range(heads_n):

        @pl.when(head_me != d)
        def _():
            remote(
                mix_out.at[d], mix_in.at[d], mix_send.at[d], mix_recv.at[d], {"head": d}
            ).wait_recv()

    mixed_ref[...] = sum(mix_in[d] for d in range(heads_n)).astype(BF16)
    for d in range(n):

        @pl.when(me != d)
        def _():
            rate_copy(me, d).wait_send()

    for j in range(groups):
        wg_copy(j).wait_recv()
        wg_in[j] = wg_out[j] + wg_in[j]
        weight_out(j).start()
    two.wait()
    rate_ref[...] = rate_two[0] + rate_two[1]
    for j in range(groups):
        wg_copy(j).wait_send()
    for d in range(heads_n):

        @pl.when(head_me != d)
        def _():
            mix_copy(d).wait_send()

    for d in range(n):

        @pl.when(me != d)
        def _():
            cot_copy(d).wait_send()

    arrivals(lambda source: to_sides(lambda h: side_copy(source, h).wait_send()))

    def drain(j, carry):
        @pl.when(me < n - 1)
        def _():
            enter_copy(j).wait_send()

        @pl.when(me > 0)
        def _():
            leave_copy(j).wait_send()

        def one(source, inner):
            @pl.when((source <= me) & (me < n - 1))
            def _():
                core_right(source, j).wait_send()

            @pl.when((source >= me) & (me > 0))
            def _():
                core_left(source, j).wait_send()

            return inner

        return lax.fori_loop(0, n, one, carry)

    lax.fori_loop(0, groups, drain, 0)
    for copy in gradients_out:
        copy.wait()
    for j in range(groups):
        weight_out(j).wait()


def hand_over_kernel(rate_ref, *refs):
    count = (len(refs) - 2) // 2
    sources, targets, rate_out, sems = refs[:count], refs[count : 2 * count], refs[-2], refs[-1]
    copies = [
        pltpu.make_async_copy(source, target, sems.at[i]) for i, (source, target) in enumerate(zip(sources, targets))
    ]
    for copy in copies:
        copy.start()
    for h in range(rate_out.shape[0]):
        rate_out[h] = rate_ref[h, 0]
    for copy in copies:
        copy.wait()


def on_device(
    query_input, key_input, value_input, beta_logit, gate_logit, decay_rate,
    doc_ids, out_weight, out_cotangent,
):
    _, length, heads, width = query_input.shape
    model_width = out_cotangent.shape[-1]
    blocks = length // CH
    groups = heads // GROUP
    factors = length * NF
    n, heads_n, dp_n = (lax.axis_size(axis) for axis in ("ctx", "head", "dp"))
    units = GROUP * blocks
    slab = model_width // n
    share = model_width // heads_n
    lanes = GROUP * width

    def vmem(*shape, dtype=F32):
        return pltpu.VMEM(shape, dtype)

    def dma(*shape):
        return pltpu.SemaphoreType.DMA(shape)

    state = (groups, units, width, width)
    moving = (groups, GROUP, width, width)
    scratch = [
        vmem(*out_weight.shape, dtype=BF16), vmem(length, heads, width, dtype=BF16),
        vmem(factors, heads, width, dtype=BF16), vmem(factors, heads, width, dtype=BF16), dma(4), dma(groups),
        vmem(length * heads, width), vmem(factors * heads, width), vmem(factors * heads, width),
        vmem(WIDTH, factors), vmem(WIDTH, length),
        vmem(groups, factors, WIDTH), vmem(groups, length, WIDTH),
        vmem(blocks, heads, SPAN), vmem(WIDTH, factors), vmem(WIDTH, length),
        vmem(groups, length, lanes),
        vmem(groups, units, SPAN, SPAN, dtype=BF16),
        vmem(groups, units, SPAN, SPAN, dtype=BF16),
        vmem(groups, units, SPAN, width),
        vmem(groups, units, SPAN, width),
        vmem(groups, units, SPAN, SPAN),
        vmem(groups, units, CH, SPAN),
        vmem(groups, units, CH, SPAN),
        vmem(groups, units, SPAN, 1),
        vmem(*state), vmem(*state), vmem(*state),
        vmem(groups, units, CH, width),
        vmem(*moving), vmem(*moving), vmem(*moving), vmem(*moving),
        vmem(n, length, slab),
        vmem(n, length, slab),
        vmem(slab, n * length, dtype=BF16),
        vmem(n, groups, length, lanes),
        vmem(groups, length, lanes, dtype=BF16),
        vmem(heads_n, length, share),
        vmem(heads_n, length, share),
        vmem(groups, slab, lanes),
        vmem(groups, slab, lanes),
        vmem(n, 8, WIDTH),
        vmem(2, 8, WIDTH),
        dma(groups), dma(groups), dma(groups), dma(groups),
        dma(n), dma(n), dma(n, heads_n), dma(n, heads_n),
        dma(n, groups), dma(n, groups), dma(n, groups),
        dma(heads_n), dma(heads_n), dma(groups), dma(groups),
        dma(n), dma(n), dma(1), dma(1),
    ]
    whole = pl.BlockSpec(memory_space=pltpu.VMEM)
    scalars = pl.BlockSpec(memory_space=pltpu.SMEM)
    anywhere = pl.BlockSpec(memory_space=pl.ANY)
    dq, dk, dv, beta_grad, gate_grad, mixed, weight_grad, rate = pl.pallas_call(
        functools.partial(layer_kernel, (n, heads_n, dp_n, groups, blocks)),
        in_specs=[scalars] * 2 + [whole] * 6 + [anywhere],
        out_specs=[anywhere] * 3 + [whole] * 3 + [anywhere, whole],
        out_shape=[
            jax.ShapeDtypeStruct((length, heads, width), BF16),
            jax.ShapeDtypeStruct((factors, heads, width), BF16),
            jax.ShapeDtypeStruct((factors, heads, width), BF16),
            jax.ShapeDtypeStruct((NF, heads, length), F32),
            jax.ShapeDtypeStruct((heads, length), F32),
            jax.ShapeDtypeStruct((length, share), BF16),
            jax.ShapeDtypeStruct((slab, heads * width), F32),
            jax.ShapeDtypeStruct((8, WIDTH), F32),
        ],
        scratch_shapes=scratch,
        compiler_params=pltpu.CompilerParams(
            collective_id=0, has_side_effects=True, vmem_limit_bytes=61 << 20
        ),
        name="layer",
    )(
        doc_ids, decay_rate, query_input[0], key_input.reshape(factors, heads, width),
        value_input.reshape(factors, heads, width), beta_logit[0].transpose(1, 0, 2), gate_logit[0], out_cotangent[0], out_weight,
    )
    moved = (mixed, dq, dk, dv, beta_grad, gate_grad, weight_grad)
    mixed, dq, dk, dv, beta_grad, gate_grad, weight_grad, rate_grad = pl.pallas_call(
        hand_over_kernel,
        in_specs=[scalars] + [whole] * len(moved),
        out_specs=[anywhere] * len(moved) + [scalars],
        out_shape=[jax.ShapeDtypeStruct(x.shape, x.dtype) for x in moved]
        + [jax.ShapeDtypeStruct((heads,), F32)],
        scratch_shapes=[pltpu.SemaphoreType.DMA((len(moved),))],
        name="hand_over",
    )(rate, *moved)
    return (
        mixed[None],
        dq[None],
        dk.reshape(key_input.shape),
        dv.reshape(value_input.shape),
        beta_grad.transpose(1, 0, 2)[None],
        gate_grad[None],
        weight_grad,
        rate_grad,
    )


def solution(mesh):
    in_specs = (
        P(("groups", "dp"), "ctx", "head", None),
        P(("groups", "dp"), "ctx", None, "head", None),
        P(("groups", "dp"), "ctx", None, "head", None),
        P(("groups", "dp"), "head", None, "ctx"),
        P(("groups", "dp"), "head", "ctx"),
        P("head"),
        P(("groups", "dp"), None),
        P("head", None),
        P(("groups", "dp"), "ctx", None),
    )
    out_specs = (
        P(("groups", "dp"), "ctx", "head"),
        P(("groups", "dp"), "ctx", "head", None),
        P(("groups", "dp"), "ctx", None, "head", None),
        P(("groups", "dp"), "ctx", None, "head", None),
        P(("groups", "dp"), "head", None, "ctx"),
        P(("groups", "dp"), "head", "ctx"),
        P(("groups", "ctx"), "head"),
        P(("groups", "head")),
    )
    return jax.shard_map(
        on_device, mesh=mesh, in_specs=in_specs, out_specs=out_specs, check_vma=False
    )
```

```python
import functools

import jax
import jax.numpy as jnp
from jax import lax
from jax.experimental import pallas as pl
from jax.experimental.pallas import tpu as pltpu
from jax.sharding import PartitionSpec as P

CH = 64
NF = 3
SPAN = CH * NF
WIDTH = 128
GROUP = 2
FIELDS = 8
F32 = jnp.float32
BF16 = jnp.bfloat16
MESH = pl.DeviceIdType.MESH
BETA, CUMUL, BETA_GROWTH, GROWTH, TAIL, INVERSE_BETA, LAST = range(7)
READ_CUMUL, READ_GROWTH = range(2)


def iota(shape, dim):
    return lax.broadcasted_iota(jnp.int32, shape, dim)


def rows_of(*parts):
    return jnp.concatenate(parts, axis=0)


def lanes_of(*parts):
    return jnp.concatenate(parts, axis=1)


def split(x):
    high = x.astype(BF16)
    return high, (x - high.astype(F32)).astype(BF16)


def dot(a, b, ta=False, tb=False):
    dims = (((0 if ta else 1,), (1 if tb else 0,)), ((), ()))
    return lax.dot_general(a, b, dims, preferred_element_type=F32)


def folded(p):
    return p[:, :WIDTH] + p[:, WIDTH:]


def select(x, chosen):
    high = x.astype(BF16)
    rest = x - high.astype(F32)
    middle = rest.astype(BF16)
    low = (rest - middle.astype(F32)).astype(BF16)
    size = x.shape[0]
    p = dot(rows_of(high.astype(F32), middle.astype(F32), low.astype(F32)).astype(BF16), chosen)
    return (p[2 * size :] + p[size : 2 * size]) + p[:size]


def where_one(condition):
    return jnp.where(condition, 1.0, 0.0).astype(BF16)


def mm_exact(a, b):
    return folded(dot(a, lanes_of(*split(b))))


def mm_full(a, b):
    size = a.shape[0]
    b_high, b_low = split(b)
    p = dot(rows_of(*split(a)), lanes_of(b_high, b_low))
    return folded(p[:size]) + p[size:, :WIDTH]


def mm_wide(a, b):
    size = a.shape[0]
    a_high, a_low = split(a)
    b_high, b_low = split(b)
    p = dot(rows_of(a_high, a_low), b_high)
    return p[:size] + p[size:] + dot(a_high, b_low)


def mm_tb(a, b):
    size = a.shape[0]
    a_high, a_low = split(a)
    b_high, b_low = split(b)
    p = dot(rows_of(a_high, a_low), b_high, tb=True)
    return p[:size] + p[size:] + dot(a_high, b_low, tb=True)


def mm_ta(a, b):
    a_high, a_low = split(a)
    b_high, b_low = split(b)
    return folded(dot(a_high, lanes_of(b_high, b_low), ta=True)) + dot(a_low, b_high, ta=True)


def lower_halves(x, size):
    return rows_of(*(x[i : i + size] for i in range(size, x.shape[0], 2 * size)))


def spread_halves(low, size, total):
    zero = jnp.zeros((size, low.shape[1]), low.dtype)
    pieces, taken = [], 0
    for i in range(0, total, size):
        if (i // size) % 2:
            pieces.append(low[taken : taken + size])
            taken += size
        else:
            pieces.append(zero)
    return rows_of(*pieces)


def merge_halves(x, low, size):
    pieces, taken = [], 0
    for i in range(0, x.shape[0], size):
        if (i // size) % 2:
            pieces.append(low[taken : taken + size])
            taken += size
        else:
            pieces.append(x[i : i + size])
    return rows_of(*pieces)


def unit_inverses(lowers):
    lane, sub = iota((8, SPAN), 1), iota((8, SPAN), 0)
    lane_here = iota((8, WIDTH), 1)
    starts = []
    for lower in lowers:
        packed = jnp.zeros((8, SPAN), F32)
        for b in range(SPAN // 8):
            packed = packed + jnp.where(lane // 8 == b, lower[8 * b : 8 * b + 8], 0.0)
        wide = lanes_of(packed, jnp.zeros((8, 2 * WIDTH - SPAN), F32))
        block = jnp.where(sub == lane % 8, 1.0, 0.0)
        for c in range(7):
            index = (lane_here // 8) * 8 + c
            factor = lanes_of(
                *(jnp.take_along_axis(wide[:, at : at + WIDTH], index, axis=1) for at in (0, WIDTH))
            )[:, :SPAN]
            block = block - factor * block[c : c + 1, :]
        starts.append(rows_of(*(jnp.where(lane // 8 == b, block, 0.0) for b in range(SPAN // 8))))
    inverses = starts
    row, column = iota((SPAN, SPAN), 0), iota((SPAN, SPAN), 1)
    for level in range(3, (SPAN - 1).bit_length()):
        size = 1 << level
        here = (lower_halves(row, size) >> level) == (lower_halves(column, size) >> level) + 1
        halves = [
            mm_wide(jnp.where(here, lower_halves(low, size), 0.0), inv)
            for low, inv in zip(lowers, inverses)
        ]
        tails = [
            lower_halves(inv, size) - mm_wide(lower_halves(inv, size), spread_halves(half, size, SPAN))
            for inv, half in zip(inverses, halves)
        ]
        inverses = [merge_halves(inv, tail, size) for inv, tail in zip(inverses, tails)]
    return inverses


def layer_kernel(
    sizes,
    doc_ref, decay_ref, q_ref, k_ref, v_ref, beta_ref, gate_ref, cot_ref, w_in,
    dq_out, dk_out, dv_out, beta_out, gate_out, mixed_ref, wg_ref, rate_ref,
    w_ref, dq_ref, dk_ref, dv_ref, own_sems, weight_sems,
    qf_s, kf_s, vf_s, frow_s, trow_s, cols_s, tcols_s, grow_s, gt_s, tt_s,
    grad_s, th_s, tl_s, u_s, w_s, lg_s, reads_s, rd_s, r_s,
    map_s, offset_s, pull_s, qe_s,
    ein_s, eout_s, gin_s, gout_s, cotf_s, slab_s, slab_t, gath_s, core_s,
    mix_out, mix_in, wg_out, wg_in, rate_in, rate_two,
    e_send, e_recv, g_send, g_recv, cot_send, cot_recv, side_send, side_recv,
    right_send, left_send, core_recv,
    mix_send, mix_recv, wg_send, wg_recv,
    rate_send, rate_recv, two_send, two_recv,
):
    n, heads_n, dp_n, groups, stretches = sizes
    me = lax.axis_index("ctx")
    head_me = lax.axis_index("head")
    dp_me = lax.axis_index("dp")
    slab = slab_s.shape[-1]
    share = mix_in.shape[-1]
    scale = WIDTH ** (-0.5)
    every = [(g, s) for g in range(GROUP) for s in range(stretches)]
    partner = {"dp": lax.rem(dp_me + 1, dp_n)}

    load_w = pltpu.make_async_copy(w_in, w_ref, own_sems.at[0])
    load_w.start()
    barrier = pltpu.get_barrier_semaphore()
    for step in range(1, n):
        pl.semaphore_signal(barrier, inc=1, device_id={"ctx": lax.rem(me + step, n)}, device_id_type=MESH)
    for step in range(1, heads_n):
        pl.semaphore_signal(
            barrier, inc=1, device_id={"head": lax.rem(head_me + step, heads_n)}, device_id_type=MESH
        )
    pl.semaphore_signal(barrier, inc=1, device_id=partner, device_id_type=MESH)

    for d in range(n):
        piece = cot_ref[:, d * slab : (d + 1) * slab].astype(F32)

        @pl.when(me == d)
        def _():
            slab_s[d] = piece

        @pl.when(me != d)
        def _():
            cotf_s[d] = piece

    @pl.when(me == 0)
    def _():
        ein_s[...] = jnp.zeros_like(ein_s)

    @pl.when(me == n - 1)
    def _():
        gin_s[...] = jnp.zeros_like(gin_s)

    heads = groups * GROUP
    length = stretches * CH
    factors = length * NF
    qf_s[...] = q_ref[...].astype(F32).reshape(qf_s.shape)
    kf_s[...] = k_ref[...].astype(F32).reshape(kf_s.shape)
    vf_s[...] = v_ref[...].astype(F32).reshape(vf_s.shape)

    before, after = iota((length, length), 0), iota((length, length), 1)
    same = before // CH == after // CH
    up_to = where_one(same & (before <= after))
    closing = where_one(before == (after // CH) * CH + (CH - 1))
    widen = where_one(iota((length, factors), 0) == iota((length, factors), 1) // NF)
    source = iota((factors, factors), 0)
    weave = where_one((source % length) * NF + source // length == iota((factors, factors), 1))
    head_row = iota((heads, 1), 0)
    rate_column = jnp.zeros((heads, 1), F32)
    for h in range(heads):
        rate_column = rate_column + jnp.where(head_row == h, decay_ref[h], 0.0)
    gate = gate_ref[...]
    soft = jnp.maximum(gate, 0.0) + jnp.log1p(jnp.exp(-jnp.abs(gate)))
    sums = select(-rate_column * soft, up_to)
    last = select(sums, closing)
    growth_rows = jnp.exp(sums)
    wide = select(rows_of(sums, growth_rows, jnp.exp(last - sums), jnp.exp(last)), widen)
    beta_rows = select(lanes_of(*(2.0 / (1.0 + jnp.exp(-beta_ref[f])) for f in range(NF))), weave)
    sums_wide, growth_wide, tail_wide, last_wide = (wide[i * heads : (i + 1) * heads] for i in range(4))
    frow_s[...] = jnp.zeros_like(frow_s)
    trow_s[...] = jnp.zeros_like(trow_s)
    for field, value in (
        (BETA, beta_rows), (CUMUL, sums_wide), (BETA_GROWTH, beta_rows * growth_wide), (GROWTH, growth_wide),
        (TAIL, tail_wide), (INVERSE_BETA, 1.0 / beta_rows), (LAST, last_wide),
    ):
        for h in range(heads):
            frow_s[h * FIELDS + field : h * FIELDS + field + 1, :] = value[h : h + 1]
    for field, value in ((READ_CUMUL, sums), (READ_GROWTH, growth_rows * scale)):
        for h in range(heads):
            trow_s[h * FIELDS + field : h * FIELDS + field + 1, :] = value[h : h + 1]
    turned_fields, turned_tokens = jnp.transpose(frow_s[...]), jnp.transpose(trow_s[...])
    per_group = GROUP * FIELDS
    for j in range(groups):
        cols_s[j, :, :per_group] = turned_fields[:, j * per_group : (j + 1) * per_group]
        tcols_s[j, :, :per_group] = turned_tokens[:, j * per_group : (j + 1) * per_group]
    retains = []
    for s in range(stretches):
        place = me * stretches + s
        kept = doc_ref[0, place] == doc_ref[0, jnp.maximum(place - 1, 0)]
        retains.append(jnp.where(kept & (place > 0), 1.0, 0.0))
    pl.semaphore_wait(barrier, n - 1 + heads_n - 1 + 1)

    def remote(src, dst, send, recv, where):
        return pltpu.make_async_remote_copy(
            src_ref=src, dst_ref=dst, send_sem=send, recv_sem=recv, device_id=where, device_id_type=MESH
        )

    part = cot_ref.shape[0] // heads_n

    def part_rows(h):
        return pl.ds(pl.multiple_of(h * part, part), part)

    def cot_copy(d):
        mine = part_rows(head_me)
        return remote(cotf_s.at[d, mine], slab_s.at[me, mine], cot_send.at[d], cot_recv.at[me], {"ctx": d})

    def cot_landed(source):
        at = slab_s.at[source, part_rows(head_me)]
        return remote(at, at, cot_send.at[0], cot_recv.at[source], {"ctx": source})

    def side_copy(source, h):
        at = slab_s.at[source, part_rows(head_me)]
        return remote(at, at, side_send.at[source, h], side_recv.at[source, head_me], {"head": h})

    def side_landed(source, h):
        at = slab_s.at[source, part_rows(h)]
        return remote(at, at, side_send.at[source, h], side_recv.at[source, h], {"head": h})

    def arrivals(what):
        for d in range(n):

            @pl.when(me != d)
            def _():
                what(d)

    def to_sides(what):
        for h in range(heads_n):

            @pl.when(head_me != h)
            def _():
                what(h)

    def pass_aside():
        def one(source):
            cot_landed(source).wait_recv()
            to_sides(lambda h: side_copy(source, h).start())

        arrivals(one)

    for d in range(n):

        @pl.when(me != d)
        def _():
            cot_copy(d).start()

    def enter_copy(j):
        return remote(eout_s.at[j], ein_s.at[j], e_send.at[j], e_recv.at[j], {"ctx": lax.rem(me + 1, n)})

    def leave_copy(j):
        return remote(gout_s.at[j], gin_s.at[j], g_send.at[j], g_recv.at[j], {"ctx": lax.rem(me + n - 1, n)})

    def core_right(source, j):
        at = gath_s.at[source, j]
        return remote(at, at, right_send.at[source, j], core_recv.at[source, j], {"ctx": lax.rem(me + 1, n)})

    def core_left(source, j):
        at = gath_s.at[source, j]
        return remote(at, at, left_send.at[source, j], core_recv.at[source, j], {"ctx": lax.rem(me + n - 1, n)})

    def mix_copy(d):
        return remote(mix_out.at[d], mix_in.at[head_me], mix_send.at[d], mix_recv.at[head_me], {"head": d})

    def wg_copy(j):
        return remote(wg_out.at[j], wg_in.at[j], wg_send.at[j], wg_recv.at[j], partner)

    def lanes(j):
        return pl.ds(pl.multiple_of(j * (GROUP * WIDTH), WIDTH), GROUP * WIDTH)

    def columns(j, g, s):
        block = cols_s[j, s * SPAN : (s + 1) * SPAN]
        return lambda f: block[:, g * FIELDS + f : g * FIELDS + f + 1]

    def token_columns(j, g, s):
        block = tcols_s[j, s * CH : (s + 1) * CH]
        return lambda f: block[:, g * FIELDS + f : g * FIELDS + f + 1]

    def field_rows(j, g, s):
        block = frow_s[pl.ds(pl.multiple_of((j * GROUP + g) * FIELDS, FIELDS), FIELDS), :]
        return block[:, s * SPAN : (s + 1) * SPAN]

    def place(j, g, s, size):
        return pl.ds(s * size * heads + j * GROUP + g, size, stride=heads)

    def unit(j, g, s):
        return j, g * stretches + s

    def local_maps(j):
        eye = iota((SPAN, SPAN), 0) == iota((SPAN, SPAN), 1)
        strict = iota((SPAN, SPAN), 0) > iota((SPAN, SPAN), 1)
        diagonal = iota((WIDTH, WIDTH), 0) == iota((WIDTH, WIDTH), 1)
        visible = iota((CH, SPAN), 0) * NF + (NF - 1) >= iota((CH, SPAN), 1)
        w_rows = w_ref[pl.ds(pl.multiple_of(j * (GROUP * WIDTH), WIDTH), GROUP * WIDTH), :]
        grad = dot(cot_ref[...], w_rows, tb=True)
        grad_s[j] = grad
        lowers, kept = [], []
        for g, s in every:
            at = slice(g * WIDTH, (g + 1) * WIDTH)
            k = kf_s[place(j, g, s, SPAN), :].astype(BF16)
            q = qf_s[place(j, g, s, CH), :].astype(BF16)
            col, tok = columns(j, g, s), token_columns(j, g, s)
            row = field_rows(j, g, s)
            cumul_row = row[CUMUL : CUMUL + 1]
            both = dot(rows_of(k, q), k, tb=True)
            gram, scores = both[:SPAN], both[SPAN:]
            squares = jnp.where(eye, gram, 0.0)
            r = lax.rsqrt(jnp.sum(squares, axis=1, keepdims=True) + 1e-06)
            r_row = lax.rsqrt(jnp.sum(squares, axis=0, keepdims=True) + 1e-06)
            pair = jnp.exp(jnp.where(strict, col(CUMUL) - cumul_row, -1e30)) * r_row
            lower_gain = (col(BETA) * r) * pair
            lower = lower_gain * gram
            read_gain = jnp.exp(
                jnp.where(visible, tok(READ_CUMUL) - cumul_row, -1e30)
            ) * (r_row * scale)
            reads = read_gain * scores
            here = unit(j, g, s)
            r_s[here] = r
            lg_s[here] = lower_gain
            rd_s[here] = read_gain
            reads_s[here] = reads
            lowers.append(lower)
            kept.append((k, q, col, tok, row, r, r_row, reads))
        for (g, s), (k, q, col, tok, row, r, r_row, reads), inverse in zip(every, kept, unit_inverses(lowers)):
            here = unit(j, g, s)
            at = slice(g * WIDTH, (g + 1) * WIDTH)
            th_s[here], tl_s[here] = split(inverse)
            v = vf_s[place(j, g, s, SPAN), :].astype(BF16)
            p = dot(rows_of(*split(inverse * row[BETA : BETA + 1])), v)
            solved_v = p[:SPAN] + p[SPAN:]
            p = dot(rows_of(*split(inverse * (row[BETA_GROWTH : BETA_GROWTH + 1] * r_row))), k)
            solved_k = p[:SPAN] + p[SPAN:]
            u_s[here] = solved_v
            w_s[here] = solved_k
            high, low = split(lanes_of(solved_v, solved_k) * (col(TAIL) * r))
            moved = dot(k, high, ta=True) + dot(k, low, ta=True)
            offset_s[here] = moved[:, :WIDTH]
            map_s[here] = jnp.where(diagonal, col(LAST)[:1], 0.0) - moved[:, WIDTH:]
            route = tok(READ_GROWTH) * q.astype(F32) - mm_full(reads, solved_k)
            pull_s[here] = mm_ta(route, grad[s * CH : (s + 1) * CH, at])

    def forward(j):
        @pl.when(me > 0)
        def _():
            enter_copy(j).wait_recv()

        entries = {}
        for g in range(GROUP):
            state = ein_s[j, g]
            for s in range(stretches):
                entry = retains[s] * state
                entries[g, s] = entry
                state = mm_full(map_s[unit(j, g, s)], entry) + offset_s[unit(j, g, s)]
                offset_s[unit(j, g, s)] = entry
            eout_s[j, g] = state

        @pl.when(me < n - 1)
        def _():
            enter_copy(j).start()

        for g, s in every:
            here = unit(j, g, s)
            at = slice(g * WIDTH, (g + 1) * WIDTH)
            k = kf_s[place(j, g, s, SPAN), :].astype(BF16)
            q = qf_s[place(j, g, s, CH), :].astype(BF16)
            tok = token_columns(j, g, s)
            on_entry = mm_exact(rows_of(k, q), entries[g, s])
            key_entry, query_entry = r_s[here] * on_entry[:SPAN], on_entry[SPAN:]
            correction = u_s[here] - mm_full(w_s[here], entries[g, s])
            core = tok(READ_GROWTH) * query_entry + mm_full(reads_s[here], correction)
            rounded = core.astype(BF16)
            w_s[here] = key_entry
            qe_s[here] = query_entry
            u_s[here] = correction
            core_s[j, s * CH : (s + 1) * CH, at] = rounded
            gath_s[me, j, s * CH : (s + 1) * CH, at] = rounded.astype(F32)

        @pl.when(me < n - 1)
        def _():
            core_right(me, j).start()

        @pl.when(me > 0)
        def _():
            core_left(me, j).start()

    def backward_wave(j):
        @pl.when(me < n - 1)
        def _():
            leave_copy(j).wait_recv()

        for g in range(GROUP):
            state = gin_s[j, g]
            for s in reversed(range(stretches)):
                here = unit(j, g, s)
                maps_high, maps_low = split(map_s[here])
                high, low = split(state)
                carried = folded(dot(maps_high, lanes_of(high, low), ta=True)) + dot(maps_low, high, ta=True)
                before = retains[s] * (carried + pull_s[here])
                pull_s[here] = state
                state = before
            gout_s[j, g] = state

        @pl.when(me > 0)
        def _():
            leave_copy(j).start()

    def project():
        core = lanes_of(*(core_s[j] for j in range(groups)))

        def columns_of(d):
            return dot(core, w_ref[:, d * share : (d + 1) * share])

        for d in range(heads_n):

            @pl.when(head_me != d)
            def _():
                mix_out[d] = columns_of(d)
                mix_copy(d).start()

        for d in range(heads_n):

            @pl.when(head_me == d)
            def _():
                mix_in[d] = columns_of(d)

    def backward(j):
        token = iota((CH, 1), 0)
        for g, s in every:
            here = unit(j, g, s)
            at = slice(g * WIDTH, (g + 1) * WIDTH)
            key = kf_s[place(j, g, s, SPAN), :]
            v = vf_s[place(j, g, s, SPAN), :]
            k, q = key.astype(BF16), qf_s[place(j, g, s, CH), :].astype(BF16)
            col = columns(j, g, s)
            beta, growth, tail, read_growth = col(BETA), col(GROWTH), col(TAIL), token_columns(j, g, s)(READ_GROWTH)
            grad = grad_s[j, s * CH : (s + 1) * CH, at]
            entry, leaving, r = offset_s[here], pull_s[here], r_s[here]
            correction, key_entry, query_entry = u_s[here], w_s[here], qe_s[here]
            reads = reads_s[here]
            key_leave = r * mm_exact(k, leaving)
            correction_grad = mm_ta(reads, grad) + tail * key_leave
            high, low = split(correction_grad)
            right_grad = folded(dot(th_s[here], lanes_of(high, low), ta=True)) + dot(tl_s[here], high, ta=True)
            rest_grad = beta * right_grad
            outer = mm_tb(rows_of(right_grad, grad), correction)
            outer_key, outer_read = outer[:SPAN], outer[SPAN:]
            gram_grad = -outer_key * lg_s[here]
            score_grad = outer_read * rd_s[here]
            pairs = -gram_grad * dot(k, k, tb=True)
            read_pairs = outer_read * reads
            tailed = tail * correction
            back = mm_tb(
                rows_of(
                    lanes_of(-growth * rest_grad, tailed),
                    lanes_of(read_growth * grad, jnp.zeros((CH, WIDTH), F32)),
                ),
                lanes_of(entry, leaving),
            )
            high, low = split(rows_of(gram_grad, score_grad))
            both = rows_of(k, q)
            p = dot(rows_of(high, low), k)
            direct = p[: SPAN + CH] + p[SPAN + CH :]
            turned = dot(high, both, ta=True) + dot(low, both, ta=True)
            key_grad = r * back[:SPAN] + direct[:SPAN] + turned
            dk = key_grad - key * (r * r * jnp.sum(key * key_grad, axis=1, keepdims=True))
            dq = back[SPAN:] + direct[SPAN:]
            fill = jnp.zeros((SPAN, 2 * WIDTH - SPAN), F32)
            pairs_fold = folded(lanes_of(pairs, fill))
            tail_pairs = tailed * key_leave
            factor_cumul = -jnp.sum(
                pairs_fold + growth * rest_grad * key_entry + tail_pairs, axis=1, keepdims=True
            )
            beta_grad = jnp.sum(
                right_grad * (v - growth * key_entry) - col(INVERSE_BETA) * pairs_fold, axis=1, keepdims=True
            )
            token_cumul = jnp.sum(
                folded(lanes_of(read_pairs, fill[:CH])) + read_growth * grad * query_entry, axis=1, keepdims=True
            )
            last_grad = jnp.sum(
                jnp.sum(tail_pairs, axis=0, keepdims=True)
                + col(LAST)[:1] * jnp.sum(entry * leaving, axis=0, keepdims=True),
                axis=1, keepdims=True,
            )
            token_cumul = token_cumul + jnp.where(token == CH - 1, last_grad, 0.0)
            row_cumul = jnp.sum(pairs, axis=0, keepdims=True) - jnp.sum(read_pairs, axis=0, keepdims=True)
            lane_at = WIDTH // 2 + g * FIELDS
            rows_here = slice(s * SPAN, (s + 1) * SPAN)
            cols_s[j, rows_here, lane_at : lane_at + 1] = beta_grad
            cols_s[j, rows_here, lane_at + 1 : lane_at + 2] = factor_cumul
            tcols_s[j, s * CH : (s + 1) * CH, lane_at : lane_at + 1] = token_cumul
            grow_s[s, pl.ds(j * GROUP + g, 1), :] = row_cumul
            qf_s[place(j, g, s, CH), :] = dq
            kf_s[place(j, g, s, SPAN), :] = dk
            vf_s[place(j, g, s, SPAN), :] = rest_grad

    gradients_out = [
        pltpu.make_async_copy(source, target, own_sems.at[1 + i])
        for i, (source, target) in enumerate(((dq_ref, dq_out), (dk_ref, dk_out), (dv_ref, dv_out)))
    ]

    def weight_out(j):
        return pltpu.make_async_copy(wg_in.at[j], wg_ref.at[:, j * GROUP * WIDTH : (j + 1) * GROUP * WIDTH], weight_sems.at[j])

    def finish_local():
        fill = jnp.zeros((factors, WIDTH - groups * per_group), F32)
        gt_s[...] = jnp.transpose(lanes_of(*(cols_s[j, :, WIDTH // 2 : WIDTH // 2 + per_group] for j in range(groups)), fill))
        tt_s[...] = jnp.transpose(lanes_of(*(tcols_s[j, :, WIDTH // 2 : WIDTH // 2 + per_group] for j in range(groups)), fill[:length]))

        def field(ref, f):
            return rows_of(*(ref[h * FIELDS + f : h * FIELDS + f + 1, :] for h in range(heads)))

        cumul_wide = field(gt_s, 1) + lanes_of(*(grow_s[s] for s in range(stretches)))
        narrow = where_one(iota((factors, length), 0) // NF == iota((factors, length), 1))
        cumul_grad = select(cumul_wide, narrow) + field(tt_s, 0)
        decay_grad = select(cumul_grad, where_one(same & (before >= after)))
        gate_out[...] = -rate_column * decay_grad / (1.0 + jnp.exp(-gate))
        share_of = jnp.sum(-soft * decay_grad, axis=1, keepdims=True)
        rate_ref[...] = jnp.zeros_like(rate_ref)
        rate_ref[:heads] = jnp.broadcast_to(share_of, (heads, WIDTH))
        target = iota((factors, factors), 1)
        unweave = where_one((target % length) * NF + target // length == iota((factors, factors), 0))
        beta_parts = select(field(gt_s, 0), unweave)
        for f in range(NF):
            sigmoid = 1.0 / (1.0 + jnp.exp(-beta_ref[f]))
            beta_out[f] = beta_parts[:, f * length : (f + 1) * length] * (2.0 * sigmoid * (1.0 - sigmoid))
        dq_ref[...] = qf_s[...].reshape(dq_ref.shape).astype(BF16)
        dk_ref[...] = kf_s[...].reshape(dk_ref.shape).astype(BF16)
        dv_ref[...] = vf_s[...].reshape(dv_ref.shape).astype(BF16)
        for copy in gradients_out:
            copy.start()

    def turn_slabs():
        arrivals(lambda source: to_sides(lambda h: side_landed(source, h).wait_recv()))
        for d in range(n):
            slab_t[:, d * length : (d + 1) * length] = jnp.transpose(slab_s[d]).astype(BF16)

    def own_weight(j):
        wg_out[j] = dot(slab_t[...], rows_of(*(gath_s[d, j] for d in range(n))).astype(BF16))
        wg_copy(j).start()

    def relay(i):
        j = i - me - (groups - 1)

        @pl.when((j >= 0) & (j < groups))
        def _():
            def from_left(step, carry):
                source = me - step

                @pl.when(source >= 0)
                def _():
                    core_right(source, j).wait_recv()

                    @pl.when(me < n - 1)
                    def _():
                        core_right(source, j).start()

                return carry

            lax.fori_loop(1, n, from_left, 0)

        def from_right(step, carry):
            source = me + step
            late = i - me - 2 * step

            @pl.when((source < n) & (late >= 0) & (late < groups))
            def _():
                core_left(source, late).wait_recv()

                @pl.when(me > 0)
                def _():
                    core_left(source, late).start()

            return carry

        lax.fori_loop(1, n, from_right, 0)

    def when_group(j, what):
        @pl.when((j >= 0) & (j < groups))
        def _():
            what(j)

    def rate_copy(source, target):
        return remote(rate_ref, rate_in.at[source], rate_send.at[target], rate_recv.at[source], {"ctx": target})

    def step(i, carry):
        @pl.when(i < groups)
        def _():
            local_maps(i)

        back = i - (n - 1 - me)

        @pl.when((back >= 0) & (back < groups))
        def _():
            backward_wave(back)

        @pl.when((i >= me) & (i < groups + me))
        def _():
            forward(i - me)

        @pl.when(i == groups - 1 + me)
        def _():
            project()

        @pl.when(i == min(groups - 1, 2))
        def _():
            pass_aside()

        @pl.when(i == groups)
        def _():
            turn_slabs()

        relay(i)
        when_group(i - jnp.maximum(jnp.maximum(2 * (n - 1) - me, me + (groups - 1)), groups), own_weight)
        ready = i - (n - 1 + 0)

        @pl.when((ready >= 0) & (ready < groups))
        def _():
            backward(ready)

        @pl.when(ready == groups - 1)
        def _():
            finish_local()
            for d in range(n):

                @pl.when(me != d)
                def _():
                    rate_copy(me, d).start()

        return carry

    load_w.wait()
    lax.fori_loop(0, groups + 2 * (n - 1), step, 0)

    for d in range(n):

        @pl.when(me != d)
        def _():
            rate_copy(d, me).wait_recv()

        @pl.when(me == d)
        def _():
            rate_in[d] = rate_ref[...]

    rate_two[0] = sum(rate_in[d] for d in range(n))
    two = remote(rate_two.at[0], rate_two.at[1], two_send.at[0], two_recv.at[0], partner)
    two.start()
    for d in range(heads_n):

        @pl.when(head_me != d)
        def _():
            remote(
                mix_out.at[d], mix_in.at[d], mix_send.at[d], mix_recv.at[d], {"head": d}
            ).wait_recv()

    mixed_ref[...] = sum(mix_in[d] for d in range(heads_n)).astype(BF16)
    for d in range(n):

        @pl.when(me != d)
        def _():
            rate_copy(me, d).wait_send()

    for j in range(groups):
        wg_copy(j).wait_recv()
        wg_in[j] = wg_out[j] + wg_in[j]
        weight_out(j).start()
    two.wait()
    rate_ref[...] = rate_two[0] + rate_two[1]
    for j in range(groups):
        wg_copy(j).wait_send()
    for d in range(heads_n):

        @pl.when(head_me != d)
        def _():
            mix_copy(d).wait_send()

    for d in range(n):

        @pl.when(me != d)
        def _():
            cot_copy(d).wait_send()

    arrivals(lambda source: to_sides(lambda h: side_copy(source, h).wait_send()))

    def drain(j, carry):
        @pl.when(me < n - 1)
        def _():
            enter_copy(j).wait_send()

        @pl.when(me > 0)
        def _():
            leave_copy(j).wait_send()

        def one(source, inner):
            @pl.when((source <= me) & (me < n - 1))
            def _():
                core_right(source, j).wait_send()

            @pl.when((source >= me) & (me > 0))
            def _():
                core_left(source, j).wait_send()

            return inner

        return lax.fori_loop(0, n, one, carry)

    lax.fori_loop(0, groups, drain, 0)
    for copy in gradients_out:
        copy.wait()
    for j in range(groups):
        weight_out(j).wait()


def hand_over_kernel(rate_ref, *refs):
    count = (len(refs) - 1) // 2
    for source, target in zip(refs[:count], refs[count : 2 * count]):
        target[...] = source[...]
    for h in range(refs[-1].shape[0]):
        refs[-1][h] = rate_ref[h, 0]


def streamed(x, parts):
    if x.shape[0] % (16 * parts):
        return pl.BlockSpec(x.shape, lambda i: (0,) * x.ndim)
    return pl.BlockSpec((x.shape[0] // parts,) + x.shape[1:], lambda i: (i,) + (0,) * (x.ndim - 1))


def on_device(
    query_input, key_input, value_input, beta_logit, gate_logit, decay_rate,
    doc_ids, out_weight, out_cotangent,
):
    _, length, heads, width = query_input.shape
    model_width = out_cotangent.shape[-1]
    blocks = length // CH
    groups = heads // GROUP
    factors = length * NF
    n, heads_n, dp_n = (lax.axis_size(axis) for axis in ("ctx", "head", "dp"))
    units = GROUP * blocks
    slab = model_width // n
    share = model_width // heads_n
    lanes = GROUP * width

    def vmem(*shape, dtype=F32):
        return pltpu.VMEM(shape, dtype)

    def dma(*shape):
        return pltpu.SemaphoreType.DMA(shape)

    state = (groups, units, width, width)
    moving = (groups, GROUP, width, width)
    scratch = [
        vmem(*out_weight.shape, dtype=BF16), vmem(length, heads, width, dtype=BF16),
        vmem(factors, heads, width, dtype=BF16), vmem(factors, heads, width, dtype=BF16), dma(4), dma(groups),
        vmem(length * heads, width), vmem(factors * heads, width), vmem(factors * heads, width),
        vmem(WIDTH, factors), vmem(WIDTH, length),
        vmem(groups, factors, WIDTH), vmem(groups, length, WIDTH),
        vmem(blocks, heads, SPAN), vmem(WIDTH, factors), vmem(WIDTH, length),
        vmem(groups, length, lanes),
        vmem(groups, units, SPAN, SPAN, dtype=BF16),
        vmem(groups, units, SPAN, SPAN, dtype=BF16),
        vmem(groups, units, SPAN, width),
        vmem(groups, units, SPAN, width),
        vmem(groups, units, SPAN, SPAN),
        vmem(groups, units, CH, SPAN),
        vmem(groups, units, CH, SPAN),
        vmem(groups, units, SPAN, 1),
        vmem(*state), vmem(*state), vmem(*state),
        vmem(groups, units, CH, width),
        vmem(*moving), vmem(*moving), vmem(*moving), vmem(*moving),
        vmem(n, length, slab),
        vmem(n, length, slab),
        vmem(slab, n * length, dtype=BF16),
        vmem(n, groups, length, lanes),
        vmem(groups, length, lanes, dtype=BF16),
        vmem(heads_n, length, share),
        vmem(heads_n, length, share),
        vmem(groups, slab, lanes),
        vmem(groups, slab, lanes),
        vmem(n, 8, WIDTH),
        vmem(2, 8, WIDTH),
        dma(groups), dma(groups), dma(groups), dma(groups),
        dma(n), dma(n), dma(n, heads_n), dma(n, heads_n),
        dma(n, groups), dma(n, groups), dma(n, groups),
        dma(heads_n), dma(heads_n), dma(groups), dma(groups),
        dma(n), dma(n), dma(1), dma(1),
    ]
    whole = pl.BlockSpec(memory_space=pltpu.VMEM)
    scalars = pl.BlockSpec(memory_space=pltpu.SMEM)
    anywhere = pl.BlockSpec(memory_space=pl.ANY)
    dq, dk, dv, beta_grad, gate_grad, mixed, weight_grad, rate = pl.pallas_call(
        functools.partial(layer_kernel, (n, heads_n, dp_n, groups, blocks)),
        in_specs=[scalars] * 2 + [whole] * 6 + [anywhere],
        out_specs=[anywhere] * 3 + [whole] * 3 + [anywhere, whole],
        out_shape=[
            jax.ShapeDtypeStruct((length, heads, width), BF16),
            jax.ShapeDtypeStruct((factors, heads, width), BF16),
            jax.ShapeDtypeStruct((factors, heads, width), BF16),
            jax.ShapeDtypeStruct((NF, heads, length), F32),
            jax.ShapeDtypeStruct((heads, length), F32),
            jax.ShapeDtypeStruct((length, share), BF16),
            jax.ShapeDtypeStruct((slab, heads * width), F32),
            jax.ShapeDtypeStruct((8, WIDTH), F32),
        ],
        scratch_shapes=scratch,
        compiler_params=pltpu.CompilerParams(
            collective_id=0, has_side_effects=True, vmem_limit_bytes=61 << 20
        ),
        name="layer",
    )(
        doc_ids, decay_rate, query_input[0], key_input.reshape(factors, heads, width),
        value_input.reshape(factors, heads, width), beta_logit[0].transpose(1, 0, 2), gate_logit[0], out_cotangent[0], out_weight,
    )
    moved = (mixed, dq, dk, dv, beta_grad, gate_grad, weight_grad)
    mixed, dq, dk, dv, beta_grad, gate_grad, weight_grad, rate_grad = pl.pallas_call(
        hand_over_kernel,
        grid=(4,),
        in_specs=[scalars] + [streamed(x, 4) for x in moved],
        out_specs=[streamed(x, 4) for x in moved] + [scalars],
        out_shape=[jax.ShapeDtypeStruct(x.shape, x.dtype) for x in moved]
        + [jax.ShapeDtypeStruct((heads,), F32)],
        name="hand_over",
    )(rate, *moved)
    return (
        mixed[None],
        dq[None],
        dk.reshape(key_input.shape),
        dv.reshape(value_input.shape),
        beta_grad.transpose(1, 0, 2)[None],
        gate_grad[None],
        weight_grad,
        rate_grad,
    )


def solution(mesh):
    in_specs = (
        P(("groups", "dp"), "ctx", "head", None),
        P(("groups", "dp"), "ctx", None, "head", None),
        P(("groups", "dp"), "ctx", None, "head", None),
        P(("groups", "dp"), "head", None, "ctx"),
        P(("groups", "dp"), "head", "ctx"),
        P("head"),
        P(("groups", "dp"), None),
        P("head", None),
        P(("groups", "dp"), "ctx", None),
    )
    out_specs = (
        P(("groups", "dp"), "ctx", "head"),
        P(("groups", "dp"), "ctx", "head", None),
        P(("groups", "dp"), "ctx", None, "head", None),
        P(("groups", "dp"), "ctx", None, "head", None),
        P(("groups", "dp"), "head", None, "ctx"),
        P(("groups", "dp"), "head", "ctx"),
        P(("groups", "ctx"), "head"),
        P(("groups", "head")),
    )
    return jax.shard_map(
        on_device, mesh=mesh, in_specs=in_specs, out_specs=out_specs, check_vma=False
    )
```
